256 devices in a mesh: dp: 16 (over x, z_hi), slab: 16 (over z_lo, y, core).
Axes of the slice: x: 4, y: 4, z: 8 (z_hi: 4, z_lo: 2; z = z_hi * 2 + z_lo), core: 2. Of those that a mesh axis runs over, the one named last changes fastest.
Arguments:
- field: bfloat16 [16, 64, 64, 4096], P('dp', None, 'slab'), may hold values from -6 to 6
- cotangent: bfloat16 [16, 64, 64, 4096], P('dp', None, 'slab'), may hold values from -6 to 6
- spectral_weight: bfloat16 [16, 256, 64, 128], P(None, 'slab'), may hold values from -0.375 to 0.375
- point_weight: bfloat16 [64, 64], replicated, may hold values from -0.75 to 0.75
- bias: float32 [64], replicated, may hold values from -3 to 3
Outputs:
- input_grad: bfloat16 [16, 64, 64, 4096], P('dp', None, 'slab')
- spectral_grad: float32 [16, 256, 64, 128], P('dp', 'slab')
- point_grad: float32 [64, 64], replicated
- bias_grad: float32 [64], replicated
The draws below stay inside these ranges and needn't reach their ends.
All inputs are finite; a program needn't handle non-finite values.
Results may differ from the reference program's by a relative error of at most 0.015.
Values may be sent and summed in bfloat16 or wider, within the bound.
No kernel may reach another device: no remote copies, remote signals or barrier semaphores. Data moves between devices by JAX's collectives and lax.ppermute only.
A program may use at most 64 MiB of HBM per device.

```python
import math
import jax
import jax.numpy as jnp
from jax import lax

C = 64
NX = 64
NY = 64
NZ = 64
MX = 16
MY = 16
MZ = 16
B = 16
NYZ = 4096
MYZ = 256


def block_scale(key, dims, split, smallest, high):
    level, own = 1.0, jax.random.fold_in(key, 6)
    for dim, shards_of in split:
        steps = jnp.exp(jax.random.uniform(jax.random.fold_in(own, dim), (shards_of,), jnp.float32, smallest / len(split), high / len(split)))
        level = level * jnp.repeat(steps, dims[dim] // shards_of).reshape([-1 if axis == dim else 1 for axis in range(len(dims))])
    return level


def gaussian(stream_key, dims, spread, reach, split=(), held_as=jnp.bfloat16):
    entries = jax.random.normal(stream_key, dims, jnp.float32) * spread
    if len(split) > 0:
        entries = block_scale(stream_key, dims, split, -0.22, 0.18) * entries
    return jnp.clip(entries, min=-reach, max=reach).astype(held_as)


def setup_inputs(seed: int = 0) -> dict:
    streams_of = jax.random.split(jax.random.key(seed), 6)
    return {
        "field": gaussian(streams_of[0], (B, C, NX, NYZ), 1.0, 6.0, ((0, 16), (2, 16))),
        "cotangent": gaussian(streams_of[1], (B, C, NX, NYZ), 1.0, 6.0, ((0, 16), (2, 16))),
        "spectral_weight": gaussian(streams_of[2], (MX, MYZ, C, 2 * C), (4 * C) ** -0.5, 0.375, ((1, 16),)),
        "point_weight": gaussian(streams_of[3], (C, C), C ** -0.5, 0.75),
        "bias": gaussian(streams_of[4], (C,), 0.5, 3.0, (), jnp.float32),
    }


def yz_tables():
    cell_index = jnp.arange(NY * NZ, dtype=jnp.int32)
    y_pos = cell_index // NZ
    z_pos = cell_index % NZ
    mode_index = jnp.arange(MY * MZ, dtype=jnp.int32)
    y_mode = mode_index // MZ
    z_mode = mode_index % MZ
    y_wave = jnp.where(y_mode < MY // 2, y_mode, NY - MY + y_mode)
    phases = y_wave[None, :] * y_pos[:, None] % NY * NZ + z_mode[None, :] * z_pos[:, None] % NZ * NY
    angles = 2.0 * math.pi / (NY * NZ) * (phases % (NY * NZ)).astype(jnp.float32)
    factor = 1.0 / math.sqrt(NY * NZ)
    forward = jnp.concatenate([jnp.cos(angles) * factor, -jnp.sin(angles) * factor], axis=1).astype(jnp.bfloat16)
    doubling = jnp.where(z_mode == 0, 1.0, 2.0).astype(jnp.bfloat16)
    doubled = forward * jnp.concatenate([doubling, doubling])[None, :]
    return (forward, doubled)

def x_tables():
    x_index = jnp.arange(NX, dtype=jnp.int32)
    wave_index = jnp.arange(MX, dtype=jnp.int32)
    x_wave = jnp.where(wave_index < MX // 2, wave_index, NX - MX + wave_index)
    angles = 2.0 * math.pi / NX * (x_index[:, None] * x_wave[None, :] % NX).astype(jnp.float32)
    factor = 1.0 / math.sqrt(NX)
    return ((jnp.cos(angles) * factor).astype(jnp.bfloat16), (jnp.sin(angles) * factor).astype(jnp.bfloat16))

def contract(formula, left_side, right_side):
    return jnp.einsum(formula, left_side.astype(jnp.float32), right_side.astype(jnp.float32), precision=lax.Precision.HIGHEST)

def forward_x(real_part, imag_part, cosine_table, sine_table):
    formula = 'bcxj,xi->bcij'
    real_out = contract(formula, real_part, cosine_table) + contract(formula, imag_part, sine_table)
    imag_out = contract(formula, imag_part, cosine_table) - contract(formula, real_part, sine_table)
    return (real_out.astype(jnp.bfloat16), imag_out.astype(jnp.bfloat16))

def inverse_x(real_part, imag_part, cosine_table, sine_table):
    formula = 'bcij,xi->bcxj'
    real_out = contract(formula, real_part, cosine_table) - contract(formula, imag_part, sine_table)
    imag_out = contract(formula, real_part, sine_table) + contract(formula, imag_part, cosine_table)
    return (real_out.astype(jnp.bfloat16), imag_out.astype(jnp.bfloat16))

def gelu_slope(argument):
    normal_cdf = 0.5 * (1.0 + jax.scipy.special.erf(argument / math.sqrt(2.0)))
    return normal_cdf + argument * jnp.exp(-0.5 * argument * argument) / math.sqrt(2.0 * math.pi)

def reference(field, cotangent, spectral_weight, point_weight, bias):
    forward, doubled = yz_tables()
    cosine_table, sine_table = x_tables()
    batch = field.shape[0]
    mode_count = MY * MZ
    cell_count = NY * NZ
    contraction = (((1,), (1,)), ((), ()))

    def to_spectra(sample):
        product = jnp.dot(sample.reshape(C * NX, cell_count), forward, preferred_element_type=jnp.float32)
        return product.astype(jnp.bfloat16).reshape(C, NX, 2 * mode_count)
    spectra = lax.map(to_spectra, field)
    modes_re, modes_im = forward_x(spectra[..., :mode_count], spectra[..., mode_count:], cosine_table, sine_table)
    w_real = spectral_weight[..., :C]
    w_imag = spectral_weight[..., C:]
    mixing = 'bcij,ijco->boij'
    mixed_re = (contract(mixing, modes_re, w_real) - contract(mixing, modes_im, w_imag)).astype(jnp.bfloat16)
    mixed_im = (contract(mixing, modes_re, w_imag) + contract(mixing, modes_im, w_real)).astype(jnp.bfloat16)
    back_re, back_im = inverse_x(mixed_re, mixed_im, cosine_table, sine_table)
    back = jnp.concatenate([back_re, back_im], axis=3)

    def cell_pass(inputs_tuple):
        sample, grad_in, spectrum = inputs_tuple
        spectral_part = lax.dot_general(spectrum.reshape(C * NX, 2 * mode_count), doubled, contraction, preferred_element_type=jnp.float32).reshape(C, NX, cell_count)
        linear = jnp.dot(point_weight, sample.reshape(C, NX * cell_count), preferred_element_type=jnp.float32).reshape(C, NX, cell_count)
        preact = spectral_part + linear + bias[:, None, None]
        delta_cells = (grad_in.astype(jnp.float32) * gelu_slope(preact)).astype(jnp.bfloat16)
        weight_part = lax.dot_general(delta_cells.reshape(C, NX * cell_count), sample.reshape(C, NX * cell_count), contraction, preferred_element_type=jnp.float32)
        bias_part = lax.optimization_barrier(jnp.sum(delta_cells.astype(jnp.float32), axis=(1, 2)))
        grad_spectra = jnp.dot(delta_cells.reshape(C * NX, cell_count), doubled, preferred_element_type=jnp.float32)
        grad_spectra = grad_spectra.astype(jnp.bfloat16).reshape(C, NX, 2 * mode_count)
        return (delta_cells, grad_spectra, weight_part, bias_part)
    deltas, grad_spectra, weight_parts, bias_parts = lax.map(cell_pass, (field, cotangent, back))
    grad_re, grad_im = forward_x(grad_spectra[..., :mode_count], grad_spectra[..., mode_count:], cosine_table, sine_table)
    outer = 'bcij,boij->ijco'
    real_grad = contract(outer, modes_re, grad_re) + contract(outer, modes_im, grad_im)
    imag_grad = contract(outer, modes_re, grad_im) - contract(outer, modes_im, grad_re)
    spectral_grad = jnp.concatenate([real_grad, imag_grad], axis=3) * (1.0 / math.sqrt(batch))
    adjoint_mix = 'boij,ijco->bcij'
    adjoint_re = (contract(adjoint_mix, grad_re, w_real) + contract(adjoint_mix, grad_im, w_imag)).astype(jnp.bfloat16)
    adjoint_im = (contract(adjoint_mix, grad_im, w_real) - contract(adjoint_mix, grad_re, w_imag)).astype(jnp.bfloat16)
    adjoint_back_re, adjoint_back_im = inverse_x(adjoint_re, adjoint_im, cosine_table, sine_table)
    adjoint_back = jnp.concatenate([adjoint_back_re, adjoint_back_im], axis=3)

    def input_pass(inputs_tuple):
        delta_cells, spectrum = inputs_tuple
        spectral_part = lax.dot_general(spectrum.reshape(C * NX, 2 * mode_count), forward, contraction, preferred_element_type=jnp.float32).reshape(C, NX, cell_count)
        point_part = lax.dot_general(point_weight, delta_cells.reshape(C, NX * cell_count), (((0,), (0,)), ((), ())), preferred_element_type=jnp.float32).reshape(C, NX, cell_count)
        return (spectral_part + point_part).astype(jnp.bfloat16)
    input_grad = lax.map(input_pass, (deltas, adjoint_back))
    grad_scale = 1.0 / math.sqrt(batch * NX * NY * NZ)
    point_grad = lax.optimization_barrier(jnp.sum(weight_parts, axis=0)) * grad_scale
    bias_grad = lax.optimization_barrier(jnp.sum(bias_parts, axis=0)) * grad_scale
    return (input_grad, spectral_grad, point_grad, bias_grad)
```

```python
import functools
import math

import jax
import jax.numpy as jnp
import numpy as np
from jax import lax
from jax.experimental import pallas as pl
from jax.experimental.pallas import tpu as pltpu
from jax.sharding import PartitionSpec as P

C = 64
N = 64
XL = 4
S = 16
L = 16
CELLS = 4096
ROWS = C * XL
Q = 512
F32 = jnp.float32
BF16 = jnp.bfloat16


def mm(a, b):
    return jnp.dot(a, b, preferred_element_type=F32)


def nt(a, b):
    return lax.dot_general(a, b, (((1,), (1,)), ((), ())), preferred_element_type=F32)


def tn(a, b):
    return lax.dot_general(a, b, (((0,), (0,)), ((), ())), preferred_element_type=F32)


def waves(count, size):
    return np.array([i if i < count // 2 else size - count + i for i in range(count)])


def phase_tables():
    y = np.arange(CELLS) // N
    k = waves(S, N)
    ang = 2.0 * np.pi * ((k[:, None] * y[None, :]) % N) / N
    ang = ang[:, None, :] + np.array([0.0, np.pi / 2])[None, :, None]
    ang = ang.reshape(2 * S, CELLS)
    z = np.arange(128) % N
    angz = 2.0 * np.pi * ((np.arange(L)[:, None] * z[None, :]) % N) / N
    f = np.float32
    return (
        (np.cos(ang) / N).astype(f),
        (np.sin(ang) / N).astype(f),
        np.cos(angz).astype(f),
        np.sin(angz).astype(f),
    )


def x_tables():
    ang = 2.0 * np.pi * ((np.arange(N)[:, None] * waves(16, N)[None, :]) % N) / N
    return np.cos(ang) / 8.0, np.sin(ang) / 8.0


def constants():
    cos, sin = x_tables()
    perm = np.zeros((ROWS, ROWS))
    for c in range(C):
        for x in range(XL):
            perm[c * XL + x, x * C + c] = 1
    order = np.zeros((128, 128))
    for j in range(S):
        for x in range(XL):
            for a in range(2):
                order[j * 8 + x * 2 + a, x * 32 + j * 2 + a] = 1
    fx = np.zeros((64, 128))
    fo = np.zeros((64, 128))
    iv = np.zeros((128, 64))
    ia = np.zeros((128, 64))
    for i in range(16):
        for h in range(2):
            for x in range(N):
                c, s = cos[x, i], sin[x, i]
                re, im = i * 4 + h * 2, i * 4 + h * 2 + 1
                fx[re, 2 * x : 2 * x + 2] = (c, s)
                fx[im, 2 * x : 2 * x + 2] = (-s, c)
                fo[re, 2 * x : 2 * x + 2] = (-s, c)
                fo[im, 2 * x : 2 * x + 2] = (-c, -s)
                vre, vim = (re, im) if h == 0 else (im, re)
                iv[2 * x, vre], iv[2 * x, vim] = c, -s
                iv[2 * x + 1, vre], iv[2 * x + 1, vim] = s, c
                ia[2 * x, re], ia[2 * x, im] = c, -s
                ia[2 * x + 1, re], ia[2 * x + 1, im] = s, c
    ext = np.zeros((128, 128))
    for s in range(S):
        for r in range(4):
            ext[s * 8 + r, s * 4 + r] = 1
            ext[s * 8 + 4 + r, 64 + s * 4 + r] = 1
    gather = np.zeros((2, 128, 128))
    for i in range(16):
        for h in range(2):
            for q in range(4):
                gather[h, i * 8 + h * 4 + q, (q // 2) * 64 + i * 4 + q % 2] = 1
    pick = np.zeros((6, 32, 128))
    for b in range(16):
        for h in range(2):
            base = b * 8 + h * 4
            pick[h * 3, b * 2, base] = 1
            pick[h * 3, b * 2 + 1, base + 1] = 1
            pick[h * 3 + 1, b * 2, base + 2] = 1
            pick[h * 3 + 1, b * 2 + 1, base + 3] = 1
            pick[h * 3 + 2, b * 2, base + 3] = 1
            pick[h * 3 + 2, b * 2 + 1, base + 2] = -1
    bf = lambda v: jnp.asarray(np.asarray(v, np.float32), BF16)
    return {
        "perm": bf(perm),
        "order": bf(order),
        "order_t": bf(order.T),
        "fx": bf(fx),
        "fo": bf(fo),
        "iv": bf(iv),
        "ia": bf(ia),
        "ext": bf(ext),
        "ext_t": bf(ext.T),
        "gather": bf(gather),
        "pick": bf(pick),
    }


def lanes(shape):
    return lax.broadcasted_iota(jnp.int32, shape, 1)


def subl(shape):
    return lax.broadcasted_iota(jnp.int32, shape, 0)


def low_half(shape):
    return (lanes(shape) & 64) == 0


def half_turn(v):
    return pltpu.roll(v, 64, 1)


def pack_spectra(acc, perm, order, z_ref):
    s = mm(acc.astype(BF16), perm)
    low = low_half((32, 128))
    for u in range(L // 2):
        for t in range(2):
            a = s[u * 64 : u * 64 + 32, t * 128 : t * 128 + 128]
            b = s[u * 64 + 32 : u * 64 + 64, t * 128 : t * 128 + 128]
            even = jnp.where(low, a, half_turn(b))
            odd = jnp.where(low, half_turn(a), b)
            z_ref[t * 64 : t * 64 + 32, u * 128 : u * 128 + 128] = even.astype(BF16)
            z_ref[t * 64 + 32 : t * 64 + 64, u * 128 : u * 128 + 128] = odd.astype(BF16)
    return mm(order, z_ref[...]).astype(BF16)


def unpack_back(arrived, perm, order_t, b_ref, doubled):
    z = mm(order_t, arrived)
    low = low_half((32, 128))
    for u in range(L // 2):
        for t in range(2):
            a = z[t * 64 : t * 64 + 32, u * 128 : u * 128 + 128]
            b = z[t * 64 + 32 : t * 64 + 64, u * 128 : u * 128 + 128]
            first = jnp.where(low, a, half_turn(b))
            second = jnp.where(low, half_turn(a), b)
            if doubled:
                first = first * (1.0 if u == 0 else 2.0)
                second = second * 2.0
            b_ref[u * 64 : u * 64 + 32, t * 128 : t * 128 + 128] = first.astype(BF16)
            b_ref[u * 64 + 32 : u * 64 + 64, t * 128 : t * 128 + 128] = second.astype(BF16)
    return nt(perm, b_ref[...]).astype(BF16)


def split(v):
    hi = v.astype(BF16)
    lo = (v - hi.astype(F32)).astype(BF16)
    return jnp.where(low_half(v.shape), hi.astype(F32), lo.astype(F32)).astype(BF16)


def spread_weight(w, transposed):
    e = (subl((ROWS, C)) // XL == lanes((ROWS, C))).astype(BF16)
    left = tn(w, e.T) if False else mm(e, w)
    full = nt(left.astype(BF16), e)
    same = (subl((ROWS, ROWS)) & 3) == (lanes((ROWS, ROWS)) & 3)
    return jnp.where(same, full, 0.0).astype(BF16)


STEPS = 8
CHUNK = CELLS // STEPS


def spectra_kernel(f_ref, ca_ref, sa_ref, cb_ref, sb_ref, perm_ref, order_ref, out_ref, t_ref, acc_ref, z_ref):
    step = pl.program_id(0)
    for g in range(CHUNK // 128):
        cols = slice(g * 128, g * 128 + 128)
        ca, sa = ca_ref[:, cols], sa_ref[:, cols]
        for l in range(L):
            cb, sb = cb_ref[l : l + 1, :], sb_ref[l : l + 1, :]
            t_ref[l * 32 : l * 32 + 32, cols] = (ca * cb - sa * sb).astype(BF16)
    part = nt(t_ref[...], f_ref[...])

    @pl.when(step == 0)
    def _():
        acc_ref[...] = part

    @pl.when(step > 0)
    def _():
        acc_ref[...] += part

    @pl.when(step == STEPS - 1)
    def _():
        out_ref[...] = pack_spectra(acc_ref[...], perm_ref[...], order_ref[...], z_ref)


def mix_kernel(r_ref, w_ref, fx_ref, iv_ref, out_ref, m_ref, mask_ref, v_ref):
    u = pl.program_id(0)

    @pl.when(u == 0)
    def _():
        m = mm(fx_ref[...], r_ref[...])
        m_ref[...] = m.astype(BF16)
        shape = m.shape
        keep = ((lanes(shape) >> 6) & 1) == ((subl(shape) >> 1) & 1)
        mask_ref[...] = jnp.where(keep, m, 0.0)

    cols = pl.ds(pl.multiple_of(u * 128, 128), 128)
    row, lane = subl((8, 128)), lanes((8, 128))
    top = row < 4
    even = (row & 1) == 0
    sign = jnp.where(lane < 64, -1.0, 1.0)
    keep = (lane >> 6) == ((row >> 1) & 1)
    for t in range(8):
        left = mask_ref[8 * t : 8 * t + 8, cols].astype(BF16)
        right = jnp.concatenate(
            [w_ref[2 * t].reshape(128, 128), w_ref[2 * t + 1].reshape(128, 128)], axis=1
        )
        o = mm(left, right)
        res = jnp.where(top, o[:, :128], o[:, 128:])
        turned = half_turn(res)
        above = pltpu.roll(turned, 7, 0)
        below = pltpu.roll(turned, 1, 0)
        v = jnp.where(even, res + sign * above, below - sign * res)
        v_ref[8 * t : 8 * t + 8, cols] = jnp.where(keep, v, 0.0)

    @pl.when(u == L // 2 - 1)
    def _():
        out_ref[...] = mm(iv_ref[...], v_ref[...].astype(BF16)).astype(BF16)


def slope(v):
    a = jnp.abs(v)
    e = jnp.exp(v * v * -0.5)
    t = 1.0 / (1.0 + (0.3275911 / math.sqrt(2.0)) * a)
    poly = t * (
        0.5 * 0.254829592
        + t
        * (
            0.5 * -0.284496736
            + t * (0.5 * 1.421413741 + t * (0.5 * -1.453152027 + t * (0.5 * 1.061405429)))
        )
    )
    tail = poly * e
    return jnp.where(v < 0, tail, 1.0 - tail) + v * e * (1.0 / math.sqrt(2.0 * math.pi))


def delta_kernel(
    r_ref, f_ref, ct_ref, t_ref, w_ref, bias_ref, perm_ref, order_ref, order_t_ref, ext_ref,
    out_ref, d_ref, b_ref, lw_ref, pre_ref, s_ref, g_ref, bs_ref, bt_ref, z_ref,
):
    step = pl.program_id(0)

    @pl.when(step == 0)
    def _():
        b_ref[...] = unpack_back(r_ref[...], perm_ref[...], order_t_ref[...], bt_ref, True)
        lw_ref[...] = spread_weight(w_ref[...], False)
        s_ref[...] = jnp.zeros_like(s_ref)
        g_ref[...] = jnp.zeros_like(g_ref)
        bs_ref[...] = jnp.zeros_like(bs_ref)

    pre_ref[...] = mm(b_ref[...], t_ref[...]) + mm(lw_ref[...], f_ref[...])
    for r in range(0, ROWS, 16):
        rows = slice(r, r + 16)
        v = pre_ref[rows, :] + bias_ref[rows, :]
        d = (ct_ref[rows, :].astype(F32) * slope(v)).astype(BF16)
        d_ref[rows, :] = d
        df = d.astype(F32)
        part = df[:, :128]
        for g in range(1, CHUNK // 128):
            part = part + df[:, g * 128 : g * 128 + 128]
        bs_ref[rows, :] += part
    s_ref[...] += nt(t_ref[...], d_ref[...])
    g_ref[...] += nt(d_ref[...], f_ref[...])

    @pl.when(step == STEPS - 1)
    def _():
        doubled = jnp.where(subl((Q, ROWS)) < 32, 1.0, 2.0)
        out_ref[:, :1024] = pack_spectra(s_ref[...] * doubled, perm_ref[...], order_ref[...], z_ref)
        same = (subl((ROWS, ROWS)) & 3) == (lanes((ROWS, ROWS)) & 3)
        g = jnp.where(same, g_ref[...], 0.0)
        e = (subl((C, ROWS)) == lanes((C, ROWS)) // XL).astype(F32)
        e2 = ((subl((ROWS, 128)) // XL) == (lanes((ROWS, 128)) & 63)).astype(F32)
        hi = functools.partial(jnp.dot, precision=lax.Precision.HIGHEST, preferred_element_type=F32)
        wg = hi(hi(e, g), e2)
        bg = jnp.sum(hi(e, bs_ref[...]), axis=1, keepdims=True)
        both = jnp.concatenate([wg, jnp.broadcast_to(bg, (C, 128))], axis=0)
        out_ref[:, 1024:] = mm(ext_ref[...], split(both)).astype(BF16)


def total_of(ext):
    shape = (8, 128)
    pick = ((lanes(shape) & 7) == subl(shape)).astype(BF16)
    v = mm(pick, ext)
    return v + half_turn(v)


def spread_total(v):
    return jnp.concatenate([split(v).astype(F32)] * S, axis=0).astype(BF16)


def grad_modes_kernel(r_ref, m_ref, fx_ref, fo_ref, gather_ref, left_ref, dp_ref):
    r = r_ref[:, :1024]
    a = mm(fx_ref[...], r)
    b = mm(fo_ref[...], r)
    row = subl((64, 128))
    first = ((row >> 1) & 1) == 0
    low = low_half((64, 128))
    for u in range(8):
        cols = slice(u * 128, u * 128 + 128)
        au, bu = a[:, cols], b[:, cols]
        left_ref[:, cols] = jnp.where(
            first, jnp.where(low, au, half_turn(bu)), jnp.where(low, half_turn(au), bu)
        ).astype(BF16)
    both = jnp.concatenate([m_ref[...], a.astype(BF16)], axis=0)
    dp_ref[:, :512] = (
        mm(gather_ref[0], both[:, :512]) + mm(gather_ref[1], both[:, 512:])
    ).astype(BF16)
    dp_ref[:, 512:] = spread_total(total_of(r_ref[:, 1024:]))


def adjoint_kernel(left_ref, w_ref, out_ref):
    row, lane = subl((8, 128)), lanes((8, 128))
    top = row < 4
    keep = (lane >> 6) == ((row >> 1) & 1)
    for t in range(8):
        right = jnp.concatenate(
            [w_ref[2 * t].reshape(128, 128), w_ref[2 * t + 1].reshape(128, 128)], axis=0
        )
        o = nt(left_ref[8 * t : 8 * t + 8, :], right)
        res = jnp.where(top, o[:, :128], o[:, 128:])
        out_ref[8 * t : 8 * t + 8, :] = jnp.where(keep, res, 0.0).astype(BF16)


def adjoint_back_kernel(v_ref, dp_ref, ia_ref, out_ref):
    out_ref[:, :1024] = mm(ia_ref[...], v_ref[...]).astype(BF16)
    out_ref[:, 1024:] = spread_total(total_of(dp_ref[:, 512:]))


def weight_grad_kernel(dp_ref, pick_ref, out_ref):
    low = low_half((32, 128))
    data = dp_ref[:, :512]
    for h in range(2):
        m = mm(pick_ref[h * 3], data)
        g1 = mm(pick_ref[h * 3 + 1], data)
        g2 = mm(pick_ref[h * 3 + 2], data)
        for v in range(4):
            cols = slice(v * 128, v * 128 + 128)
            a, b = g1[:, cols], g2[:, cols]
            right = jnp.concatenate(
                [jnp.where(low, a, half_turn(b)), jnp.where(low, half_turn(a), b)], axis=1
            )
            o = tn(m[:, cols].astype(BF16), right.astype(BF16)) * 0.25
            l = h * 8 + v * 2
            out_ref[l] = o[:64, :128]
            out_ref[l + 1] = o[64:, 128:]


def input_grad_kernel(
    r_ref, d_ref, t_ref, w_ref, perm_ref, order_t_ref, ext_t_ref,
    out_ref, pg_ref, b_ref, lw_ref, bt_ref,
):
    step = pl.program_id(0)

    @pl.when(step == 0)
    def _():
        b_ref[...] = unpack_back(r_ref[:, :1024], perm_ref[...], order_t_ref[...], bt_ref, False)
        lw = spread_weight(w_ref[...], False).astype(F32)
        lw_ref[...] = lw.T.astype(BF16)
        v = mm(ext_t_ref[...], r_ref[:, 1024:])
        pg_ref[...] = (v + half_turn(v)) * (1.0 / 2048.0)

    out_ref[...] = (mm(b_ref[...], t_ref[...]) + mm(lw_ref[...], d_ref[...])).astype(BF16)


def whole(shape):
    return pl.BlockSpec(shape, lambda *_: (0,) * len(shape))


def chunked(rows):
    return pl.BlockSpec((rows, CHUNK), lambda i: (0, i))


def sds(shape, dtype=BF16):
    return jax.ShapeDtypeStruct(shape, dtype)


def exchange(v, axis):
    width = v.shape[1]
    out = lax.all_to_all(v.reshape(S, 8, width), axis, split_axis=0, concat_axis=0, tiled=True)
    return out.reshape(128, width)


def body(field, cotangent, spectral_weight, point_weight, bias):
    k = constants()
    ca, sa, cb, sb = (jnp.asarray(v) for v in phase_tables())
    field2 = field.reshape(ROWS, CELLS)
    cot2 = cotangent.reshape(ROWS, CELLS)
    bias_rows = jnp.broadcast_to(bias[:, None], (C, XL)).reshape(ROWS, 1)
    w_spec = pl.BlockSpec((16, 2, 64, 128), lambda u: (0, u, 0, 0))

    spectra, table = pl.pallas_call(
        spectra_kernel,
        grid=(STEPS,),
        in_specs=[chunked(ROWS), chunked(32), chunked(32), whole((L, 128)), whole((L, 128)),
                  whole((ROWS, ROWS)), whole((128, 128))],
        out_specs=[whole((128, 1024)), chunked(Q)],
        out_shape=[sds((128, 1024)), sds((Q, CELLS))],
        scratch_shapes=[pltpu.VMEM((Q, ROWS), F32), pltpu.VMEM((128, 1024), BF16)],
        name="spectra",
    )(field2, ca, sa, cb, sb, k["perm"], k["order"])
    arrived = exchange(spectra, "slab")

    back, modes = pl.pallas_call(
        mix_kernel,
        grid=(L // 2,),
        in_specs=[whole((128, 1024)), w_spec, whole((64, 128)), whole((128, 64))],
        out_specs=[whole((128, 1024)), whole((64, 1024))],
        out_shape=[sds((128, 1024)), sds((64, 1024))],
        scratch_shapes=[pltpu.VMEM((64, 1024), F32), pltpu.VMEM((64, 1024), F32)],
        name="mix",
    )(arrived, spectral_weight, k["fx"], k["iv"])
    arrived = exchange(back, "slab")

    grad_spectra, delta = pl.pallas_call(
        delta_kernel,
        grid=(STEPS,),
        in_specs=[whole((128, 1024)), chunked(ROWS), chunked(ROWS), chunked(Q), whole((C, C)),
                  whole((ROWS, 1)), whole((ROWS, ROWS)), whole((128, 128)), whole((128, 128)),
                  whole((128, 128))],
        out_specs=[whole((128, 1152)), chunked(ROWS)],
        out_shape=[sds((128, 1152)), sds((ROWS, CELLS))],
        scratch_shapes=[
            pltpu.VMEM((ROWS, Q), BF16),
            pltpu.VMEM((ROWS, ROWS), BF16),
            pltpu.VMEM((ROWS, CHUNK), F32),
            pltpu.VMEM((Q, ROWS), F32),
            pltpu.VMEM((ROWS, ROWS), F32),
            pltpu.VMEM((ROWS, 128), F32),
            pltpu.VMEM((Q, ROWS), BF16),
            pltpu.VMEM((128, 1024), BF16),
        ],
        name="delta",
    )(arrived, field2, cot2, table, point_weight, bias_rows, k["perm"], k["order"], k["order_t"],
      k["ext"])
    arrived = exchange(grad_spectra, "slab")

    left, shared = pl.pallas_call(
        grad_modes_kernel,
        out_shape=[sds((64, 1024)), sds((128, 640))],
        name="grad_modes",
    )(arrived, modes, k["fx"], k["fo"], k["gather"])
    shared = exchange(shared, "dp")

    adjoint = pl.pallas_call(
        adjoint_kernel,
        grid=(L // 2,),
        in_specs=[pl.BlockSpec((64, 128), lambda u: (0, u)), w_spec],
        out_specs=pl.BlockSpec((64, 128), lambda u: (0, u)),
        out_shape=sds((64, 1024)),
        name="adjoint",
    )(left, spectral_weight)
    adjoint_back = pl.pallas_call(
        adjoint_back_kernel,
        out_shape=sds((128, 1152)),
        name="adjoint_back",
    )(adjoint, shared, k["ia"])
    arrived = exchange(adjoint_back, "slab")

    spectral_grad = pl.pallas_call(
        weight_grad_kernel,
        out_shape=sds((L, C, 128), F32),
        name="weight_grad",
    )(shared, k["pick"])

    input_grad, small = pl.pallas_call(
        input_grad_kernel,
        grid=(STEPS,),
        in_specs=[whole((128, 1152)), chunked(ROWS), chunked(Q), whole((C, C)), whole((ROWS, ROWS)),
                  whole((128, 128)), whole((128, 128))],
        out_specs=[chunked(ROWS), whole((128, 128))],
        out_shape=[sds((ROWS, CELLS)), sds((128, 128), F32)],
        scratch_shapes=[
            pltpu.VMEM((ROWS, Q), BF16),
            pltpu.VMEM((ROWS, ROWS), BF16),
            pltpu.VMEM((Q, ROWS), BF16),
        ],
        name="input_grad",
    )(arrived, delta, table, point_weight, k["perm"], k["order_t"], k["ext_t"])
    return (
        input_grad.reshape(field.shape),
        spectral_grad[None],
        small[:C, :C],
        small[C:, 0],
    )


def solution(mesh):
    return jax.shard_map(
        body,
        mesh=mesh,
        in_specs=(
            P("dp", None, "slab", None),
            P("dp", None, "slab", None),
            P(None, "slab", None, None),
            P(),
            P(),
        ),
        out_specs=(P("dp", None, "slab", None), P("dp", "slab", None, None), P(), P()),
        check_vma=False,
    )
```

```python
import functools
import math

import jax
import jax.numpy as jnp
import numpy as np
from jax import lax
from jax.experimental import pallas as pl
from jax.experimental.pallas import tpu as pltpu
from jax.sharding import PartitionSpec as P

C = 64
N = 64
XL = 4
S = 16
L = 16
CELLS = 4096
ROWS = C * XL
Q = 512
F32 = jnp.float32
BF16 = jnp.bfloat16


def mm(a, b):
    return jnp.dot(a, b, preferred_element_type=F32)


def nt(a, b):
    return lax.dot_general(a, b, (((1,), (1,)), ((), ())), preferred_element_type=F32)


def tn(a, b):
    return lax.dot_general(a, b, (((0,), (0,)), ((), ())), preferred_element_type=F32)


def waves(count, size):
    return np.array([i if i < count // 2 else size - count + i for i in range(count)])


def phase_tables():
    f = np.float32
    k = np.repeat(waves(S, N), 2)[:, None]
    part = np.tile([0.0, np.pi / 2], S)[:, None]
    unit = 2.0 * np.pi / N
    ang = unit * (k * (np.arange(128) // N)[None, :]) + part
    turn = unit * np.broadcast_to(2 * k, (2 * S, 128))
    angz = unit * ((np.arange(L)[:, None] * (np.arange(128) % N)[None, :]) % N)
    pair = lambda a, scale: np.concatenate([np.cos(a), np.sin(a)]) * scale
    return np.concatenate([pair(ang, 1.0 / N), pair(turn, 1.0), pair(angz, 1.0)]).astype(f)


def x_tables():
    ang = 2.0 * np.pi * ((np.arange(N)[:, None] * waves(16, N)[None, :]) % N) / N
    return np.cos(ang) / 8.0, np.sin(ang) / 8.0


def constants():
    cos, sin = x_tables()
    fx = np.zeros((64, 128))
    fo = np.zeros((64, 128))
    iv = np.zeros((128, 64))
    ia = np.zeros((128, 64))
    for i in range(16):
        for h in range(2):
            for x in range(N):
                c, s = cos[x, i], sin[x, i]
                re, im = i * 4 + h * 2, i * 4 + h * 2 + 1
                fx[re, 2 * x : 2 * x + 2] = (c, s)
                fx[im, 2 * x : 2 * x + 2] = (-s, c)
                fo[re, 2 * x : 2 * x + 2] = (-s, c)
                fo[im, 2 * x : 2 * x + 2] = (-c, -s)
                vre, vim = (re, im) if h == 0 else (im, re)
                iv[2 * x, vre], iv[2 * x, vim] = c, -s
                iv[2 * x + 1, vre], iv[2 * x + 1, vim] = s, c
                ia[2 * x, re], ia[2 * x, im] = c, -s
                ia[2 * x + 1, re], ia[2 * x + 1, im] = s, c
    gather = np.zeros((2, 128, 128))
    for i in range(16):
        for h in range(2):
            for q in range(4):
                gather[h, i * 8 + h * 4 + q, (q // 2) * 64 + i * 4 + q % 2] = 1
    pick = np.zeros((6, 32, 128))
    for b in range(16):
        for h in range(2):
            base = b * 8 + h * 4
            pick[h * 3, b * 2, base] = 1
            pick[h * 3, b * 2 + 1, base + 1] = 1
            pick[h * 3 + 1, b * 2, base + 2] = 1
            pick[h * 3 + 1, b * 2 + 1, base + 3] = 1
            pick[h * 3 + 2, b * 2, base + 3] = 1
            pick[h * 3 + 2, b * 2 + 1, base + 2] = -1
    bf = lambda v: jnp.asarray(np.asarray(v, np.float32), BF16)
    return {
        "fx": bf(fx),
        "fo": bf(fo),
        "iv": bf(iv),
        "ia": bf(ia),
        "gather": bf(gather),
        "pick": bf(pick),
    }


def lanes(shape):
    return lax.broadcasted_iota(jnp.int32, shape, 1)


def subl(shape):
    return lax.broadcasted_iota(jnp.int32, shape, 0)


def low_half(shape):
    return (lanes(shape) & 64) == 0


def half_turn(v):
    return pltpu.roll(v, 64, 1)


def pack_spectra(acc, perm, order, z_ref):
    s = mm(acc.astype(BF16), perm)
    low = low_half((32, 128))
    for u in range(L // 2):
        for t in range(2):
            a = s[u * 64 : u * 64 + 32, t * 128 : t * 128 + 128]
            b = s[u * 64 + 32 : u * 64 + 64, t * 128 : t * 128 + 128]
            even = jnp.where(low, a, half_turn(b))
            odd = jnp.where(low, half_turn(a), b)
            z_ref[t * 64 : t * 64 + 32, u * 128 : u * 128 + 128] = even.astype(BF16)
            z_ref[t * 64 + 32 : t * 64 + 64, u * 128 : u * 128 + 128] = odd.astype(BF16)
    return mm(order, z_ref[...]).astype(BF16)


def unpack_back(arrived, perm, order_t, b_ref, doubled):
    z = mm(order_t, arrived)
    low = low_half((32, 128))
    for u in range(L // 2):
        for t in range(2):
            a = z[t * 64 : t * 64 + 32, u * 128 : u * 128 + 128]
            b = z[t * 64 + 32 : t * 64 + 64, u * 128 : u * 128 + 128]
            first = jnp.where(low, a, half_turn(b))
            second = jnp.where(low, half_turn(a), b)
            if doubled:
                first = first * (1.0 if u == 0 else 2.0)
                second = second * 2.0
            b_ref[u * 64 : u * 64 + 32, t * 128 : t * 128 + 128] = first.astype(BF16)
            b_ref[u * 64 + 32 : u * 64 + 64, t * 128 : t * 128 + 128] = second.astype(BF16)
    return nt(perm, b_ref[...]).astype(BF16)


def split(v):
    hi = v.astype(BF16)
    lo = (v - hi.astype(F32)).astype(BF16)
    return jnp.where(low_half(v.shape), hi.astype(F32), lo.astype(F32)).astype(BF16)


def spread_weight(w):
    e = (subl((ROWS, C)) // XL == lanes((ROWS, C))).astype(BF16)
    left = mm(e, w)
    full = nt(left.astype(BF16), e)
    same = (subl((ROWS, ROWS)) & 3) == (lanes((ROWS, ROWS)) & 3)
    return jnp.where(same, full, 0.0).astype(BF16)


def onehot(match):
    return jnp.where(match, 1.0, 0.0).astype(BF16)


def lane_order():
    r, k = subl((ROWS, ROWS)), lanes((ROWS, ROWS))
    return onehot(((r >> 2) == (k & 63)) & ((r & 3) == (k >> 6)))


def row_order(r, k):
    return onehot(((r >> 3) == ((k >> 1) & 15)) & (((r >> 1) & 3) == (k >> 5)) & ((r & 1) == (k & 1)))


def ext_order(r, k):
    return onehot(((r >> 3) == ((k >> 2) & 15)) & (((r >> 2) & 1) == (k >> 6)) & ((r & 3) == (k & 3)))


SQUARE = (128, 128)

STEPS = 8
CHUNK = CELLS // STEPS
EXACT = functools.partial(
    lax.dot_general, precision=lax.Precision.HIGHEST, preferred_element_type=F32
)
NT = (((1,), (1,)), ((), ()))
NN = (((1,), (0,)), ((), ()))


def at(step):
    return pl.ds(pl.multiple_of(step * CHUNK, CHUNK), CHUNK)


def planes(src, dst, sems, step):
    return pltpu.make_async_copy(src.at[:, :, at(step)], dst.at[:, :, at(step)], sems.at[step])


def columns(src, dst, sems, step):
    return pltpu.make_async_copy(src.at[:, at(step)], dst.at[:, at(step)], sems.at[step])


def modes_pair(src, dst, sems, u):
    return pltpu.make_async_copy(src.at[:, pl.ds(2 * u, 2)], dst.at[:, pl.ds(2 * u, 2)], sems.at[u])


def start_all(copy, src, dst, sems):
    for n in range(STEPS):
        copy(src, dst, sems, n).start()


def wait_all(copy, src, dst, sems):
    for n in range(STEPS):
        copy(src, dst, sems, n).wait()


def spectra_kernel(
    f_hbm, phase_hbm,
    out_ref, t_hbm, flat_hbm,
    f_ref, t_ref, flat_ref, ta_ref, tb_ref, acc_ref, pack_ref, phase_ref, f_sem, t_sem, p_sem, flat_sem,
):
    phases = pltpu.make_async_copy(phase_hbm, phase_ref, p_sem.at[0])
    phases.start()
    start_all(planes, f_hbm, f_ref, f_sem)
    acc_ref[...] = jnp.zeros_like(acc_ref)
    phases.wait()
    cr, sr = phase_ref[64:96, :], phase_ref[96:128, :]

    def make(n, ca, sa, buf_ref):
        for g in range(CHUNK // 128):
            cols = pl.ds(pl.multiple_of(n * CHUNK + g * 128, 128), 128)
            for l in range(L):
                v = (ca * phase_ref[128 + l : 129 + l, :] - sa * phase_ref[144 + l : 145 + l, :]).astype(BF16)
                buf_ref[l * 32 : l * 32 + 32, g * 128 : g * 128 + 128] = v
                t_ref[l * 32 : l * 32 + 32, cols] = v
            ca, sa = ca * cr - sa * sr, sa * cr + ca * sr
        return ca, sa

    def add(n, buf_ref):
        flat = f_ref[:, :, at(n)].reshape(ROWS, CHUNK)
        flat_ref[:, at(n)] = flat
        acc_ref[...] += nt(buf_ref[...], flat)
        columns(flat_ref, flat_hbm, flat_sem, n).start()

    ca, sa = make(0, phase_ref[:32, :], phase_ref[32:64, :], ta_ref)
    columns(t_ref, t_hbm, t_sem, 0).start()

    def step(m, carry):
        n = 2 * m
        planes(f_hbm, f_ref, f_sem, n).wait()
        planes(f_hbm, f_ref, f_sem, n + 1).wait()
        add(n, ta_ref)
        carry = make(n + 1, *carry, tb_ref)
        columns(t_ref, t_hbm, t_sem, n + 1).start()
        add(n + 1, tb_ref)
        carry = make(n + 2, *carry, ta_ref)
        columns(t_ref, t_hbm, t_sem, n + 2).start()
        return carry

    ca, sa = lax.fori_loop(0, STEPS // 2 - 1, step, (ca, sa))
    planes(f_hbm, f_ref, f_sem, STEPS - 2).wait()
    planes(f_hbm, f_ref, f_sem, STEPS - 1).wait()
    add(STEPS - 2, ta_ref)
    make(STEPS - 1, ca, sa, tb_ref)
    columns(t_ref, t_hbm, t_sem, STEPS - 1).start()
    add(STEPS - 1, tb_ref)
    out_ref[...] = pack_spectra(acc_ref[...], lane_order(), row_order(subl(SQUARE), lanes(SQUARE)), pack_ref)
    wait_all(columns, t_ref, t_hbm, t_sem)
    wait_all(columns, flat_ref, flat_hbm, flat_sem)


def mix_kernel(r_ref, w_hbm, fx_ref, iv_ref, out_ref, m_ref, w_ref, mask_ref, v_ref, w_sem):
    start_all(modes_pair, w_hbm, w_ref, w_sem)
    m = mm(fx_ref[...], r_ref[...])
    m_ref[...] = m.astype(BF16)
    shape = m.shape
    own = ((lanes(shape) >> 6) & 1) == ((subl(shape) >> 1) & 1)
    mask_ref[...] = jnp.where(own, m, 0.0)
    row, lane = subl((8, 128)), lanes((8, 128))
    top = row < 4
    even = (row & 1) == 0
    sign = jnp.where(lane < 64, -1.0, 1.0)
    keep = (lane >> 6) == ((row >> 1) & 1)

    def step(u, carry):
        cols = pl.ds(pl.multiple_of(u * 128, 128), 128)
        pair = pl.ds(2 * u, 2)
        modes_pair(w_hbm, w_ref, w_sem, u).wait()
        for t in range(8):
            left = mask_ref[8 * t : 8 * t + 8, cols].astype(BF16)
            right = jnp.concatenate(
                [w_ref[2 * t, pair].reshape(128, 128), w_ref[2 * t + 1, pair].reshape(128, 128)],
                axis=1,
            )
            o = mm(left, right)
            res = jnp.where(top, o[:, :128], o[:, 128:])
            turned = half_turn(res)
            above = pltpu.roll(turned, 7, 0)
            below = pltpu.roll(turned, 1, 0)
            v = jnp.where(even, res + sign * above, below - sign * res)
            v_ref[8 * t : 8 * t + 8, cols] = jnp.where(keep, v, 0.0)
        return carry

    lax.fori_loop(0, L // 2, step, 0)
    out_ref[...] = mm(iv_ref[...], v_ref[...].astype(BF16)).astype(BF16)


def slope(v):
    a = jnp.abs(v)
    e = jnp.exp(v * v * -0.5)
    t = 1.0 / (1.0 + (0.3275911 / math.sqrt(2.0)) * a)
    poly = t * (
        0.5 * 0.254829592
        + t
        * (
            0.5 * -0.284496736
            + t * (0.5 * 1.421413741 + t * (0.5 * -1.453152027 + t * (0.5 * 1.061405429)))
        )
    )
    tail = e * (poly - a * (1.0 / math.sqrt(2.0 * math.pi)))
    return jnp.where(v < 0, tail, 1.0 - tail)


def delta_kernel(
    r_ref, f_hbm, ct_hbm, t_hbm, w_ref, bias_ref,
    out_ref, d_hbm,
    f_ref, ct_ref, t_ref, d_ref, b_ref, lw_ref, shift_ref, pa_ref, pb_ref, da_ref, db_ref,
    s_ref, g_ref, bt_ref, z_ref, f_sem, ct_sem, t_sem, d_sem,
):
    for n in range(STEPS):
        columns(t_hbm, t_ref.at[:Q], t_sem, n).start()
        columns(f_hbm, f_ref, f_sem, n).start()
        columns(ct_hbm, ct_ref, ct_sem, n).start()
    t_ref[Q:, :] = jnp.ones((16, CELLS), BF16)
    b_ref[...] = unpack_back(
        r_ref[...], lane_order(), row_order(lanes(SQUARE), subl(SQUARE)), bt_ref, True
    )
    lw_ref[...] = spread_weight(w_ref[...])
    e = (subl((ROWS, C)) // XL == lanes((ROWS, C))).astype(F32)
    shift_ref[...] = EXACT(e, jnp.broadcast_to(bias_ref[...], (128, C)), NT)
    s_ref[...] = jnp.zeros_like(s_ref)
    g_ref[...] = jnp.zeros_like(g_ref)
    db_ref[...] = jnp.zeros_like(db_ref)

    def arrive(n):
        columns(t_hbm, t_ref.at[:Q], t_sem, n).wait()
        columns(f_hbm, f_ref, f_sem, n).wait()

    def before(n, p_ref, halves=(0, 1)):
        for h in halves:
            cols = pl.ds(pl.multiple_of(n * CHUNK + h * 256, 256), 256)
            p_ref[:, h * 256 : h * 256 + 256] = mm(b_ref[...], t_ref[:Q, cols]) + mm(
                lw_ref[...], f_ref[:, cols]
            )

    def add_spectra(n, own_ref, first, last):
        s_ref[first:last, :] += nt(t_ref[first:last, at(n)], own_ref[...])

    def add_point(n, own_ref):
        g_ref[...] += nt(own_ref[...], f_ref[:, at(n)])

    def bend(n, p_ref, own_ref, blocks):
        for r in blocks:
            rows = slice(r * 16, r * 16 + 16)
            v = p_ref[rows, :] + jnp.concatenate([shift_ref[rows, :]] * (CHUNK // 128), axis=1)
            d = (ct_ref[rows, at(n)].astype(F32) * slope(v)).astype(BF16)
            own_ref[rows, :] = d
            d_ref[rows, at(n)] = d

    def weave(n, p_ref, next_ref, own_ref, past_ref):
        past, later = jnp.maximum(n - 1, 0), jnp.minimum(n + 1, STEPS - 1)
        add_spectra(past, past_ref, 0, 256)
        bend(n, p_ref, own_ref, range(0, 3))
        add_spectra(past, past_ref, 256, Q + 16)
        bend(n, p_ref, own_ref, range(3, 6))
        add_point(past, past_ref)
        bend(n, p_ref, own_ref, range(6, 9))
        before(later, next_ref, (0,))
        bend(n, p_ref, own_ref, range(9, 12))
        before(later, next_ref, (1,))
        bend(n, p_ref, own_ref, range(12, 16))
        columns(d_ref, d_hbm, d_sem, n).start()

    arrive(0)
    before(0, pa_ref)

    def step(m, carry):
        n = 2 * m
        columns(ct_hbm, ct_ref, ct_sem, n).wait()
        columns(ct_hbm, ct_ref, ct_sem, n + 1).wait()
        arrive(n + 1)

        @pl.when(m < STEPS // 2 - 1)
        def _():
            arrive(n + 2)

        weave(n, pa_ref, pb_ref, da_ref, db_ref)
        weave(n + 1, pb_ref, pa_ref, db_ref, da_ref)
        return carry

    lax.fori_loop(0, STEPS // 2, step, 0)
    add_spectra(STEPS - 1, db_ref, 0, Q + 16)
    add_point(STEPS - 1, db_ref)
    doubled = jnp.where(subl((Q, ROWS)) < 32, 1.0, 2.0)
    out_ref[:, :1024] = pack_spectra(
        s_ref[:Q, :] * doubled, lane_order(), row_order(subl(SQUARE), lanes(SQUARE)), z_ref
    )
    same = (subl((ROWS, ROWS)) & 3) == (lanes((ROWS, ROWS)) & 3)
    g = jnp.where(same, g_ref[...], 0.0)
    e = (subl((C, ROWS)) == lanes((C, ROWS)) // XL).astype(F32)
    e2 = ((subl((ROWS, 128)) // XL) == (lanes((ROWS, 128)) & 63)).astype(F32)
    wg = EXACT(EXACT(e, g, NN), e2, NN)
    bg = EXACT(e, jnp.broadcast_to(s_ref[Q : Q + 1, :], (128, ROWS)), NT)
    both = jnp.concatenate([wg, bg], axis=0)
    out_ref[:, 1024:] = mm(ext_order(subl(SQUARE), lanes(SQUARE)), split(both)).astype(BF16)
    wait_all(columns, d_ref, d_hbm, d_sem)


def total_of(ext):
    shape = (8, 128)
    pick = ((lanes(shape) & 7) == subl(shape)).astype(BF16)
    v = mm(pick, ext)
    return v + half_turn(v)


def spread_total(v):
    return jnp.concatenate([split(v).astype(F32)] * S, axis=0).astype(BF16)


def grad_modes_kernel(r_ref, m_ref, fx_ref, fo_ref, gather_ref, left_ref, dp_ref):
    r = r_ref[:, :1024]
    a = mm(fx_ref[...], r)
    b = mm(fo_ref[...], r)
    row = subl((64, 128))
    first = ((row >> 1) & 1) == 0
    low = low_half((64, 128))
    for u in range(8):
        cols = slice(u * 128, u * 128 + 128)
        au, bu = a[:, cols], b[:, cols]
        left_ref[:, cols] = jnp.where(
            first, jnp.where(low, au, half_turn(bu)), jnp.where(low, half_turn(au), bu)
        ).astype(BF16)
    both = jnp.concatenate([m_ref[...], a.astype(BF16)], axis=0)
    dp_ref[:, :512] = (
        mm(gather_ref[0], both[:, :512]) + mm(gather_ref[1], both[:, 512:])
    ).astype(BF16)
    dp_ref[:, 512:] = spread_total(total_of(r_ref[:, 1024:]))


def adjoint_kernel(left_ref, w_hbm, ia_ref, out_ref, w_ref, v_ref, w_sem):
    start_all(modes_pair, w_hbm, w_ref, w_sem)
    row, lane = subl((8, 128)), lanes((8, 128))
    top = row < 4
    keep = (lane >> 6) == ((row >> 1) & 1)

    def step(u, carry):
        cols = pl.ds(pl.multiple_of(u * 128, 128), 128)
        pair = pl.ds(2 * u, 2)
        modes_pair(w_hbm, w_ref, w_sem, u).wait()
        for t in range(8):
            right = jnp.concatenate(
                [w_ref[2 * t, pair].reshape(128, 128), w_ref[2 * t + 1, pair].reshape(128, 128)],
                axis=0,
            )
            o = nt(left_ref[8 * t : 8 * t + 8, cols], right)
            res = jnp.where(top, o[:, :128], o[:, 128:])
            v_ref[8 * t : 8 * t + 8, cols] = jnp.where(keep, res, 0.0)
        return carry

    lax.fori_loop(0, L // 2, step, 0)
    out_ref[...] = mm(ia_ref[...], v_ref[...].astype(BF16)).astype(BF16)


def join_kernel(v_ref, dp_ref, out_ref):
    out_ref[:, :1024] = v_ref[...]
    out_ref[:, 1024:] = spread_total(total_of(dp_ref[:, 512:]))


def weight_grad_kernel(dp_ref, pick_ref, out_ref):
    low = low_half((32, 128))
    data = dp_ref[:, :512]
    for h in range(2):
        m = mm(pick_ref[h * 3], data)
        g1 = mm(pick_ref[h * 3 + 1], data)
        g2 = mm(pick_ref[h * 3 + 2], data)
        for v in range(4):
            cols = slice(v * 128, v * 128 + 128)
            a, b = g1[:, cols], g2[:, cols]
            right = jnp.concatenate(
                [jnp.where(low, a, half_turn(b)), jnp.where(low, half_turn(a), b)], axis=1
            )
            o = tn(m[:, cols].astype(BF16), right.astype(BF16)) * 0.25
            l = h * 8 + v * 2
            out_ref[l] = o[:64, :128]
            out_ref[l + 1] = o[64:, 128:]


def input_grad_kernel(
    r_ref, d_hbm, t_hbm, w_ref,
    out_hbm, pg_hbm, bg_hbm,
    d_ref, t_ref, o_ref, b_ref, lw_ref, bt_ref, pg_ref, bg_ref, d_sem, t_sem, o_sem, g_sem,
):
    for n in range(STEPS):
        columns(t_hbm, t_ref, t_sem, n).start()
        columns(d_hbm, d_ref, d_sem, n).start()
    b_ref[...] = unpack_back(
        r_ref[:, :1024], lane_order(), row_order(lanes(SQUARE), subl(SQUARE)), bt_ref, False
    )
    lw_ref[...] = spread_weight(w_ref[...]).astype(F32).T.astype(BF16)
    v = mm(ext_order(lanes(SQUARE), subl(SQUARE)), r_ref[:, 1024:])
    v = (v + half_turn(v)) * (1.0 / 2048.0)
    pg_ref[...] = v[:C, :C]
    diag = subl((C, C)) == lanes((C, C))
    bg_ref[...] = jnp.sum(jnp.where(diag, v[C:, :C], 0.0), axis=0, keepdims=True)
    small = [
        pltpu.make_async_copy(pg_ref, pg_hbm, g_sem.at[0]),
        pltpu.make_async_copy(bg_ref, bg_hbm, g_sem.at[1]),
    ]
    for copy in small:
        copy.start()

    def step(n, carry):
        columns(t_hbm, t_ref, t_sem, n).wait()
        columns(d_hbm, d_ref, d_sem, n).wait()
        out = mm(b_ref[...], t_ref[:, at(n)]) + mm(lw_ref[...], d_ref[:, at(n)])
        o_ref[:, :, at(n)] = out.astype(BF16).reshape(C, XL, CHUNK)
        planes(o_ref, out_hbm, o_sem, n).start()
        return carry

    lax.fori_loop(0, STEPS, step, 0)
    wait_all(planes, o_ref, out_hbm, o_sem)
    for copy in small:
        copy.wait()


def call(kernel, name, outs, scratch, args, big=(), big_outs=(), sems=0):
    place = lambda n, far: pl.BlockSpec(memory_space=pltpu.HBM if n in far else pltpu.VMEM)
    return pl.pallas_call(
        kernel,
        in_specs=[place(n, big) for n in range(len(args))],
        out_specs=[place(n, big_outs) for n in range(len(outs))],
        out_shape=[
            (pltpu.HBM if n in big_outs else pltpu.VMEM)(shape, dtype)
            for n, (shape, dtype) in enumerate(outs)
        ],
        scratch_shapes=[pltpu.VMEM(shape, dtype) for shape, dtype in scratch]
        + [pltpu.SemaphoreType.DMA((STEPS,))] * sems,
        compiler_params=pltpu.CompilerParams(vmem_limit_bytes=40 << 20),
        name=name,
    )(
        *[
            pltpu.with_memory_space_constraint(a, pltpu.HBM if n in big else pltpu.VMEM)
            for n, a in enumerate(args)
        ]
    )


def exchange(v, axis):
    width = v.shape[1]
    out = lax.all_to_all(v.reshape(S, 8, width), axis, split_axis=0, concat_axis=0, tiled=True)
    return out.reshape(128, width)


def body(field, cotangent, spectral_weight, point_weight, bias):
    k = constants()
    field3 = field.reshape(C, XL, CELLS)
    cot2 = cotangent.reshape(ROWS, CELLS)
    planes_shape = ((C, XL, CELLS), BF16)
    cells_shape = ((ROWS, CELLS), BF16)
    weight_shape = (spectral_weight.shape, BF16)

    spectra, table, flat = call(
        spectra_kernel,
        "spectra",
        [((128, 1024), BF16), ((Q, CELLS), BF16), cells_shape],
        [planes_shape, ((Q, CELLS), BF16), cells_shape, ((Q, CHUNK), BF16), ((Q, CHUNK), BF16),
         ((Q, ROWS), F32), ((128, 1024), BF16), ((160, 128), F32)],
        [field3, jnp.asarray(phase_tables())],
        big=(0, 1), big_outs=(1, 2), sems=4,
    )
    arrived = exchange(spectra, "slab")
    back, modes = call(
        mix_kernel,
        "mix",
        [((128, 1024), BF16), ((64, 1024), BF16)],
        [weight_shape, ((64, 1024), F32), ((64, 1024), F32)],
        [arrived, spectral_weight, k["fx"], k["iv"]],
        big=(1,), sems=1,
    )
    arrived = exchange(back, "slab")
    grad_spectra, delta = call(
        delta_kernel,
        "delta",
        [((128, 1152), BF16), cells_shape],
        [
            cells_shape, cells_shape, ((Q + 16, CELLS), BF16), cells_shape,
            ((ROWS, Q), BF16), ((ROWS, ROWS), BF16), ((ROWS, 128), F32),
            ((ROWS, CHUNK), F32), ((ROWS, CHUNK), F32), ((ROWS, CHUNK), BF16), ((ROWS, CHUNK), BF16),
            ((Q + 16, ROWS), F32), ((ROWS, ROWS), F32), ((Q, ROWS), BF16), ((128, 1024), BF16),
        ],
        [arrived, flat, cot2, table, point_weight, bias.reshape(1, C)],
        big=(1, 2, 3), big_outs=(1,), sems=4,
    )
    arrived = exchange(grad_spectra, "slab")
    left, shared = call(
        grad_modes_kernel,
        "grad_modes",
        [((64, 1024), BF16), ((128, 640), BF16)],
        [],
        [arrived, modes, k["fx"], k["fo"], k["gather"]],
    )
    shared = exchange(shared, "dp")
    (adjoint,) = call(
        adjoint_kernel,
        "adjoint",
        [((128, 1024), BF16)],
        [weight_shape, ((64, 1024), F32)],
        [left, spectral_weight, k["ia"]],
        big=(1,), sems=1,
    )
    (joined,) = call(join_kernel, "join", [((128, 1152), BF16)], [], [adjoint, shared])
    arrived = exchange(joined, "slab")
    (spectral_grad,) = call(
        weight_grad_kernel, "weight_grad", [((L, C, 128), F32)], [], [shared, k["pick"]]
    )
    input_grad, point_grad, bias_grad = call(
        input_grad_kernel,
        "input_grad",
        [planes_shape, ((C, C), F32), ((1, C), F32)],
        [cells_shape, ((Q, CELLS), BF16), planes_shape,
         ((ROWS, Q), BF16), ((ROWS, ROWS), BF16), ((Q, ROWS), BF16), ((C, C), F32), ((1, C), F32)],
        [arrived, delta, table, point_weight],
        big=(1, 2), big_outs=(0, 1, 2), sems=4,
    )
    return (
        input_grad.reshape(field.shape),
        spectral_grad[None],
        point_grad,
        bias_grad.reshape(C),
    )


def solution(mesh):
    return jax.shard_map(
        body,
        mesh=mesh,
        in_specs=(
            P("dp", None, "slab", None),
            P("dp", None, "slab", None),
            P(None, "slab", None, None),
            P(),
            P(),
        ),
        out_specs=(P("dp", None, "slab", None), P("dp", "slab", None, None), P(), P()),
        check_vma=False,
    )
```

```python
import functools
import math

import jax
import jax.numpy as jnp
import numpy as np
from jax import lax
from jax.experimental import pallas as pl
from jax.experimental.pallas import tpu as pltpu
from jax.sharding import PartitionSpec as P

C = 64
N = 64
XL = 4
S = 16
L = 16
CELLS = 4096
ROWS = C * XL
Q = 512
F32 = jnp.float32
BF16 = jnp.bfloat16


def mm(a, b):
    return jnp.dot(a, b, preferred_element_type=F32)


def nt(a, b):
    return lax.dot_general(a, b, (((1,), (1,)), ((), ())), preferred_element_type=F32)


def tn(a, b):
    return lax.dot_general(a, b, (((0,), (0,)), ((), ())), preferred_element_type=F32)


def waves(count, size):
    return np.array([i if i < count // 2 else size - count + i for i in range(count)])


def phase_tables():
    f = np.float32
    k = np.tile(waves(S, N), 2)[:, None]
    part = np.repeat([0.0, np.pi / 2], S)[:, None]
    unit = 2.0 * np.pi / N
    ang = unit * (k * (np.arange(128) // N)[None, :]) + part
    turn = unit * np.broadcast_to(2 * k, (2 * S, 128))
    angz = unit * ((np.arange(L)[:, None] * (np.arange(128) % N)[None, :]) % N)
    pair = lambda a, scale: np.concatenate([np.cos(a), np.sin(a)]) * scale
    return np.concatenate([pair(ang, 1.0 / N), pair(turn, 1.0), pair(angz, 1.0)]).astype(f)


def x_tables():
    ang = 2.0 * np.pi * ((np.arange(N)[:, None] * waves(16, N)[None, :]) % N) / N
    return np.cos(ang) / 8.0, np.sin(ang) / 8.0


def constants():
    cos, sin = x_tables()
    fx = np.zeros((64, 128))
    fo = np.zeros((64, 128))
    iv = np.zeros((128, 64))
    ia = np.zeros((128, 64))
    for i in range(16):
        for h in range(2):
            for x in range(N):
                c, s = cos[x, i], sin[x, i]
                re, im = i * 4 + h * 2, i * 4 + h * 2 + 1
                fx[re, 2 * x : 2 * x + 2] = (c, s)
                fx[im, 2 * x : 2 * x + 2] = (-s, c)
                fo[re, 2 * x : 2 * x + 2] = (-s, c)
                fo[im, 2 * x : 2 * x + 2] = (-c, -s)
                vre, vim = (re, im) if h == 0 else (im, re)
                iv[2 * x, vre], iv[2 * x, vim] = c, -s
                iv[2 * x + 1, vre], iv[2 * x + 1, vim] = s, c
                ia[2 * x, re], ia[2 * x, im] = c, -s
                ia[2 * x + 1, re], ia[2 * x + 1, im] = s, c
    gather = np.zeros((2, 128, 128))
    for i in range(16):
        for h in range(2):
            for q in range(4):
                gather[h, i * 8 + h * 4 + q, (q // 2) * 64 + i * 4 + q % 2] = 1
    pick = np.zeros((6, 32, 128))
    for b in range(16):
        for h in range(2):
            base = b * 8 + h * 4
            pick[h * 3, b * 2, base] = 1
            pick[h * 3, b * 2 + 1, base + 1] = 1
            pick[h * 3 + 1, b * 2, base + 2] = 1
            pick[h * 3 + 1, b * 2 + 1, base + 3] = 1
            pick[h * 3 + 2, b * 2, base + 3] = 1
            pick[h * 3 + 2, b * 2 + 1, base + 2] = -1
    bf = lambda v: jnp.asarray(np.asarray(v, np.float32), BF16)
    return {
        "fx": bf(fx),
        "fo": bf(fo),
        "iv": bf(iv),
        "ia": bf(ia),
        "gather": bf(gather),
        "pick": bf(pick),
    }


def lanes(shape):
    return lax.broadcasted_iota(jnp.int32, shape, 1)


def subl(shape):
    return lax.broadcasted_iota(jnp.int32, shape, 0)


def low_half(shape):
    return (lanes(shape) & 64) == 0


def half_turn(v):
    return pltpu.roll(v, 64, 1)


def pack_spectra(acc, perm, z_ref, out_ref):
    s = mm(acc.astype(BF16), perm)
    low = low_half((32, 128))

    def put(x, u, v):
        z_ref[u, pl.ds(2 * x, S, stride=8), :] = v[:S]
        z_ref[u, pl.ds(2 * x + 1, S, stride=8), :] = v[S:]

    for u in range(L // 2):
        for t in range(2):
            a = s[u * 64 : u * 64 + 32, t * 128 : t * 128 + 128]
            b = s[u * 64 + 32 : u * 64 + 64, t * 128 : t * 128 + 128]
            put(2 * t, u, jnp.where(low, a, half_turn(b)))
            put(2 * t + 1, u, jnp.where(low, half_turn(a), b))
    for u in range(L // 2):
        out_ref[:, u * 128 : u * 128 + 128] = z_ref[u].astype(BF16)


def unpack_back(arrived, perm, z_ref, b_ref, doubled):
    for u in range(L // 2):
        z_ref[u] = arrived[:, u * 128 : u * 128 + 128].astype(F32)
    low = low_half((32, 128))

    def take(x, u):
        parts = [z_ref[u, pl.ds(2 * x + p, S, stride=8), :] for p in range(2)]
        return jnp.concatenate(parts, axis=0)

    for u in range(L // 2):
        for t in range(2):
            a, b = take(2 * t, u), take(2 * t + 1, u)
            first = jnp.where(low, a, half_turn(b))
            second = jnp.where(low, half_turn(a), b)
            if doubled:
                first = first * (1.0 if u == 0 else 2.0)
                second = second * 2.0
            b_ref[u * 64 : u * 64 + 32, t * 128 : t * 128 + 128] = first.astype(BF16)
            b_ref[u * 64 + 32 : u * 64 + 64, t * 128 : t * 128 + 128] = second.astype(BF16)
    return nt(perm, b_ref[...]).astype(BF16)


def halves_of(v):
    hi = v.astype(BF16)
    return hi, (v - hi.astype(F32)).astype(BF16)


def split(v):
    hi, lo = halves_of(v)
    return jnp.where(low_half(v.shape), hi.astype(F32), lo.astype(F32)).astype(BF16)


def spread_weight(w):
    e = (subl((ROWS, C)) // XL == lanes((ROWS, C))).astype(BF16)
    left = mm(e, w)
    full = nt(left.astype(BF16), e)
    same = (subl((ROWS, ROWS)) & 3) == (lanes((ROWS, ROWS)) & 3)
    return jnp.where(same, full, 0.0).astype(BF16)


def onehot(match):
    return jnp.where(match, 1.0, 0.0).astype(BF16)


def lane_order():
    r, k = subl((ROWS, ROWS)), lanes((ROWS, ROWS))
    return onehot(((r >> 2) == (k & 63)) & ((r & 3) == (k >> 6)))


def ext_order(r, k):
    return onehot(((r >> 3) == ((k >> 2) & 15)) & (((r >> 2) & 1) == (k >> 6)) & ((r & 3) == (k & 3)))


SQUARE = (128, 128)

STEPS = 8
CHUNK = CELLS // STEPS
EXACT = functools.partial(
    lax.dot_general, precision=lax.Precision.HIGHEST, preferred_element_type=F32
)
NT = (((1,), (1,)), ((), ()))
NN = (((1,), (0,)), ((), ()))


def at(step):
    if isinstance(step, int):
        return slice(step * CHUNK, step * CHUNK + CHUNK)
    return pl.ds(pl.multiple_of(step * CHUNK, CHUNK), CHUNK)


def planes(src, dst, sems, step):
    return pltpu.make_async_copy(src.at[:, :, at(step)], dst.at[:, :, at(step)], sems.at[step])


def columns(src, dst, sems, step):
    return pltpu.make_async_copy(src.at[:, at(step)], dst.at[:, at(step)], sems.at[step])


def modes_pair(src, dst, sems, u):
    return pltpu.make_async_copy(src.at[:, pl.ds(2 * u, 2)], dst.at[:, pl.ds(2 * u, 2)], sems.at[u])


def start_all(copy, src, dst, sems):
    for n in range(STEPS):
        copy(src, dst, sems, n).start()


def wait_all(copy, src, dst, sems):
    for n in range(STEPS):
        copy(src, dst, sems, n).wait()


def spectra_kernel(
    f_hbm, phase_hbm,
    out_ref, t_hbm,
    f_ref, t_ref, ta_ref, tb_ref, acc_ref, z_ref, phase_ref, f_sem, t_sem, p_sem,
):
    phases = pltpu.make_async_copy(phase_hbm, phase_ref, p_sem.at[0])
    phases.start()
    start_all(planes, f_hbm, f_ref, f_sem)
    acc_ref[...] = jnp.zeros_like(acc_ref)
    perm = lane_order()
    phases.wait()
    cr, sr = phase_ref[64:96, :], phase_ref[96:128, :]

    def make(n, ca, sa, buf_ref, tiles):
        for g in tiles:
            cols = pl.ds(pl.multiple_of(n * CHUNK + g * 128, 128), 128)
            for l in range(L):
                cb, sb = phase_ref[128 + l : 129 + l, :], phase_ref[144 + l : 145 + l, :]
                v = (ca * cb - sa * sb).astype(BF16)
                buf_ref[l * 32 : l * 32 + 32, g * 128 : g * 128 + 128] = v
                t_ref[l * 32 : l * 32 + 32, cols] = v
            ca, sa = ca * cr - sa * sr, sa * cr + ca * sr
        return ca, sa

    def add(n, buf_ref, first):
        acc_ref[first : first + 256, :] += nt(
            buf_ref[first : first + 256, :], f_ref[:, :, at(n)].reshape(ROWS, CHUNK)
        )

    def weave(n, ca, sa, own_ref, next_ref):
        add(n, own_ref, 0)
        ca, sa = make(n + 1, ca, sa, next_ref, (0, 1))
        add(n, own_ref, 256)
        ca, sa = make(n + 1, ca, sa, next_ref, (2, 3))
        columns(t_ref, t_hbm, t_sem, n + 1).start()
        return ca, sa

    ca, sa = make(0, phase_ref[:32, :], phase_ref[32:64, :], ta_ref, range(4))
    columns(t_ref, t_hbm, t_sem, 0).start()

    def step(m, carry):
        n = 2 * m
        planes(f_hbm, f_ref, f_sem, n).wait()
        planes(f_hbm, f_ref, f_sem, n + 1).wait()
        carry = weave(n, *carry, ta_ref, tb_ref)
        return weave(n + 1, *carry, tb_ref, ta_ref)

    ca, sa = lax.fori_loop(0, STEPS // 2 - 1, step, (ca, sa))
    planes(f_hbm, f_ref, f_sem, STEPS - 2).wait()
    planes(f_hbm, f_ref, f_sem, STEPS - 1).wait()
    weave(STEPS - 2, ca, sa, ta_ref, tb_ref)
    add(STEPS - 1, tb_ref, 0)
    add(STEPS - 1, tb_ref, 256)
    pack_spectra(acc_ref[...], perm, z_ref, out_ref)
    wait_all(columns, t_ref, t_hbm, t_sem)


def mix_kernel(r_ref, w_hbm, fx_ref, iv_ref, out_ref, m_ref, w_ref, mask_ref, v_ref, w_sem):
    start_all(modes_pair, w_hbm, w_ref, w_sem)
    m = mm(fx_ref[...], r_ref[...])
    m_ref[...] = m.astype(BF16)
    shape = m.shape
    own = ((lanes(shape) >> 6) & 1) == ((subl(shape) >> 1) & 1)
    mask_ref[...] = jnp.where(own, m, 0.0)
    row, lane = subl((8, 128)), lanes((8, 128))
    top = row < 4
    even = (row & 1) == 0
    sign = jnp.where(lane < 64, -1.0, 1.0)
    keep = (lane >> 6) == ((row >> 1) & 1)

    def step(u, carry):
        cols = pl.ds(pl.multiple_of(u * 128, 128), 128)
        pair = pl.ds(2 * u, 2)
        modes_pair(w_hbm, w_ref, w_sem, u).wait()
        for t in range(8):
            left = mask_ref[8 * t : 8 * t + 8, cols].astype(BF16)
            right = jnp.concatenate(
                [w_ref[2 * t, pair].reshape(128, 128), w_ref[2 * t + 1, pair].reshape(128, 128)],
                axis=1,
            )
            o = mm(left, right)
            res = jnp.where(top, o[:, :128], o[:, 128:])
            turned = half_turn(res)
            above = pltpu.roll(turned, 7, 0)
            below = pltpu.roll(turned, 1, 0)
            v = jnp.where(even, res + sign * above, below - sign * res)
            v_ref[8 * t : 8 * t + 8, cols] = jnp.where(keep, v, 0.0)
        return carry

    lax.fori_loop(0, L // 2, step, 0)
    out_ref[...] = mm(iv_ref[...], v_ref[...].astype(BF16)).astype(BF16)


def slope(v):
    a = jnp.abs(v)
    e = jnp.exp(v * v * -0.5)
    t = 1.0 / (1.0 + (0.3275911 / math.sqrt(2.0)) * a)
    poly = t * (
        0.5 * 0.254829592
        + t
        * (
            0.5 * -0.284496736
            + t * (0.5 * 1.421413741 + t * (0.5 * -1.453152027 + t * (0.5 * 1.061405429)))
        )
    )
    tail = e * (poly - a * (1.0 / math.sqrt(2.0 * math.pi)))
    return jnp.where(v < 0, tail, 1.0 - tail)


def delta_kernel(
    r_ref, f_hbm, ct_hbm, t_hbm, w_ref, bias_ref,
    out_ref, d_hbm,
    ct_ref, tf_ref, d_ref, bl_ref, shift_ref, pa_ref, pb_ref, da_ref, db_ref,
    sg_ref, bt_ref, z_ref, f_sem, ct_sem, t_sem, d_sem,
):
    table, flat = tf_ref.at[:Q], tf_ref.at[Q : Q + ROWS]
    for n in range(STEPS):
        columns(t_hbm, table, t_sem, n).start()
        columns(f_hbm, flat, f_sem, n).start()
        columns(ct_hbm, ct_ref, ct_sem, n).start()
    tf_ref[Q + ROWS :, :] = jnp.ones((16, CELLS), BF16)
    bl_ref[:, :Q] = unpack_back(r_ref[...], lane_order(), z_ref, bt_ref, True)
    bl_ref[:, Q:] = spread_weight(w_ref[...])
    e = (subl((ROWS, C)) // XL == lanes((ROWS, C))).astype(F32)
    shift_ref[...] = EXACT(e, jnp.broadcast_to(bias_ref[...], (128, C)), NT)
    sg_ref[...] = jnp.zeros_like(sg_ref)
    db_ref[...] = jnp.zeros_like(db_ref)

    def arrive(n):
        columns(t_hbm, table, t_sem, n).wait()
        columns(f_hbm, flat, f_sem, n).wait()

    def before(n, p_ref, halves=(0, 1)):
        for h in halves:
            cols = pl.ds(pl.multiple_of(n * CHUNK + h * 256, 256), 256)
            p_ref[:, h * 256 : h * 256 + 256] = mm(bl_ref[...], tf_ref[: Q + ROWS, cols])

    def add(n, own_ref, first, last):
        sg_ref[first:last, :] += nt(tf_ref[first:last, at(n)], own_ref[...])

    def bend(n, p_ref, own_ref, blocks):
        for r in blocks:
            rows = slice(r * 16, r * 16 + 16)
            v = p_ref[rows, :] + jnp.concatenate([shift_ref[rows, :]] * (CHUNK // 128), axis=1)
            d = (ct_ref[rows, at(n)].astype(F32) * slope(v)).astype(BF16)
            own_ref[rows, :] = d
            d_ref[rows, at(n)] = d

    def weave(n, p_ref, next_ref, own_ref, past_ref):
        past, later = jnp.maximum(n - 1, 0), jnp.minimum(n + 1, STEPS - 1)
        add(past, past_ref, 0, 256)
        bend(n, p_ref, own_ref, range(0, 3))
        add(past, past_ref, 256, 512)
        bend(n, p_ref, own_ref, range(3, 6))
        add(past, past_ref, 512, 784)
        bend(n, p_ref, own_ref, range(6, 9))
        before(later, next_ref, (0,))
        bend(n, p_ref, own_ref, range(9, 12))
        before(later, next_ref, (1,))
        bend(n, p_ref, own_ref, range(12, 16))
        columns(d_ref, d_hbm, d_sem, n).start()

    arrive(0)
    before(0, pa_ref)

    def step(m, carry):
        n = 2 * m
        columns(ct_hbm, ct_ref, ct_sem, n).wait()
        columns(ct_hbm, ct_ref, ct_sem, n + 1).wait()
        arrive(n + 1)

        @pl.when(m < STEPS // 2 - 1)
        def _():
            arrive(n + 2)

        weave(n, pa_ref, pb_ref, da_ref, db_ref)
        weave(n + 1, pb_ref, pa_ref, db_ref, da_ref)
        return carry

    lax.fori_loop(0, STEPS // 2, step, 0)
    add(STEPS - 1, db_ref, 0, 784)
    doubled = jnp.where(subl((Q, ROWS)) < 32, 1.0, 2.0)
    pack_spectra(sg_ref[:Q, :] * doubled, lane_order(), z_ref, out_ref)
    same = (subl((ROWS, ROWS)) & 3) == (lanes((ROWS, ROWS)) & 3)
    g = jnp.where(same, sg_ref[Q : Q + ROWS, :], 0.0)
    e = onehot(subl((C, ROWS)) == lanes((C, ROWS)) // XL)
    e2 = onehot((subl((ROWS, 128)) // XL) == (lanes((ROWS, 128)) & 63))
    wg = [nt(e, half) for half in halves_of(g)]
    wg = [mm(half, e2) for half in halves_of(wg[0] + wg[1])]
    sums = jnp.broadcast_to(sg_ref[Q + ROWS : Q + ROWS + 1, :], (128, ROWS))
    bg = [nt(e, half) for half in halves_of(sums)]
    both = jnp.concatenate([wg[0] + wg[1], bg[0] + bg[1]], axis=0)
    out_ref[:, 1024:] = mm(ext_order(subl(SQUARE), lanes(SQUARE)), split(both)).astype(BF16)
    wait_all(columns, d_ref, d_hbm, d_sem)


def total_of(ext):
    shape = (8, 128)
    pick = ((lanes(shape) & 7) == subl(shape)).astype(BF16)
    v = mm(pick, ext)
    return v + half_turn(v)


def spread_total(v):
    return jnp.concatenate([split(v).astype(F32)] * S, axis=0).astype(BF16)


def grad_modes_kernel(r_ref, m_ref, fx_ref, fo_ref, gather_ref, left_ref, dp_ref):
    r = r_ref[:, :1024]
    a = mm(fx_ref[...], r)
    b = mm(fo_ref[...], r)
    row = subl((64, 128))
    first = ((row >> 1) & 1) == 0
    low = low_half((64, 128))
    for u in range(8):
        cols = slice(u * 128, u * 128 + 128)
        au, bu = a[:, cols], b[:, cols]
        left_ref[:, cols] = jnp.where(
            first, jnp.where(low, au, half_turn(bu)), jnp.where(low, half_turn(au), bu)
        ).astype(BF16)
    both = jnp.concatenate([m_ref[...], a.astype(BF16)], axis=0)
    dp_ref[:, :512] = (
        mm(gather_ref[0], both[:, :512]) + mm(gather_ref[1], both[:, 512:])
    ).astype(BF16)
    dp_ref[:, 512:] = spread_total(total_of(r_ref[:, 1024:]))


def adjoint_kernel(left_ref, w_hbm, ia_ref, out_ref, w_ref, v_ref, w_sem):
    start_all(modes_pair, w_hbm, w_ref, w_sem)
    row, lane = subl((8, 128)), lanes((8, 128))
    top = row < 4
    keep = (lane >> 6) == ((row >> 1) & 1)

    def step(u, carry):
        cols = pl.ds(pl.multiple_of(u * 128, 128), 128)
        pair = pl.ds(2 * u, 2)
        modes_pair(w_hbm, w_ref, w_sem, u).wait()
        for t in range(8):
            right = jnp.concatenate(
                [w_ref[2 * t, pair].reshape(128, 128), w_ref[2 * t + 1, pair].reshape(128, 128)],
                axis=0,
            )
            o = nt(left_ref[8 * t : 8 * t + 8, cols], right)
            res = jnp.where(top, o[:, :128], o[:, 128:])
            v_ref[8 * t : 8 * t + 8, cols] = jnp.where(keep, res, 0.0)
        return carry

    lax.fori_loop(0, L // 2, step, 0)
    out_ref[...] = mm(ia_ref[...], v_ref[...].astype(BF16)).astype(BF16)


def join_kernel(v_ref, dp_ref, out_ref):
    out_ref[:, :1024] = v_ref[...]
    out_ref[:, 1024:] = spread_total(total_of(dp_ref[:, 512:]))


def weight_grad_kernel(dp_ref, pick_ref, out_ref):
    low = low_half((32, 128))
    data = dp_ref[:, :512]
    for h in range(2):
        m = mm(pick_ref[h * 3], data)
        g1 = mm(pick_ref[h * 3 + 1], data)
        g2 = mm(pick_ref[h * 3 + 2], data)
        for v in range(4):
            cols = slice(v * 128, v * 128 + 128)
            a, b = g1[:, cols], g2[:, cols]
            right = jnp.concatenate(
                [jnp.where(low, a, half_turn(b)), jnp.where(low, half_turn(a), b)], axis=1
            )
            o = tn(m[:, cols].astype(BF16), right.astype(BF16)) * 0.25
            l = h * 8 + v * 2
            out_ref[l] = o[:64, :128]
            out_ref[l + 1] = o[64:, 128:]


def input_grad_kernel(
    r_ref, d_hbm, t_hbm, w_ref,
    out_hbm, pg_hbm, bg_hbm,
    td_ref, o_ref, bl_ref, bt_ref, z_ref, pg_ref, bg_ref, d_sem, t_sem, o_sem, g_sem,
):
    table, delta = td_ref.at[:Q], td_ref.at[Q:]
    for n in range(STEPS):
        columns(t_hbm, table, t_sem, n).start()
        columns(d_hbm, delta, d_sem, n).start()
    bl_ref[:, :Q] = unpack_back(r_ref[:, :1024], lane_order(), z_ref, bt_ref, False)
    bl_ref[:, Q:] = spread_weight(w_ref[...]).astype(F32).T.astype(BF16)
    v = mm(ext_order(lanes(SQUARE), subl(SQUARE)), r_ref[:, 1024:])
    v = (v + half_turn(v)) * (1.0 / 2048.0)
    pg_ref[...] = v[:C, :C]
    diag = subl((C, C)) == lanes((C, C))
    bg_ref[...] = jnp.sum(jnp.where(diag, v[C:, :C], 0.0), axis=0, keepdims=True)
    small = [
        pltpu.make_async_copy(pg_ref, pg_hbm, g_sem.at[0]),
        pltpu.make_async_copy(bg_ref, bg_hbm, g_sem.at[1]),
    ]
    for copy in small:
        copy.start()
    for p in range(STEPS // 2):
        for n in (2 * p, 2 * p + 1):
            columns(t_hbm, table, t_sem, n).wait()
            columns(d_hbm, delta, d_sem, n).wait()
        for n in (2 * p, 2 * p + 1):
            out = mm(bl_ref[...], td_ref[:, at(n)])
            o_ref[:, :, at(n)] = out.astype(BF16).reshape(C, XL, CHUNK)
        for n in (2 * p, 2 * p + 1):
            planes(o_ref, out_hbm, o_sem, n).start()
    wait_all(planes, o_ref, out_hbm, o_sem)
    for copy in small:
        copy.wait()


def call(kernel, name, outs, scratch, args, big=(), big_outs=(), sems=0):
    place = lambda n, far: pl.BlockSpec(memory_space=pltpu.HBM if n in far else pltpu.VMEM)
    return pl.pallas_call(
        kernel,
        in_specs=[place(n, big) for n in range(len(args))],
        out_specs=[place(n, big_outs) for n in range(len(outs))],
        out_shape=[
            (pltpu.HBM if n in big_outs else pltpu.VMEM)(shape, dtype)
            for n, (shape, dtype) in enumerate(outs)
        ],
        scratch_shapes=[pltpu.VMEM(shape, dtype) for shape, dtype in scratch]
        + [pltpu.SemaphoreType.DMA((STEPS,))] * sems,
        compiler_params=pltpu.CompilerParams(vmem_limit_bytes=40 << 20),
        name=name,
    )(
        *[
            pltpu.with_memory_space_constraint(a, pltpu.HBM if n in big else pltpu.VMEM)
            for n, a in enumerate(args)
        ]
    )


def exchange(v, axis):
    width = v.shape[1]
    out = lax.all_to_all(v.reshape(S, 8, width), axis, split_axis=0, concat_axis=0, tiled=True)
    return out.reshape(128, width)


def body(field, cotangent, spectral_weight, point_weight, bias):
    k = constants()
    field3 = field.reshape(C, XL, CELLS)
    flat = field.reshape(ROWS, CELLS)
    cot2 = cotangent.reshape(ROWS, CELLS)
    planes_shape = ((C, XL, CELLS), BF16)
    cells_shape = ((ROWS, CELLS), BF16)
    weight_shape = (spectral_weight.shape, BF16)

    spectra, table = call(
        spectra_kernel,
        "spectra",
        [((128, 1024), BF16), ((Q, CELLS), BF16)],
        [planes_shape, ((Q, CELLS), BF16), ((Q, CHUNK), BF16), ((Q, CHUNK), BF16), ((Q, ROWS), F32), ((L // 2, 128, 128), F32),
         ((160, 128), F32)],
        [field3, jnp.asarray(phase_tables())],
        big=(0, 1), big_outs=(1,), sems=3,
    )
    arrived, flat = lax.optimization_barrier((exchange(spectra, "slab"), flat))
    back, modes = call(
        mix_kernel,
        "mix",
        [((128, 1024), BF16), ((64, 1024), BF16)],
        [weight_shape, ((64, 1024), F32), ((64, 1024), F32)],
        [arrived, spectral_weight, k["fx"], k["iv"]],
        big=(1,), sems=1,
    )
    arrived = exchange(back, "slab")
    grad_spectra, delta = call(
        delta_kernel,
        "delta",
        [((128, 1152), BF16), cells_shape],
        [
            cells_shape, ((Q + ROWS + 16, CELLS), BF16), cells_shape,
            ((ROWS, Q + ROWS), BF16), ((ROWS, 128), F32),
            ((ROWS, CHUNK), F32), ((ROWS, CHUNK), F32), ((ROWS, CHUNK), BF16), ((ROWS, CHUNK), BF16),
            ((Q + ROWS + 16, ROWS), F32), ((Q, ROWS), BF16), ((L // 2, 128, 128), F32),
        ],
        [arrived, flat, cot2, table, point_weight, bias.reshape(1, C)],
        big=(1, 2, 3), big_outs=(1,), sems=4,
    )
    arrived = exchange(grad_spectra, "slab")
    left, shared = call(
        grad_modes_kernel,
        "grad_modes",
        [((64, 1024), BF16), ((128, 640), BF16)],
        [],
        [arrived, modes, k["fx"], k["fo"], k["gather"]],
    )
    shared = exchange(shared, "dp")
    (adjoint,) = call(
        adjoint_kernel,
        "adjoint",
        [((128, 1024), BF16)],
        [weight_shape, ((64, 1024), F32)],
        [left, spectral_weight, k["ia"]],
        big=(1,), sems=1,
    )
    (joined,) = call(join_kernel, "join", [((128, 1152), BF16)], [], [adjoint, shared])
    arrived = exchange(joined, "slab")
    (spectral_grad,) = call(
        weight_grad_kernel, "weight_grad", [((L, C, 128), F32)], [], [shared, k["pick"]]
    )
    input_grad, point_grad, bias_grad = call(
        input_grad_kernel,
        "input_grad",
        [planes_shape, ((C, C), F32), ((1, C), F32)],
        [((Q + ROWS, CELLS), BF16), planes_shape, ((ROWS, Q + ROWS), BF16), ((Q, ROWS), BF16),
         ((L // 2, 128, 128), F32), ((C, C), F32), ((1, C), F32)],
        [arrived, delta, table, point_weight],
        big=(1, 2), big_outs=(0, 1, 2), sems=4,
    )
    return (
        input_grad.reshape(field.shape),
        spectral_grad[None],
        point_grad,
        bias_grad.reshape(C),
    )


def solution(mesh):
    return jax.shard_map(
        body,
        mesh=mesh,
        in_specs=(
            P("dp", None, "slab", None),
            P("dp", None, "slab", None),
            P(None, "slab", None, None),
            P(),
            P(),
        ),
        out_specs=(P("dp", None, "slab", None), P("dp", "slab", None, None), P(), P()),
        check_vma=False,
    )
```

```python
import functools
import math

import jax
import jax.numpy as jnp
import numpy as np
from jax import lax
from jax.experimental import pallas as pl
from jax.experimental.pallas import tpu as pltpu
from jax.sharding import PartitionSpec as P

C = 64
N = 64
XL = 4
S = 16
L = 16
CELLS = 4096
ROWS = C * XL
Q = 512
F32 = jnp.float32
BF16 = jnp.bfloat16


def mm(a, b):
    return jnp.dot(a, b, preferred_element_type=F32)


def nt(a, b):
    return lax.dot_general(a, b, (((1,), (1,)), ((), ())), preferred_element_type=F32)


def tn(a, b):
    return lax.dot_general(a, b, (((0,), (0,)), ((), ())), preferred_element_type=F32)


def waves(count, size):
    return np.array([i if i < count // 2 else size - count + i for i in range(count)])


def phase_tables():
    f = np.float32
    k = np.tile(waves(S, N), 2)[:, None]
    part = np.repeat([0.0, np.pi / 2], S)[:, None]
    unit = 2.0 * np.pi / N
    ang = unit * (k * (np.arange(128) // N)[None, :]) + part
    turn = unit * np.broadcast_to(2 * k, (2 * S, 128))
    angz = unit * ((np.arange(L)[:, None] * (np.arange(128) % N)[None, :]) % N)
    pair = lambda a, scale: np.concatenate([np.cos(a), np.sin(a)]) * scale
    return np.concatenate([pair(ang, 1.0 / N), pair(turn, 1.0), pair(angz, 1.0)]).astype(f)


def x_tables():
    ang = 2.0 * np.pi * ((np.arange(N)[:, None] * waves(16, N)[None, :]) % N) / N
    return np.cos(ang) / 8.0, np.sin(ang) / 8.0


def constants():
    cos, sin = x_tables()
    fx = np.zeros((64, 128))
    fo = np.zeros((64, 128))
    iv = np.zeros((128, 64))
    ia = np.zeros((128, 64))
    for i in range(16):
        for h in range(2):
            for x in range(N):
                c, s = cos[x, i], sin[x, i]
                re, im = i * 4 + h * 2, i * 4 + h * 2 + 1
                fx[re, 2 * x : 2 * x + 2] = (c, s)
                fx[im, 2 * x : 2 * x + 2] = (-s, c)
                fo[re, 2 * x : 2 * x + 2] = (-s, c)
                fo[im, 2 * x : 2 * x + 2] = (-c, -s)
                vre, vim = (re, im) if h == 0 else (im, re)
                iv[2 * x, vre], iv[2 * x, vim] = c, -s
                iv[2 * x + 1, vre], iv[2 * x + 1, vim] = s, c
                ia[2 * x, re], ia[2 * x, im] = c, -s
                ia[2 * x + 1, re], ia[2 * x + 1, im] = s, c
    gather = np.zeros((2, 128, 128))
    for i in range(16):
        for h in range(2):
            for q in range(4):
                gather[h, i * 8 + h * 4 + q, (q // 2) * 64 + i * 4 + q % 2] = 1
    pick = np.zeros((6, 32, 128))
    for b in range(16):
        for h in range(2):
            base = b * 8 + h * 4
            pick[h * 3, b * 2, base] = 1
            pick[h * 3, b * 2 + 1, base + 1] = 1
            pick[h * 3 + 1, b * 2, base + 2] = 1
            pick[h * 3 + 1, b * 2 + 1, base + 3] = 1
            pick[h * 3 + 2, b * 2, base + 3] = 1
            pick[h * 3 + 2, b * 2 + 1, base + 2] = -1
    bf = lambda v: jnp.asarray(np.asarray(v, np.float32), BF16)
    return {
        "fx": bf(fx),
        "fo": bf(fo),
        "iv": bf(iv),
        "ia": bf(ia),
        "gather": bf(gather),
        "pick": bf(pick),
    }


def lanes(shape):
    return lax.broadcasted_iota(jnp.int32, shape, 1)


def subl(shape):
    return lax.broadcasted_iota(jnp.int32, shape, 0)


def low_half(shape):
    return (lanes(shape) & 64) == 0


def half_turn(v):
    return pltpu.roll(v, 64, 1)


def pack_spectra(acc, perm, z_ref, out_ref):
    s = mm(acc.astype(BF16), perm)
    low = low_half((32, 128))

    def put(x, u, v):
        z_ref[u, pl.ds(2 * x, S, stride=8), :] = v[:S]
        z_ref[u, pl.ds(2 * x + 1, S, stride=8), :] = v[S:]

    for u in range(L // 2):
        for t in range(2):
            a = s[u * 64 : u * 64 + 32, t * 128 : t * 128 + 128]
            b = s[u * 64 + 32 : u * 64 + 64, t * 128 : t * 128 + 128]
            put(2 * t, u, jnp.where(low, a, half_turn(b)))
            put(2 * t + 1, u, jnp.where(low, half_turn(a), b))
    for u in range(L // 2):
        out_ref[:, u * 128 : u * 128 + 128] = z_ref[u].astype(BF16)


def unpack_back(arrived, perm, z_ref, b_ref, doubled):
    for u in range(L // 2):
        z_ref[u] = arrived[:, u * 128 : u * 128 + 128].astype(F32)
    low = low_half((32, 128))

    def take(x, u):
        parts = [z_ref[u, pl.ds(2 * x + p, S, stride=8), :] for p in range(2)]
        return jnp.concatenate(parts, axis=0)

    for u in range(L // 2):
        for t in range(2):
            a, b = take(2 * t, u), take(2 * t + 1, u)
            first = jnp.where(low, a, half_turn(b))
            second = jnp.where(low, half_turn(a), b)
            if doubled:
                first = first * (1.0 if u == 0 else 2.0)
                second = second * 2.0
            b_ref[u * 64 : u * 64 + 32, t * 128 : t * 128 + 128] = first.astype(BF16)
            b_ref[u * 64 + 32 : u * 64 + 64, t * 128 : t * 128 + 128] = second.astype(BF16)
    return nt(perm, b_ref[...]).astype(BF16)


def halves_of(v):
    hi = v.astype(BF16)
    return hi, (v - hi.astype(F32)).astype(BF16)


def split(v):
    hi, lo = halves_of(v)
    return jnp.where(low_half(v.shape), hi.astype(F32), lo.astype(F32)).astype(BF16)


def spread_weight(w):
    e = (subl((ROWS, C)) // XL == lanes((ROWS, C))).astype(BF16)
    left = mm(e, w)
    full = nt(left.astype(BF16), e)
    same = (subl((ROWS, ROWS)) & 3) == (lanes((ROWS, ROWS)) & 3)
    return jnp.where(same, full, 0.0).astype(BF16)


def onehot(match):
    return jnp.where(match, 1.0, 0.0).astype(BF16)


def lane_order():
    r, k = subl((ROWS, ROWS)), lanes((ROWS, ROWS))
    return onehot(((r >> 2) == (k & 63)) & ((r & 3) == (k >> 6)))


def ext_order(r, k):
    return onehot(((r >> 3) == ((k >> 2) & 15)) & (((r >> 2) & 1) == (k >> 6)) & ((r & 3) == (k & 3)))


SQUARE = (128, 128)

STEPS = 8
AHEAD = 3
CHUNK = CELLS // STEPS
EXACT = functools.partial(
    lax.dot_general, precision=lax.Precision.HIGHEST, preferred_element_type=F32
)
NT = (((1,), (1,)), ((), ()))
NN = (((1,), (0,)), ((), ()))


def at(step):
    if isinstance(step, int):
        return slice(step * CHUNK, step * CHUNK + CHUNK)
    return pl.ds(pl.multiple_of(step * CHUNK, CHUNK), CHUNK)


def planes(src, dst, sems, step):
    return pltpu.make_async_copy(src.at[:, :, at(step)], dst.at[:, :, at(step)], sems.at[step])


def columns(src, dst, sems, step):
    return pltpu.make_async_copy(src.at[:, at(step)], dst.at[:, at(step)], sems.at[step])


def modes_pair(src, dst, sems, u):
    return pltpu.make_async_copy(src.at[:, pl.ds(2 * u, 2)], dst.at[:, pl.ds(2 * u, 2)], sems.at[u])


def start_all(copy, src, dst, sems):
    for n in range(STEPS):
        copy(src, dst, sems, n).start()


def wait_all(copy, src, dst, sems):
    for n in range(STEPS):
        copy(src, dst, sems, n).wait()


def spectra_kernel(
    f_hbm, phase_hbm,
    out_ref, t_hbm,
    f_ref, t_ref, ta_ref, tb_ref, acc_ref, z_ref, phase_ref, f_sem, t_sem, p_sem,
):
    phases = pltpu.make_async_copy(phase_hbm, phase_ref, p_sem.at[0])
    phases.start()
    start_all(planes, f_hbm, f_ref, f_sem)
    acc_ref[...] = jnp.zeros_like(acc_ref)
    perm = lane_order()
    phases.wait()
    cr, sr = phase_ref[64:96, :], phase_ref[96:128, :]

    def make(n, ca, sa, buf_ref, tiles):
        for g in tiles:
            cols = pl.ds(pl.multiple_of(n * CHUNK + g * 128, 128), 128)
            for l in range(L):
                cb, sb = phase_ref[128 + l : 129 + l, :], phase_ref[144 + l : 145 + l, :]
                v = (ca * cb - sa * sb).astype(BF16)
                buf_ref[l * 32 : l * 32 + 32, g * 128 : g * 128 + 128] = v
                t_ref[l * 32 : l * 32 + 32, cols] = v
            ca, sa = ca * cr - sa * sr, sa * cr + ca * sr
        return ca, sa

    def add(n, buf_ref, first):
        acc_ref[first : first + 256, :] += nt(
            buf_ref[first : first + 256, :], f_ref[:, :, at(n)].reshape(ROWS, CHUNK)
        )

    def weave(n, ca, sa, own_ref, next_ref):
        add(n, own_ref, 0)
        ca, sa = make(n + 1, ca, sa, next_ref, (0, 1))
        add(n, own_ref, 256)
        ca, sa = make(n + 1, ca, sa, next_ref, (2, 3))
        columns(t_ref, t_hbm, t_sem, n + 1).start()
        return ca, sa

    ca, sa = make(0, phase_ref[:32, :], phase_ref[32:64, :], ta_ref, range(4))
    columns(t_ref, t_hbm, t_sem, 0).start()

    def step(m, carry):
        n = 2 * m
        planes(f_hbm, f_ref, f_sem, n).wait()
        planes(f_hbm, f_ref, f_sem, n + 1).wait()
        carry = weave(n, *carry, ta_ref, tb_ref)
        return weave(n + 1, *carry, tb_ref, ta_ref)

    ca, sa = lax.fori_loop(0, STEPS // 2 - 1, step, (ca, sa))
    planes(f_hbm, f_ref, f_sem, STEPS - 2).wait()
    planes(f_hbm, f_ref, f_sem, STEPS - 1).wait()
    weave(STEPS - 2, ca, sa, ta_ref, tb_ref)
    add(STEPS - 1, tb_ref, 0)
    add(STEPS - 1, tb_ref, 256)
    pack_spectra(acc_ref[...], perm, z_ref, out_ref)
    wait_all(columns, t_ref, t_hbm, t_sem)


def mix_kernel(r_ref, w_hbm, fx_ref, iv_ref, out_ref, m_ref, w_ref, mask_ref, v_ref, w_sem):
    for n in range(AHEAD):
        modes_pair(w_hbm, w_ref, w_sem, n).start()
    m = mm(fx_ref[...], r_ref[...])
    m_ref[...] = m.astype(BF16)
    shape = m.shape
    own = ((lanes(shape) >> 6) & 1) == ((subl(shape) >> 1) & 1)
    mask_ref[...] = jnp.where(own, m, 0.0)
    row, lane = subl((8, 128)), lanes((8, 128))
    top = row < 4
    even = (row & 1) == 0
    sign = jnp.where(lane < 64, -1.0, 1.0)
    keep = (lane >> 6) == ((row >> 1) & 1)

    def step(u, carry):
        cols = pl.ds(pl.multiple_of(u * 128, 128), 128)
        pair = pl.ds(2 * u, 2)
        modes_pair(w_hbm, w_ref, w_sem, u).wait()

        @pl.when(u < L // 2 - AHEAD)
        def _():
            modes_pair(w_hbm, w_ref, w_sem, u + AHEAD).start()

        for t in range(8):
            left = mask_ref[8 * t : 8 * t + 8, cols].astype(BF16)
            right = jnp.concatenate(
                [w_ref[2 * t, pair].reshape(128, 128), w_ref[2 * t + 1, pair].reshape(128, 128)],
                axis=1,
            )
            o = mm(left, right)
            res = jnp.where(top, o[:, :128], o[:, 128:])
            turned = half_turn(res)
            above = pltpu.roll(turned, 7, 0)
            below = pltpu.roll(turned, 1, 0)
            v = jnp.where(even, res + sign * above, below - sign * res)
            v_ref[8 * t : 8 * t + 8, cols] = jnp.where(keep, v, 0.0)
        return carry

    lax.fori_loop(0, L // 2, step, 0)
    out_ref[...] = mm(iv_ref[...], v_ref[...].astype(BF16)).astype(BF16)


def slope(v):
    a = jnp.abs(v)
    e = jnp.exp(v * v * -0.5)
    t = 1.0 / (1.0 + (0.3275911 / math.sqrt(2.0)) * a)
    poly = t * (
        0.5 * 0.254829592
        + t
        * (
            0.5 * -0.284496736
            + t * (0.5 * 1.421413741 + t * (0.5 * -1.453152027 + t * (0.5 * 1.061405429)))
        )
    )
    tail = e * (poly - a * (1.0 / math.sqrt(2.0 * math.pi)))
    return jnp.where(v < 0, tail, 1.0 - tail)


def delta_kernel(
    r_ref, f_hbm, ct_hbm, t_hbm, w_ref, bias_ref,
    out_ref, d_hbm,
    ct_ref, tf_ref, d_ref, bl_ref, shift_ref, pa_ref, pb_ref, da_ref, db_ref,
    sg_ref, bt_ref, z_ref, f_sem, ct_sem, t_sem, d_sem,
):
    table, flat = tf_ref.at[:Q], tf_ref.at[Q : Q + ROWS]

    def send(n):
        columns(t_hbm, table, t_sem, n).start()
        columns(f_hbm, flat, f_sem, n).start()
        columns(ct_hbm, ct_ref, ct_sem, n).start()

    send(0)
    send(1)
    tf_ref[Q + ROWS :, :] = jnp.ones((16, CELLS), BF16)
    bl_ref[:, :Q] = unpack_back(r_ref[...], lane_order(), z_ref, bt_ref, True)
    bl_ref[:, Q:] = spread_weight(w_ref[...])
    e = (subl((ROWS, C)) // XL == lanes((ROWS, C))).astype(F32)
    shift_ref[...] = EXACT(e, jnp.broadcast_to(bias_ref[...], (128, C)), NT)
    sg_ref[...] = jnp.zeros_like(sg_ref)
    db_ref[...] = jnp.zeros_like(db_ref)

    def arrive(n):
        columns(t_hbm, table, t_sem, n).wait()
        columns(f_hbm, flat, f_sem, n).wait()

    def before(n, p_ref, halves=(0, 1)):
        for h in halves:
            cols = pl.ds(pl.multiple_of(n * CHUNK + h * 256, 256), 256)
            p_ref[:, h * 256 : h * 256 + 256] = mm(bl_ref[...], tf_ref[: Q + ROWS, cols])

    def add(n, own_ref, first, last):
        sg_ref[first:last, :] += nt(tf_ref[first:last, at(n)], own_ref[...])

    def bend(n, p_ref, own_ref, blocks):
        for r in blocks:
            rows = slice(r * 16, r * 16 + 16)
            v = p_ref[rows, :] + jnp.concatenate([shift_ref[rows, :]] * (CHUNK // 128), axis=1)
            d = (ct_ref[rows, at(n)].astype(F32) * slope(v)).astype(BF16)
            own_ref[rows, :] = d
            d_ref[rows, at(n)] = d

    def weave(n, p_ref, next_ref, own_ref, past_ref):
        past, later = jnp.maximum(n - 1, 0), jnp.minimum(n + 1, STEPS - 1)
        add(past, past_ref, 0, 256)
        bend(n, p_ref, own_ref, range(0, 3))
        add(past, past_ref, 256, 512)
        bend(n, p_ref, own_ref, range(3, 6))
        add(past, past_ref, 512, 784)
        bend(n, p_ref, own_ref, range(6, 9))
        before(later, next_ref, (0,))
        bend(n, p_ref, own_ref, range(9, 12))
        before(later, next_ref, (1,))
        bend(n, p_ref, own_ref, range(12, 16))
        columns(d_ref, d_hbm, d_sem, n).start()

    send(2)
    arrive(0)
    before(0, pa_ref)

    def step(m, carry):
        n = 2 * m
        columns(ct_hbm, ct_ref, ct_sem, n).wait()
        columns(ct_hbm, ct_ref, ct_sem, n + 1).wait()
        arrive(n + 1)

        @pl.when(m < STEPS // 2 - 1)
        def _():
            arrive(n + 2)
            send(n + 3)

        @pl.when(m < STEPS // 2 - 2)
        def _():
            send(n + 4)

        weave(n, pa_ref, pb_ref, da_ref, db_ref)
        weave(n + 1, pb_ref, pa_ref, db_ref, da_ref)
        return carry

    lax.fori_loop(0, STEPS // 2, step, 0)
    add(STEPS - 1, db_ref, 0, 784)
    doubled = jnp.where(subl((Q, ROWS)) < 32, 1.0, 2.0)
    pack_spectra(sg_ref[:Q, :] * doubled, lane_order(), z_ref, out_ref)
    same = (subl((ROWS, ROWS)) & 3) == (lanes((ROWS, ROWS)) & 3)
    g = jnp.where(same, sg_ref[Q : Q + ROWS, :], 0.0)
    e = onehot(subl((C, ROWS)) == lanes((C, ROWS)) // XL)
    e2 = onehot((subl((ROWS, 128)) // XL) == (lanes((ROWS, 128)) & 63))
    wg = [nt(e, half) for half in halves_of(g)]
    wg = [mm(half, e2) for half in halves_of(wg[0] + wg[1])]
    sums = jnp.broadcast_to(sg_ref[Q + ROWS : Q + ROWS + 1, :], (128, ROWS))
    bg = [nt(e, half) for half in halves_of(sums)]
    both = jnp.concatenate([wg[0] + wg[1], bg[0] + bg[1]], axis=0)
    out_ref[:, 1024:] = mm(ext_order(subl(SQUARE), lanes(SQUARE)), split(both)).astype(BF16)
    wait_all(columns, d_ref, d_hbm, d_sem)


def total_of(ext):
    shape = (8, 128)
    pick = ((lanes(shape) & 7) == subl(shape)).astype(BF16)
    v = mm(pick, ext)
    return v + half_turn(v)


def spread_total(v):
    return jnp.concatenate([split(v).astype(F32)] * S, axis=0).astype(BF16)


def grad_modes_kernel(r_ref, m_ref, fx_ref, fo_ref, gather_ref, left_ref, dp_ref):
    r = r_ref[:, :1024]
    a = mm(fx_ref[...], r)
    b = mm(fo_ref[...], r)
    row = subl((64, 128))
    first = ((row >> 1) & 1) == 0
    low = low_half((64, 128))
    for u in range(8):
        cols = slice(u * 128, u * 128 + 128)
        au, bu = a[:, cols], b[:, cols]
        left_ref[:, cols] = jnp.where(
            first, jnp.where(low, au, half_turn(bu)), jnp.where(low, half_turn(au), bu)
        ).astype(BF16)
    both = jnp.concatenate([m_ref[...], a.astype(BF16)], axis=0)
    dp_ref[:, :512] = (
        mm(gather_ref[0], both[:, :512]) + mm(gather_ref[1], both[:, 512:])
    ).astype(BF16)
    dp_ref[:, 512:] = spread_total(total_of(r_ref[:, 1024:]))


def adjoint_kernel(left_ref, w_hbm, ia_ref, out_ref, w_ref, v_ref, w_sem):
    for n in range(AHEAD):
        modes_pair(w_hbm, w_ref, w_sem, n).start()
    row, lane = subl((8, 128)), lanes((8, 128))
    top = row < 4
    keep = (lane >> 6) == ((row >> 1) & 1)

    def step(u, carry):
        cols = pl.ds(pl.multiple_of(u * 128, 128), 128)
        pair = pl.ds(2 * u, 2)
        modes_pair(w_hbm, w_ref, w_sem, u).wait()

        @pl.when(u < L // 2 - AHEAD)
        def _():
            modes_pair(w_hbm, w_ref, w_sem, u + AHEAD).start()

        for t in range(8):
            right = jnp.concatenate(
                [w_ref[2 * t, pair].reshape(128, 128), w_ref[2 * t + 1, pair].reshape(128, 128)],
                axis=0,
            )
            o = nt(left_ref[8 * t : 8 * t + 8, cols], right)
            res = jnp.where(top, o[:, :128], o[:, 128:])
            v_ref[8 * t : 8 * t + 8, cols] = jnp.where(keep, res, 0.0)
        return carry

    lax.fori_loop(0, L // 2, step, 0)
    out_ref[...] = mm(ia_ref[...], v_ref[...].astype(BF16)).astype(BF16)


def join_kernel(v_ref, dp_ref, out_ref):
    out_ref[:, :1024] = v_ref[...]
    out_ref[:, 1024:] = spread_total(total_of(dp_ref[:, 512:]))


def weight_grad_kernel(dp_ref, pick_ref, out_ref):
    low = low_half((32, 128))
    data = dp_ref[:, :512]
    for h in range(2):
        m = mm(pick_ref[h * 3], data)
        g1 = mm(pick_ref[h * 3 + 1], data)
        g2 = mm(pick_ref[h * 3 + 2], data)
        for v in range(4):
            cols = slice(v * 128, v * 128 + 128)
            a, b = g1[:, cols], g2[:, cols]
            right = jnp.concatenate(
                [jnp.where(low, a, half_turn(b)), jnp.where(low, half_turn(a), b)], axis=1
            )
            o = tn(m[:, cols].astype(BF16), right.astype(BF16)) * 0.25
            l = h * 8 + v * 2
            out_ref[l] = o[:64, :128]
            out_ref[l + 1] = o[64:, 128:]


def input_grad_kernel(
    r_ref, d_hbm, t_hbm, w_ref,
    out_hbm, pg_hbm, bg_hbm,
    td_ref, o_ref, bl_ref, bt_ref, z_ref, pg_ref, bg_ref, d_sem, t_sem, o_sem, g_sem,
):
    table, delta = td_ref.at[:Q], td_ref.at[Q:]

    def send(p):
        for n in (2 * p, 2 * p + 1):
            columns(t_hbm, table, t_sem, n).start()
            columns(d_hbm, delta, d_sem, n).start()

    send(0)
    bl_ref[:, :Q] = unpack_back(r_ref[:, :1024], lane_order(), z_ref, bt_ref, False)
    bl_ref[:, Q:] = spread_weight(w_ref[...]).astype(F32).T.astype(BF16)
    v = mm(ext_order(lanes(SQUARE), subl(SQUARE)), r_ref[:, 1024:])
    v = (v + half_turn(v)) * (1.0 / 2048.0)
    pg_ref[...] = v[:C, :C]
    diag = subl((C, C)) == lanes((C, C))
    bg_ref[...] = jnp.sum(jnp.where(diag, v[C:, :C], 0.0), axis=0, keepdims=True)
    small = [
        pltpu.make_async_copy(pg_ref, pg_hbm, g_sem.at[0]),
        pltpu.make_async_copy(bg_ref, bg_hbm, g_sem.at[1]),
    ]
    for copy in small:
        copy.start()
    send(1)
    for p in range(STEPS // 2):
        for n in (2 * p, 2 * p + 1):
            columns(t_hbm, table, t_sem, n).wait()
            columns(d_hbm, delta, d_sem, n).wait()
        if p + 2 < STEPS // 2:
            send(p + 2)
        for n in (2 * p, 2 * p + 1):
            out = mm(bl_ref[...], td_ref[:, at(n)])
            o_ref[:, :, at(n)] = out.astype(BF16).reshape(C, XL, CHUNK)
        for n in (2 * p, 2 * p + 1):
            planes(o_ref, out_hbm, o_sem, n).start()
    wait_all(planes, o_ref, out_hbm, o_sem)
    for copy in small:
        copy.wait()


def call(kernel, name, outs, scratch, args, big=(), big_outs=(), sems=0):
    place = lambda n, far: pl.BlockSpec(memory_space=pltpu.HBM if n in far else pltpu.VMEM)
    return pl.pallas_call(
        kernel,
        in_specs=[place(n, big) for n in range(len(args))],
        out_specs=[place(n, big_outs) for n in range(len(outs))],
        out_shape=[
            (pltpu.HBM if n in big_outs else pltpu.VMEM)(shape, dtype)
            for n, (shape, dtype) in enumerate(outs)
        ],
        scratch_shapes=[pltpu.VMEM(shape, dtype) for shape, dtype in scratch]
        + [pltpu.SemaphoreType.DMA((STEPS,))] * sems,
        compiler_params=pltpu.CompilerParams(vmem_limit_bytes=40 << 20),
        name=name,
    )(
        *[
            pltpu.with_memory_space_constraint(a, pltpu.HBM if n in big else pltpu.VMEM)
            for n, a in enumerate(args)
        ]
    )


def exchange(v, axis):
    width = v.shape[1]
    out = lax.all_to_all(v.reshape(S, 8, width), axis, split_axis=0, concat_axis=0, tiled=True)
    return out.reshape(128, width)


def body(field, cotangent, spectral_weight, point_weight, bias):
    k = constants()
    field3 = field.reshape(C, XL, CELLS)
    flat = field.reshape(ROWS, CELLS)
    cot2 = cotangent.reshape(ROWS, CELLS)
    planes_shape = ((C, XL, CELLS), BF16)
    cells_shape = ((ROWS, CELLS), BF16)
    weight_shape = (spectral_weight.shape, BF16)

    spectra, table = call(
        spectra_kernel,
        "spectra",
        [((128, 1024), BF16), ((Q, CELLS), BF16)],
        [planes_shape, ((Q, CELLS), BF16), ((Q, CHUNK), BF16), ((Q, CHUNK), BF16), ((Q, ROWS), F32), ((L // 2, 128, 128), F32),
         ((160, 128), F32)],
        [field3, jnp.asarray(phase_tables())],
        big=(0, 1), big_outs=(1,), sems=3,
    )
    arrived, flat = lax.optimization_barrier((exchange(spectra, "slab"), flat))
    back, modes = call(
        mix_kernel,
        "mix",
        [((128, 1024), BF16), ((64, 1024), BF16)],
        [weight_shape, ((64, 1024), F32), ((64, 1024), F32)],
        [arrived, spectral_weight, k["fx"], k["iv"]],
        big=(1,), sems=1,
    )
    arrived = exchange(back, "slab")
    grad_spectra, delta = call(
        delta_kernel,
        "delta",
        [((128, 1152), BF16), cells_shape],
        [
            cells_shape, ((Q + ROWS + 16, CELLS), BF16), cells_shape,
            ((ROWS, Q + ROWS), BF16), ((ROWS, 128), F32),
            ((ROWS, CHUNK), F32), ((ROWS, CHUNK), F32), ((ROWS, CHUNK), BF16), ((ROWS, CHUNK), BF16),
            ((Q + ROWS + 16, ROWS), F32), ((Q, ROWS), BF16), ((L // 2, 128, 128), F32),
        ],
        [arrived, flat, cot2, table, point_weight, bias.reshape(1, C)],
        big=(1, 2, 3), big_outs=(1,), sems=4,
    )
    arrived = exchange(grad_spectra, "slab")
    left, shared = call(
        grad_modes_kernel,
        "grad_modes",
        [((64, 1024), BF16), ((128, 640), BF16)],
        [],
        [arrived, modes, k["fx"], k["fo"], k["gather"]],
    )
    shared = exchange(shared, "dp")
    (adjoint,) = call(
        adjoint_kernel,
        "adjoint",
        [((128, 1024), BF16)],
        [weight_shape, ((64, 1024), F32)],
        [left, spectral_weight, k["ia"]],
        big=(1,), sems=1,
    )
    (joined,) = call(join_kernel, "join", [((128, 1152), BF16)], [], [adjoint, shared])
    arrived = exchange(joined, "slab")
    (spectral_grad,) = call(
        weight_grad_kernel, "weight_grad", [((L, C, 128), F32)], [], [shared, k["pick"]]
    )
    input_grad, point_grad, bias_grad = call(
        input_grad_kernel,
        "input_grad",
        [planes_shape, ((C, C), F32), ((1, C), F32)],
        [((Q + ROWS, CELLS), BF16), planes_shape, ((ROWS, Q + ROWS), BF16), ((Q, ROWS), BF16),
         ((L // 2, 128, 128), F32), ((C, C), F32), ((1, C), F32)],
        [arrived, delta, table, point_weight],
        big=(1, 2), big_outs=(0, 1, 2), sems=4,
    )
    return (
        input_grad.reshape(field.shape),
        spectral_grad[None],
        point_grad,
        bias_grad.reshape(C),
    )


def solution(mesh):
    return jax.shard_map(
        body,
        mesh=mesh,
        in_specs=(
            P("dp", None, "slab", None),
            P("dp", None, "slab", None),
            P(None, "slab", None, None),
            P(),
            P(),
        ),
        out_specs=(P("dp", None, "slab", None), P("dp", "slab", None, None), P(), P()),
        check_vma=False,
    )
```

```python
import functools
import math

import jax
import jax.numpy as jnp
import numpy as np
from jax import lax
from jax.experimental import pallas as pl
from jax.experimental.pallas import tpu as pltpu
from jax.sharding import PartitionSpec as P

C = 64
N = 64
XL = 4
S = 16
L = 16
CELLS = 4096
ROWS = C * XL
Q = 512
F32 = jnp.float32
BF16 = jnp.bfloat16


def mm(a, b):
    return jnp.dot(a, b, preferred_element_type=F32)


def nt(a, b):
    return lax.dot_general(a, b, (((1,), (1,)), ((), ())), preferred_element_type=F32)


def tn(a, b):
    return lax.dot_general(a, b, (((0,), (0,)), ((), ())), preferred_element_type=F32)


def waves(count, size):
    return np.array([i if i < count // 2 else size - count + i for i in range(count)])


def phase_tables():
    f = np.float32
    k = np.tile(waves(S, N), 2)[:, None]
    part = np.repeat([0.0, np.pi / 2], S)[:, None]
    unit = 2.0 * np.pi / N
    ang = unit * (k * (np.arange(128) // N)[None, :]) + part
    turn = unit * np.broadcast_to(2 * k, (2 * S, 128))
    angz = unit * ((np.arange(L)[:, None] * (np.arange(128) % N)[None, :]) % N)
    pair = lambda a, scale: np.concatenate([np.cos(a), np.sin(a)]) * scale
    return np.concatenate([pair(ang, 1.0 / N), pair(turn, 1.0), pair(angz, 1.0)]).astype(f)


def x_tables():
    ang = 2.0 * np.pi * ((np.arange(N)[:, None] * waves(16, N)[None, :]) % N) / N
    return np.cos(ang) / 8.0, np.sin(ang) / 8.0


def constants():
    cos, sin = x_tables()
    fx = np.zeros((64, 128))
    fo = np.zeros((64, 128))
    iv = np.zeros((128, 64))
    ia = np.zeros((128, 64))
    for i in range(16):
        for h in range(2):
            for x in range(N):
                c, s = cos[x, i], sin[x, i]
                re, im = i * 4 + h * 2, i * 4 + h * 2 + 1
                fx[re, 2 * x : 2 * x + 2] = (c, s)
                fx[im, 2 * x : 2 * x + 2] = (-s, c)
                fo[re, 2 * x : 2 * x + 2] = (-s, c)
                fo[im, 2 * x : 2 * x + 2] = (-c, -s)
                vre, vim = (re, im) if h == 0 else (im, re)
                iv[2 * x, vre], iv[2 * x, vim] = c, -s
                iv[2 * x + 1, vre], iv[2 * x + 1, vim] = s, c
                ia[2 * x, re], ia[2 * x, im] = c, -s
                ia[2 * x + 1, re], ia[2 * x + 1, im] = s, c
    gather = np.zeros((2, 128, 128))
    for i in range(16):
        for h in range(2):
            for q in range(4):
                gather[h, i * 8 + h * 4 + q, (q // 2) * 64 + i * 4 + q % 2] = 1
    pick = np.zeros((6, 32, 128))
    for b in range(16):
        for h in range(2):
            base = b * 8 + h * 4
            pick[h * 3, b * 2, base] = 1
            pick[h * 3, b * 2 + 1, base + 1] = 1
            pick[h * 3 + 1, b * 2, base + 2] = 1
            pick[h * 3 + 1, b * 2 + 1, base + 3] = 1
            pick[h * 3 + 2, b * 2, base + 3] = 1
            pick[h * 3 + 2, b * 2 + 1, base + 2] = -1
    bf = lambda v: jnp.asarray(np.asarray(v, np.float32), BF16)
    return {
        "fx": bf(fx),
        "fo": bf(fo),
        "iv": bf(iv),
        "ia": bf(ia),
        "gather": bf(gather),
        "pick": bf(pick),
    }


def lanes(shape):
    return lax.broadcasted_iota(jnp.int32, shape, 1)


def subl(shape):
    return lax.broadcasted_iota(jnp.int32, shape, 0)


def low_half(shape):
    return (lanes(shape) & 64) == 0


def half_turn(v):
    return pltpu.roll(v, 64, 1)


def pack_spectra(acc, perm, z_ref, out_ref):
    s = mm(acc.astype(BF16), perm)
    low = low_half((32, 128))

    def put(x, u, v):
        z_ref[u, pl.ds(2 * x, S, stride=8), :] = v[:S]
        z_ref[u, pl.ds(2 * x + 1, S, stride=8), :] = v[S:]

    for u in range(L // 2):
        for t in range(2):
            a = s[u * 64 : u * 64 + 32, t * 128 : t * 128 + 128]
            b = s[u * 64 + 32 : u * 64 + 64, t * 128 : t * 128 + 128]
            put(2 * t, u, jnp.where(low, a, half_turn(b)))
            put(2 * t + 1, u, jnp.where(low, half_turn(a), b))
    for u in range(L // 2):
        out_ref[:, u * 128 : u * 128 + 128] = z_ref[u].astype(BF16)


def unpack_back(arrived, perm, z_ref, b_ref, doubled):
    for u in range(L // 2):
        z_ref[u] = arrived[:, u * 128 : u * 128 + 128].astype(F32)
    low = low_half((32, 128))

    def take(x, u):
        parts = [z_ref[u, pl.ds(2 * x + p, S, stride=8), :] for p in range(2)]
        return jnp.concatenate(parts, axis=0)

    for u in range(L // 2):
        for t in range(2):
            a, b = take(2 * t, u), take(2 * t + 1, u)
            first = jnp.where(low, a, half_turn(b))
            second = jnp.where(low, half_turn(a), b)
            if doubled:
                first = first * (1.0 if u == 0 else 2.0)
                second = second * 2.0
            b_ref[u * 64 : u * 64 + 32, t * 128 : t * 128 + 128] = first.astype(BF16)
            b_ref[u * 64 + 32 : u * 64 + 64, t * 128 : t * 128 + 128] = second.astype(BF16)
    return nt(perm, b_ref[...]).astype(BF16)


def halves_of(v):
    hi = v.astype(BF16)
    return hi, (v - hi.astype(F32)).astype(BF16)


def split(v):
    hi, lo = halves_of(v)
    return jnp.where(low_half(v.shape), hi.astype(F32), lo.astype(F32)).astype(BF16)


def spread_weight(w):
    e = (subl((ROWS, C)) // XL == lanes((ROWS, C))).astype(BF16)
    left = mm(e, w)
    full = nt(left.astype(BF16), e)
    same = (subl((ROWS, ROWS)) & 3) == (lanes((ROWS, ROWS)) & 3)
    return jnp.where(same, full, 0.0).astype(BF16)


def onehot(match):
    return jnp.where(match, 1.0, 0.0).astype(BF16)


def lane_order():
    r, k = subl((ROWS, ROWS)), lanes((ROWS, ROWS))
    return onehot(((r >> 2) == (k & 63)) & ((r & 3) == (k >> 6)))


def ext_order(r, k):
    return onehot(((r >> 3) == ((k >> 2) & 15)) & (((r >> 2) & 1) == (k >> 6)) & ((r & 3) == (k & 3)))


SQUARE = (128, 128)

STEPS = 8
CHUNK = CELLS // STEPS
EXACT = functools.partial(
    lax.dot_general, precision=lax.Precision.HIGHEST, preferred_element_type=F32
)
NT = (((1,), (1,)), ((), ()))
NN = (((1,), (0,)), ((), ()))


def at(step):
    if isinstance(step, int):
        return slice(step * CHUNK, step * CHUNK + CHUNK)
    return pl.ds(pl.multiple_of(step * CHUNK, CHUNK), CHUNK)


def planes(src, dst, sems, step):
    return pltpu.make_async_copy(src.at[:, :, at(step)], dst.at[:, :, at(step)], sems.at[step])


def columns(src, dst, sems, step):
    return pltpu.make_async_copy(src.at[:, at(step)], dst.at[:, at(step)], sems.at[step])


def modes_pair(src, dst, sems, u):
    return pltpu.make_async_copy(src.at[:, pl.ds(2 * u, 2)], dst.at[:, pl.ds(2 * u, 2)], sems.at[u])


def start_all(copy, src, dst, sems):
    for n in range(STEPS):
        copy(src, dst, sems, n).start()


def wait_all(copy, src, dst, sems):
    for n in range(STEPS):
        copy(src, dst, sems, n).wait()


def make_table(phase_ref, ca, sa, refs, tiles):
    cr, sr = phase_ref[64:96, :], phase_ref[96:128, :]
    for g in tiles:
        for l in range(L):
            cb, sb = phase_ref[128 + l : 129 + l, :], phase_ref[144 + l : 145 + l, :]
            v = (ca * cb - sa * sb).astype(BF16)
            for ref, start in refs:
                ref[l * 32 : l * 32 + 32, pl.ds(start + g * 128, 128)] = v
        ca, sa = ca * cr - sa * sr, sa * cr + ca * sr
    return ca, sa


def spectra_kernel(
    f_hbm, phase_hbm,
    out_ref, tf_ref,
    f_ref, ta_ref, tb_ref, acc_ref, z_ref, phase_ref, f_sem, p_sem,
):
    phases = pltpu.make_async_copy(phase_hbm, phase_ref, p_sem.at[0])
    phases.start()
    start_all(planes, f_hbm, f_ref, f_sem)
    acc_ref[...] = jnp.zeros_like(acc_ref)
    tf_ref[Q + ROWS :, :] = jnp.ones((16, CELLS), BF16)
    perm = lane_order()
    phases.wait()

    def make(n, ca, sa, buf_ref):
        start = n * CHUNK if isinstance(n, int) else pl.multiple_of(n * CHUNK, CHUNK)
        return make_table(phase_ref, ca, sa, ((buf_ref, 0), (tf_ref, start)), range(4))

    def add(n, buf_ref):
        flat = f_ref[:, :, at(n)].reshape(ROWS, CHUNK)
        tf_ref[Q : Q + ROWS, at(n)] = flat
        acc_ref[...] += nt(buf_ref[...], flat)

    ca, sa = make(0, phase_ref[:32, :], phase_ref[32:64, :], ta_ref)

    def step(m, carry):
        n = 2 * m
        planes(f_hbm, f_ref, f_sem, n).wait()
        planes(f_hbm, f_ref, f_sem, n + 1).wait()
        add(n, ta_ref)
        carry = make(n + 1, *carry, tb_ref)
        add(n + 1, tb_ref)
        return make(n + 2, *carry, ta_ref)

    ca, sa = lax.fori_loop(0, STEPS // 2 - 1, step, (ca, sa))
    planes(f_hbm, f_ref, f_sem, STEPS - 2).wait()
    planes(f_hbm, f_ref, f_sem, STEPS - 1).wait()
    add(STEPS - 2, ta_ref)
    make(STEPS - 1, ca, sa, tb_ref)
    add(STEPS - 1, tb_ref)
    pack_spectra(acc_ref[...], perm, z_ref, out_ref)


def mix_kernel(r_ref, w_hbm, fx_ref, iv_ref, out_ref, m_ref, w_ref, mask_ref, v_ref, w_sem):
    start_all(modes_pair, w_hbm, w_ref, w_sem)
    m = mm(fx_ref[...], r_ref[...])
    m_ref[...] = m.astype(BF16)
    shape = m.shape
    own = ((lanes(shape) >> 6) & 1) == ((subl(shape) >> 1) & 1)
    mask_ref[...] = jnp.where(own, m, 0.0)
    row, lane = subl((8, 128)), lanes((8, 128))
    top = row < 4
    even = (row & 1) == 0
    sign = jnp.where(lane < 64, -1.0, 1.0)
    keep = (lane >> 6) == ((row >> 1) & 1)

    def step(u, carry):
        cols = pl.ds(pl.multiple_of(u * 128, 128), 128)
        pair = pl.ds(2 * u, 2)
        modes_pair(w_hbm, w_ref, w_sem, u).wait()
        for t in range(8):
            left = mask_ref[8 * t : 8 * t + 8, cols].astype(BF16)
            right = jnp.concatenate(
                [w_ref[2 * t, pair].reshape(128, 128), w_ref[2 * t + 1, pair].reshape(128, 128)],
                axis=1,
            )
            o = mm(left, right)
            res = jnp.where(top, o[:, :128], o[:, 128:])
            turned = half_turn(res)
            above = pltpu.roll(turned, 7, 0)
            below = pltpu.roll(turned, 1, 0)
            v = jnp.where(even, res + sign * above, below - sign * res)
            v_ref[8 * t : 8 * t + 8, cols] = jnp.where(keep, v, 0.0)
        return carry

    lax.fori_loop(0, L // 2, step, 0)
    out_ref[...] = mm(iv_ref[...], v_ref[...].astype(BF16)).astype(BF16)


def slope(v):
    a = jnp.abs(v)
    e = jnp.exp(v * v * -0.5)
    t = 1.0 / (1.0 + (0.3275911 / math.sqrt(2.0)) * a)
    poly = t * (
        0.5 * 0.254829592
        + t
        * (
            0.5 * -0.284496736
            + t * (0.5 * 1.421413741 + t * (0.5 * -1.453152027 + t * (0.5 * 1.061405429)))
        )
    )
    tail = e * (poly - a * (1.0 / math.sqrt(2.0 * math.pi)))
    return jnp.where(v < 0, tail, 1.0 - tail)


def delta_kernel(
    r_ref, tf_ref, ct_hbm, w_ref, bias_ref,
    out_ref, d_hbm,
    ct_ref, d_ref, bl_ref, shift_ref, pa_ref, pb_ref, da_ref, db_ref,
    sg_ref, bt_ref, z_ref, ct_sem, d_sem,
):
    start_all(planes, ct_hbm, ct_ref, ct_sem)
    bl_ref[:, :Q] = unpack_back(r_ref[...], lane_order(), z_ref, bt_ref, True)
    bl_ref[:, Q:] = spread_weight(w_ref[...])
    e = (subl((ROWS, C)) // XL == lanes((ROWS, C))).astype(F32)
    shift_ref[...] = EXACT(e, jnp.broadcast_to(bias_ref[...], (128, C)), NT)
    sg_ref[...] = jnp.zeros_like(sg_ref)
    db_ref[...] = jnp.zeros_like(db_ref)

    def before(n, p_ref, halves=(0, 1)):
        for h in halves:
            cols = pl.ds(pl.multiple_of(n * CHUNK + h * 256, 256), 256)
            p_ref[:, h * 256 : h * 256 + 256] = mm(bl_ref[...], tf_ref[: Q + ROWS, cols])

    def add(n, own_ref, first, last):
        sg_ref[first:last, :] += nt(tf_ref[first:last, at(n)], own_ref[...])

    def bend(n, p_ref, own_ref, blocks):
        for r in blocks:
            rows = slice(r * 16, r * 16 + 16)
            v = p_ref[rows, :] + jnp.concatenate([shift_ref[rows, :]] * (CHUNK // 128), axis=1)
            ct = ct_ref[r * 4 : r * 4 + 4, :, at(n)].reshape(16, CHUNK)
            d = (ct.astype(F32) * slope(v)).astype(BF16)
            own_ref[rows, :] = d
            d_ref[rows, at(n)] = d

    def weave(n, p_ref, next_ref, own_ref, past_ref):
        past, later = jnp.maximum(n - 1, 0), jnp.minimum(n + 1, STEPS - 1)
        add(past, past_ref, 0, 256)
        bend(n, p_ref, own_ref, range(0, 3))
        add(past, past_ref, 256, 512)
        bend(n, p_ref, own_ref, range(3, 6))
        add(past, past_ref, 512, 784)
        bend(n, p_ref, own_ref, range(6, 9))
        before(later, next_ref, (0,))
        bend(n, p_ref, own_ref, range(9, 12))
        before(later, next_ref, (1,))
        bend(n, p_ref, own_ref, range(12, 16))
        columns(d_ref, d_hbm, d_sem, n).start()

    before(0, pa_ref)

    def step(m, carry):
        n = 2 * m
        planes(ct_hbm, ct_ref, ct_sem, n).wait()
        planes(ct_hbm, ct_ref, ct_sem, n + 1).wait()
        weave(n, pa_ref, pb_ref, da_ref, db_ref)
        weave(n + 1, pb_ref, pa_ref, db_ref, da_ref)
        return carry

    lax.fori_loop(0, STEPS // 2, step, 0)
    add(STEPS - 1, db_ref, 0, 784)
    doubled = jnp.where(subl((Q, ROWS)) < 32, 1.0, 2.0)
    pack_spectra(sg_ref[:Q, :] * doubled, lane_order(), z_ref, out_ref)
    same = (subl((ROWS, ROWS)) & 3) == (lanes((ROWS, ROWS)) & 3)
    g = jnp.where(same, sg_ref[Q : Q + ROWS, :], 0.0)
    e = onehot(subl((C, ROWS)) == lanes((C, ROWS)) // XL)
    e2 = onehot((subl((ROWS, 128)) // XL) == (lanes((ROWS, 128)) & 63))
    wg = [nt(e, half) for half in halves_of(g)]
    wg = [mm(half, e2) for half in halves_of(wg[0] + wg[1])]
    sums = jnp.broadcast_to(sg_ref[Q + ROWS : Q + ROWS + 1, :], (128, ROWS))
    bg = [nt(e, half) for half in halves_of(sums)]
    both = jnp.concatenate([wg[0] + wg[1], bg[0] + bg[1]], axis=0)
    out_ref[:, 1024:] = mm(ext_order(subl(SQUARE), lanes(SQUARE)), split(both)).astype(BF16)
    wait_all(columns, d_ref, d_hbm, d_sem)


def total_of(ext):
    shape = (8, 128)
    pick = ((lanes(shape) & 7) == subl(shape)).astype(BF16)
    v = mm(pick, ext)
    return v + half_turn(v)


def spread_total(v):
    return jnp.concatenate([split(v).astype(F32)] * S, axis=0).astype(BF16)


def grad_modes_kernel(r_ref, m_ref, fx_ref, fo_ref, gather_ref, left_ref, dp_ref):
    r = r_ref[:, :1024]
    a = mm(fx_ref[...], r)
    b = mm(fo_ref[...], r)
    row = subl((64, 128))
    first = ((row >> 1) & 1) == 0
    low = low_half((64, 128))
    for u in range(8):
        cols = slice(u * 128, u * 128 + 128)
        au, bu = a[:, cols], b[:, cols]
        left_ref[:, cols] = jnp.where(
            first, jnp.where(low, au, half_turn(bu)), jnp.where(low, half_turn(au), bu)
        ).astype(BF16)
    both = jnp.concatenate([m_ref[...], a.astype(BF16)], axis=0)
    dp_ref[:, :512] = (
        mm(gather_ref[0], both[:, :512]) + mm(gather_ref[1], both[:, 512:])
    ).astype(BF16)
    dp_ref[:, 512:] = spread_total(total_of(r_ref[:, 1024:]))


def adjoint_kernel(left_ref, w_hbm, ia_ref, out_ref, w_ref, v_ref, w_sem):
    start_all(modes_pair, w_hbm, w_ref, w_sem)
    row, lane = subl((8, 128)), lanes((8, 128))
    top = row < 4
    keep = (lane >> 6) == ((row >> 1) & 1)

    def step(u, carry):
        cols = pl.ds(pl.multiple_of(u * 128, 128), 128)
        pair = pl.ds(2 * u, 2)
        modes_pair(w_hbm, w_ref, w_sem, u).wait()
        for t in range(8):
            right = jnp.concatenate(
                [w_ref[2 * t, pair].reshape(128, 128), w_ref[2 * t + 1, pair].reshape(128, 128)],
                axis=0,
            )
            o = nt(left_ref[8 * t : 8 * t + 8, cols], right)
            res = jnp.where(top, o[:, :128], o[:, 128:])
            v_ref[8 * t : 8 * t + 8, cols] = jnp.where(keep, res, 0.0)
        return carry

    lax.fori_loop(0, L // 2, step, 0)
    out_ref[...] = mm(ia_ref[...], v_ref[...].astype(BF16)).astype(BF16)


def join_kernel(v_ref, dp_ref, out_ref):
    out_ref[:, :1024] = v_ref[...]
    out_ref[:, 1024:] = spread_total(total_of(dp_ref[:, 512:]))


def weight_grad_kernel(dp_ref, pick_ref, out_ref):
    low = low_half((32, 128))
    data = dp_ref[:, :512]
    for h in range(2):
        m = mm(pick_ref[h * 3], data)
        g1 = mm(pick_ref[h * 3 + 1], data)
        g2 = mm(pick_ref[h * 3 + 2], data)
        for v in range(4):
            cols = slice(v * 128, v * 128 + 128)
            a, b = g1[:, cols], g2[:, cols]
            right = jnp.concatenate(
                [jnp.where(low, a, half_turn(b)), jnp.where(low, half_turn(a), b)], axis=1
            )
            o = tn(m[:, cols].astype(BF16), right.astype(BF16)) * 0.25
            l = h * 8 + v * 2
            out_ref[l] = o[:64, :128]
            out_ref[l + 1] = o[64:, 128:]


def input_grad_kernel(
    r_ref, d_hbm, w_ref, phase_ref,
    out_hbm, pg_hbm, bg_hbm,
    d_ref, ta_ref, tb_ref, o_ref, bl_ref, bt_ref, z_ref, pg_ref, bg_ref, d_sem, o_sem, g_sem,
):
    start_all(columns, d_hbm, d_ref, d_sem)
    bl_ref[:, :Q] = unpack_back(r_ref[:, :1024], lane_order(), z_ref, bt_ref, False)
    bl_ref[:, Q:] = spread_weight(w_ref[...]).astype(F32).T.astype(BF16)
    v = mm(ext_order(lanes(SQUARE), subl(SQUARE)), r_ref[:, 1024:])
    v = (v + half_turn(v)) * (1.0 / 2048.0)
    pg_ref[...] = v[:C, :C]
    diag = subl((C, C)) == lanes((C, C))
    bg_ref[...] = jnp.sum(jnp.where(diag, v[C:, :C], 0.0), axis=0, keepdims=True)
    small = [
        pltpu.make_async_copy(pg_ref, pg_hbm, g_sem.at[0]),
        pltpu.make_async_copy(bg_ref, bg_hbm, g_sem.at[1]),
    ]
    for copy in small:
        copy.start()

    def finish(n, own_ref):
        out = mm(bl_ref[:, :Q], own_ref[...]) + mm(bl_ref[:, Q:], d_ref[:, at(n)])
        o_ref[:, :, at(n)] = out.astype(BF16).reshape(C, XL, CHUNK)

    def make(carry, next_ref):
        return make_table(phase_ref, *carry, ((next_ref, 0),), range(4))

    def step(m, carry):
        n = 2 * m
        columns(d_hbm, d_ref, d_sem, n).wait()
        columns(d_hbm, d_ref, d_sem, n + 1).wait()
        finish(n, ta_ref)
        carry = make(carry, tb_ref)
        finish(n + 1, tb_ref)
        carry = make(carry, ta_ref)
        planes(o_ref, out_hbm, o_sem, n).start()
        planes(o_ref, out_hbm, o_sem, n + 1).start()
        return carry

    carry = make((phase_ref[:32, :], phase_ref[32:64, :]), ta_ref)
    carry = lax.fori_loop(0, STEPS // 2 - 1, step, carry)
    columns(d_hbm, d_ref, d_sem, STEPS - 2).wait()
    columns(d_hbm, d_ref, d_sem, STEPS - 1).wait()
    finish(STEPS - 2, ta_ref)
    planes(o_ref, out_hbm, o_sem, STEPS - 2).start()
    make(carry, tb_ref)
    finish(STEPS - 1, tb_ref)
    planes(o_ref, out_hbm, o_sem, STEPS - 1).start()
    wait_all(planes, o_ref, out_hbm, o_sem)
    for copy in small:
        copy.wait()


def call(kernel, name, outs, scratch, args, big=(), big_outs=(), sems=0, room=8):
    place = lambda n, far: pl.BlockSpec(memory_space=pltpu.HBM if n in far else pltpu.VMEM)
    return pl.pallas_call(
        kernel,
        in_specs=[place(n, big) for n in range(len(args))],
        out_specs=[place(n, big_outs) for n in range(len(outs))],
        out_shape=[
            (pltpu.HBM if n in big_outs else pltpu.VMEM)(shape, dtype)
            for n, (shape, dtype) in enumerate(outs)
        ],
        scratch_shapes=[pltpu.VMEM(shape, dtype) for shape, dtype in scratch]
        + [pltpu.SemaphoreType.DMA((STEPS,))] * sems,
        compiler_params=pltpu.CompilerParams(vmem_limit_bytes=room << 20),
        name=name,
    )(
        *[
            pltpu.with_memory_space_constraint(a, pltpu.HBM if n in big else pltpu.VMEM)
            for n, a in enumerate(args)
        ]
    )


def exchange(v, axis):
    width = v.shape[1]
    out = lax.all_to_all(v.reshape(S, 8, width), axis, split_axis=0, concat_axis=0, tiled=True)
    return out.reshape(128, width)


def body(field, cotangent, spectral_weight, point_weight, bias):
    k = constants()
    field3 = field.reshape(C, XL, CELLS)
    cot3 = cotangent.reshape(C, XL, CELLS)
    planes_shape = ((C, XL, CELLS), BF16)
    cells_shape = ((ROWS, CELLS), BF16)
    weight_shape = (spectral_weight.shape, BF16)

    phases = jnp.asarray(phase_tables())
    spectra, rows = call(
        spectra_kernel,
        "spectra",
        [((128, 1024), BF16), ((Q + ROWS + 16, CELLS), BF16)],
        [planes_shape, ((Q, CHUNK), BF16), ((Q, CHUNK), BF16), ((Q, ROWS), F32),
         ((L // 2, 128, 128), F32), ((160, 128), F32)],
        [field3, phases],
        big=(0, 1), sems=2,
    )
    arrived = exchange(spectra, "slab")
    back, modes = call(
        mix_kernel,
        "mix",
        [((128, 1024), BF16), ((64, 1024), BF16)],
        [weight_shape, ((64, 1024), F32), ((64, 1024), F32)],
        [arrived, spectral_weight, k["fx"], k["iv"]],
        big=(1,), sems=1,
    )
    arrived = exchange(back, "slab")
    grad_spectra, delta = call(
        delta_kernel,
        "delta",
        [((128, 1152), BF16), cells_shape],
        [
            planes_shape, cells_shape,
            ((ROWS, Q + ROWS), BF16), ((ROWS, 128), F32),
            ((ROWS, CHUNK), F32), ((ROWS, CHUNK), F32), ((ROWS, CHUNK), BF16), ((ROWS, CHUNK), BF16),
            ((Q + ROWS + 16, ROWS), F32), ((Q, ROWS), BF16), ((L // 2, 128, 128), F32),
        ],
        [arrived, rows, cot3, point_weight, bias.reshape(1, C)],
        big=(2,), big_outs=(1,), sems=2, room=16,
    )
    arrived = exchange(grad_spectra, "slab")
    left, shared = call(
        grad_modes_kernel,
        "grad_modes",
        [((64, 1024), BF16), ((128, 640), BF16)],
        [],
        [arrived, modes, k["fx"], k["fo"], k["gather"]],
    )
    shared = exchange(shared, "dp")
    (adjoint,) = call(
        adjoint_kernel,
        "adjoint",
        [((128, 1024), BF16)],
        [weight_shape, ((64, 1024), F32)],
        [left, spectral_weight, k["ia"]],
        big=(1,), sems=1,
    )
    (joined,) = call(join_kernel, "join", [((128, 1152), BF16)], [], [adjoint, shared])
    arrived = exchange(joined, "slab")
    (spectral_grad,) = call(
        weight_grad_kernel, "weight_grad", [((L, C, 128), F32)], [], [shared, k["pick"]]
    )
    input_grad, point_grad, bias_grad = call(
        input_grad_kernel,
        "input_grad",
        [planes_shape, ((C, C), F32), ((1, C), F32)],
        [cells_shape, ((Q, CHUNK), BF16), ((Q, CHUNK), BF16), planes_shape,
         ((ROWS, Q + ROWS), BF16), ((Q, ROWS), BF16), ((L // 2, 128, 128), F32), ((C, C), F32),
         ((1, C), F32)],
        [arrived, delta, point_weight, phases],
        big=(1,), big_outs=(0, 1, 2), sems=3, room=16,
    )
    return (
        input_grad.reshape(field.shape),
        spectral_grad[None],
        point_grad,
        bias_grad.reshape(C),
    )


def solution(mesh):
    return jax.shard_map(
        body,
        mesh=mesh,
        in_specs=(
            P("dp", None, "slab", None),
            P("dp", None, "slab", None),
            P(None, "slab", None, None),
            P(),
            P(),
        ),
        out_specs=(P("dp", None, "slab", None), P("dp", "slab", None, None), P(), P()),
        check_vma=False,
    )
```

```python
import functools
import math

import jax
import jax.numpy as jnp
import numpy as np
from jax import lax
from jax.experimental import pallas as pl
from jax.experimental.pallas import tpu as pltpu
from jax.sharding import PartitionSpec as P

C = 64
N = 64
XL = 4
S = 16
L = 16
CELLS = 4096
ROWS = C * XL
Q = 512
F32 = jnp.float32
BF16 = jnp.bfloat16


def mm(a, b):
    return jnp.dot(a, b, preferred_element_type=F32)


def nt(a, b):
    return lax.dot_general(a, b, (((1,), (1,)), ((), ())), preferred_element_type=F32)


def tn(a, b):
    return lax.dot_general(a, b, (((0,), (0,)), ((), ())), preferred_element_type=F32)


def waves(count, size):
    return np.array([i if i < count // 2 else size - count + i for i in range(count)])


def phase_tables():
    f = np.float32
    k = np.tile(waves(S, N), 2)[:, None]
    part = np.repeat([0.0, np.pi / 2], S)[:, None]
    unit = 2.0 * np.pi / N
    ang = unit * (k * (np.arange(128) // N)[None, :]) + part
    turn = unit * np.broadcast_to(2 * k, (2 * S, 128))
    angz = unit * ((np.arange(L)[:, None] * (np.arange(128) % N)[None, :]) % N)
    pair = lambda a, scale: np.concatenate([np.cos(a), np.sin(a)]) * scale
    return np.concatenate([pair(ang, 1.0 / N), pair(turn, 1.0), pair(angz, 1.0)]).astype(f)


def x_tables():
    ang = 2.0 * np.pi * ((np.arange(N)[:, None] * waves(16, N)[None, :]) % N) / N
    return np.cos(ang) / 8.0, np.sin(ang) / 8.0


def constants():
    cos, sin = x_tables()
    fx = np.zeros((64, 128))
    fo = np.zeros((64, 128))
    iv = np.zeros((128, 64))
    ia = np.zeros((128, 64))
    for i in range(16):
        for h in range(2):
            for x in range(N):
                c, s = cos[x, i], sin[x, i]
                re, im = i * 4 + h * 2, i * 4 + h * 2 + 1
                fx[re, 2 * x : 2 * x + 2] = (c, s)
                fx[im, 2 * x : 2 * x + 2] = (-s, c)
                fo[re, 2 * x : 2 * x + 2] = (-s, c)
                fo[im, 2 * x : 2 * x + 2] = (-c, -s)
                vre, vim = (re, im) if h == 0 else (im, re)
                iv[2 * x, vre], iv[2 * x, vim] = c, -s
                iv[2 * x + 1, vre], iv[2 * x + 1, vim] = s, c
                ia[2 * x, re], ia[2 * x, im] = c, -s
                ia[2 * x + 1, re], ia[2 * x + 1, im] = s, c
    gather = np.zeros((2, 128, 128))
    for i in range(16):
        for h in range(2):
            for q in range(4):
                gather[h, i * 8 + h * 4 + q, (q // 2) * 64 + i * 4 + q % 2] = 1
    pick = np.zeros((6, 32, 128))
    for b in range(16):
        for h in range(2):
            base = b * 8 + h * 4
            pick[h * 3, b * 2, base] = 1
            pick[h * 3, b * 2 + 1, base + 1] = 1
            pick[h * 3 + 1, b * 2, base + 2] = 1
            pick[h * 3 + 1, b * 2 + 1, base + 3] = 1
            pick[h * 3 + 2, b * 2, base + 3] = 1
            pick[h * 3 + 2, b * 2 + 1, base + 2] = -1
    bf = lambda v: jnp.asarray(np.asarray(v, np.float32), BF16)
    return {
        "fx": bf(fx),
        "fo": bf(fo),
        "iv": bf(iv),
        "ia": bf(ia),
        "gather": bf(gather),
        "pick": bf(pick),
    }


def lanes(shape):
    return lax.broadcasted_iota(jnp.int32, shape, 1)


def subl(shape):
    return lax.broadcasted_iota(jnp.int32, shape, 0)


def low_half(shape):
    return (lanes(shape) & 64) == 0


def half_turn(v):
    return pltpu.roll(v, 64, 1)


def pack_spectra(acc, perm, z_ref, out_ref):
    s = mm(acc.astype(BF16), perm)
    low = low_half((32, 128))

    def put(x, u, v):
        z_ref[u, pl.ds(2 * x, S, stride=8), :] = v[:S]
        z_ref[u, pl.ds(2 * x + 1, S, stride=8), :] = v[S:]

    for u in range(L // 2):
        for t in range(2):
            a = s[u * 64 : u * 64 + 32, t * 128 : t * 128 + 128]
            b = s[u * 64 + 32 : u * 64 + 64, t * 128 : t * 128 + 128]
            put(2 * t, u, jnp.where(low, a, half_turn(b)))
            put(2 * t + 1, u, jnp.where(low, half_turn(a), b))
    for u in range(L // 2):
        out_ref[:, u * 128 : u * 128 + 128] = z_ref[u].astype(BF16)


def unpack_back(arrived, perm, z_ref, b_ref, doubled):
    for u in range(L // 2):
        z_ref[u] = arrived[:, u * 128 : u * 128 + 128].astype(F32)
    low = low_half((32, 128))

    def take(x, u):
        parts = [z_ref[u, pl.ds(2 * x + p, S, stride=8), :] for p in range(2)]
        return jnp.concatenate(parts, axis=0)

    for u in range(L // 2):
        for t in range(2):
            a, b = take(2 * t, u), take(2 * t + 1, u)
            first = jnp.where(low, a, half_turn(b))
            second = jnp.where(low, half_turn(a), b)
            if doubled:
                first = first * (1.0 if u == 0 else 2.0)
                second = second * 2.0
            b_ref[u * 64 : u * 64 + 32, t * 128 : t * 128 + 128] = first.astype(BF16)
            b_ref[u * 64 + 32 : u * 64 + 64, t * 128 : t * 128 + 128] = second.astype(BF16)
    return nt(perm, b_ref[...]).astype(BF16)


def halves_of(v):
    hi = v.astype(BF16)
    return hi, (v - hi.astype(F32)).astype(BF16)


def split(v):
    hi, lo = halves_of(v)
    return jnp.where(low_half(v.shape), hi.astype(F32), lo.astype(F32)).astype(BF16)


def spread_weight(w):
    e = (subl((ROWS, C)) // XL == lanes((ROWS, C))).astype(BF16)
    left = mm(e, w)
    full = nt(left.astype(BF16), e)
    same = (subl((ROWS, ROWS)) & 3) == (lanes((ROWS, ROWS)) & 3)
    return jnp.where(same, full, 0.0).astype(BF16)


def onehot(match):
    return jnp.where(match, 1.0, 0.0).astype(BF16)


def lane_order():
    r, k = subl((ROWS, ROWS)), lanes((ROWS, ROWS))
    return onehot(((r >> 2) == (k & 63)) & ((r & 3) == (k >> 6)))


def ext_order(r, k):
    return onehot(((r >> 3) == ((k >> 2) & 15)) & (((r >> 2) & 1) == (k >> 6)) & ((r & 3) == (k & 3)))


SQUARE = (128, 128)

STEPS = 8
CHUNK = CELLS // STEPS
EXACT = functools.partial(
    lax.dot_general, precision=lax.Precision.HIGHEST, preferred_element_type=F32
)
NT = (((1,), (1,)), ((), ()))
NN = (((1,), (0,)), ((), ()))


def at(step):
    if isinstance(step, int):
        return slice(step * CHUNK, step * CHUNK + CHUNK)
    return pl.ds(pl.multiple_of(step * CHUNK, CHUNK), CHUNK)


def planes(src, dst, sems, step):
    return pltpu.make_async_copy(src.at[:, :, at(step)], dst.at[:, :, at(step)], sems.at[step])


def columns(src, dst, sems, step):
    return pltpu.make_async_copy(src.at[:, at(step)], dst.at[:, at(step)], sems.at[step])


def modes_pair(src, dst, sems, u):
    return pltpu.make_async_copy(src.at[:, pl.ds(2 * u, 2)], dst.at[:, pl.ds(2 * u, 2)], sems.at[u])


def start_all(copy, src, dst, sems):
    for n in range(STEPS):
        copy(src, dst, sems, n).start()


def wait_all(copy, src, dst, sems):
    for n in range(STEPS):
        copy(src, dst, sems, n).wait()


def make_table(phase_ref, ca, sa, refs, tiles):
    cr, sr = phase_ref[64:96, :], phase_ref[96:128, :]
    for g in tiles:
        for l in range(L):
            cb, sb = phase_ref[128 + l : 129 + l, :], phase_ref[144 + l : 145 + l, :]
            v = (ca * cb - sa * sb).astype(BF16)
            for ref, start in refs:
                ref[l * 32 : l * 32 + 32, pl.ds(start + g * 128, 128)] = v
        ca, sa = ca * cr - sa * sr, sa * cr + ca * sr
    return ca, sa


def spectra_kernel(
    f_hbm, phase_hbm, w_hbm,
    out_ref, tf_ref, w_ref,
    f_ref, ta_ref, tb_ref, acc_ref, z_ref, phase_ref, f_sem, p_sem,
):
    phases = pltpu.make_async_copy(phase_hbm, phase_ref, p_sem.at[0])
    phases.start()
    start_all(planes, f_hbm, f_ref, f_sem)
    weights = pltpu.make_async_copy(w_hbm, w_ref, p_sem.at[1])
    acc_ref[...] = jnp.zeros_like(acc_ref)
    tf_ref[Q + ROWS :, :] = jnp.ones((16, CELLS), BF16)
    perm = lane_order()
    phases.wait()

    def make(n, ca, sa, buf_ref):
        start = n * CHUNK if isinstance(n, int) else pl.multiple_of(n * CHUNK, CHUNK)
        return make_table(phase_ref, ca, sa, ((buf_ref, 0), (tf_ref, start)), range(4))

    def add(n, buf_ref):
        flat = f_ref[:, :, at(n)].reshape(ROWS, CHUNK)
        tf_ref[Q : Q + ROWS, at(n)] = flat
        acc_ref[...] += nt(buf_ref[...], flat)

    ca, sa = make(0, phase_ref[:32, :], phase_ref[32:64, :], ta_ref)
    weights.start()

    def step(m, carry):
        n = 2 * m
        planes(f_hbm, f_ref, f_sem, n).wait()
        planes(f_hbm, f_ref, f_sem, n + 1).wait()
        add(n, ta_ref)
        carry = make(n + 1, *carry, tb_ref)
        add(n + 1, tb_ref)
        return make(n + 2, *carry, ta_ref)

    ca, sa = lax.fori_loop(0, STEPS // 2 - 1, step, (ca, sa))
    planes(f_hbm, f_ref, f_sem, STEPS - 2).wait()
    planes(f_hbm, f_ref, f_sem, STEPS - 1).wait()
    add(STEPS - 2, ta_ref)
    make(STEPS - 1, ca, sa, tb_ref)
    add(STEPS - 1, tb_ref)
    pack_spectra(acc_ref[...], perm, z_ref, out_ref)
    weights.wait()


def mix_kernel(r_ref, w_ref, fx_ref, iv_ref, out_ref, m_ref, mask_ref, v_ref):
    m = mm(fx_ref[...], r_ref[...])
    m_ref[...] = m.astype(BF16)
    shape = m.shape
    own = ((lanes(shape) >> 6) & 1) == ((subl(shape) >> 1) & 1)
    mask_ref[...] = jnp.where(own, m, 0.0)
    row, lane = subl((8, 128)), lanes((8, 128))
    top = row < 4
    even = (row & 1) == 0
    sign = jnp.where(lane < 64, -1.0, 1.0)
    keep = (lane >> 6) == ((row >> 1) & 1)

    def step(u, carry):
        cols = pl.ds(pl.multiple_of(u * 128, 128), 128)
        pair = pl.ds(2 * u, 2)
        for t in range(8):
            left = mask_ref[8 * t : 8 * t + 8, cols].astype(BF16)
            right = jnp.concatenate(
                [w_ref[2 * t, pair].reshape(128, 128), w_ref[2 * t + 1, pair].reshape(128, 128)],
                axis=1,
            )
            o = mm(left, right)
            res = jnp.where(top, o[:, :128], o[:, 128:])
            turned = half_turn(res)
            above = pltpu.roll(turned, 7, 0)
            below = pltpu.roll(turned, 1, 0)
            v = jnp.where(even, res + sign * above, below - sign * res)
            v_ref[8 * t : 8 * t + 8, cols] = jnp.where(keep, v, 0.0)
        return carry

    lax.fori_loop(0, L // 2, step, 0)
    out_ref[...] = mm(iv_ref[...], v_ref[...].astype(BF16)).astype(BF16)


def slope(v):
    a = jnp.abs(v)
    e = jnp.exp(v * v * -0.5)
    t = 1.0 / (1.0 + (0.3275911 / math.sqrt(2.0)) * a)
    poly = t * (
        0.5 * 0.254829592
        + t
        * (
            0.5 * -0.284496736
            + t * (0.5 * 1.421413741 + t * (0.5 * -1.453152027 + t * (0.5 * 1.061405429)))
        )
    )
    tail = e * (poly - a * (1.0 / math.sqrt(2.0 * math.pi)))
    return jnp.where(v < 0, tail, 1.0 - tail)


def delta_kernel(
    r_ref, tf_ref, ct_hbm, w_ref, bias_ref,
    out_ref, d_hbm,
    ct_ref, d_ref, bl_ref, shift_ref, pa_ref, pb_ref, da_ref, db_ref,
    sg_ref, bt_ref, z_ref, ct_sem, d_sem,
):
    start_all(planes, ct_hbm, ct_ref, ct_sem)
    bl_ref[:, :Q] = unpack_back(r_ref[...], lane_order(), z_ref, bt_ref, True)
    bl_ref[:, Q:] = spread_weight(w_ref[...])
    e = (subl((ROWS, C)) // XL == lanes((ROWS, C))).astype(F32)
    shift_ref[...] = EXACT(e, jnp.broadcast_to(bias_ref[...], (128, C)), NT)
    sg_ref[...] = jnp.zeros_like(sg_ref)
    db_ref[...] = jnp.zeros_like(db_ref)

    def before(n, p_ref, halves=(0, 1)):
        for h in halves:
            cols = pl.ds(pl.multiple_of(n * CHUNK + h * 256, 256), 256)
            p_ref[:, h * 256 : h * 256 + 256] = mm(bl_ref[...], tf_ref[: Q + ROWS, cols])

    def add(n, own_ref, first, last):
        sg_ref[first:last, :] += nt(tf_ref[first:last, at(n)], own_ref[...])

    def bend(n, p_ref, own_ref, blocks):
        for r in blocks:
            rows = slice(r * 16, r * 16 + 16)
            v = p_ref[rows, :] + jnp.concatenate([shift_ref[rows, :]] * (CHUNK // 128), axis=1)
            ct = ct_ref[r * 4 : r * 4 + 4, :, at(n)].reshape(16, CHUNK)
            d = (ct.astype(F32) * slope(v)).astype(BF16)
            own_ref[rows, :] = d
            d_ref[rows, at(n)] = d

    def weave(n, p_ref, next_ref, own_ref, past_ref):
        past, later = jnp.maximum(n - 1, 0), jnp.minimum(n + 1, STEPS - 1)
        add(past, past_ref, 0, 256)
        bend(n, p_ref, own_ref, range(0, 3))
        add(past, past_ref, 256, 512)
        bend(n, p_ref, own_ref, range(3, 6))
        add(past, past_ref, 512, 784)
        bend(n, p_ref, own_ref, range(6, 9))
        before(later, next_ref, (0,))
        bend(n, p_ref, own_ref, range(9, 12))
        before(later, next_ref, (1,))
        bend(n, p_ref, own_ref, range(12, 16))
        columns(d_ref, d_hbm, d_sem, n).start()

    before(0, pa_ref)

    def step(m, carry):
        n = 2 * m
        planes(ct_hbm, ct_ref, ct_sem, n).wait()
        planes(ct_hbm, ct_ref, ct_sem, n + 1).wait()
        weave(n, pa_ref, pb_ref, da_ref, db_ref)
        weave(n + 1, pb_ref, pa_ref, db_ref, da_ref)
        return carry

    lax.fori_loop(0, STEPS // 2, step, 0)
    add(STEPS - 1, db_ref, 0, 784)
    doubled = jnp.where(subl((Q, ROWS)) < 32, 1.0, 2.0)
    pack_spectra(sg_ref[:Q, :] * doubled, lane_order(), z_ref, out_ref)
    same = (subl((ROWS, ROWS)) & 3) == (lanes((ROWS, ROWS)) & 3)
    g = jnp.where(same, sg_ref[Q : Q + ROWS, :], 0.0)
    e = onehot(subl((C, ROWS)) == lanes((C, ROWS)) // XL)
    e2 = onehot((subl((ROWS, 128)) // XL) == (lanes((ROWS, 128)) & 63))
    wg = [nt(e, half) for half in halves_of(g)]
    wg = [mm(half, e2) for half in halves_of(wg[0] + wg[1])]
    sums = jnp.broadcast_to(sg_ref[Q + ROWS : Q + ROWS + 1, :], (128, ROWS))
    bg = [nt(e, half) for half in halves_of(sums)]
    both = jnp.concatenate([wg[0] + wg[1], bg[0] + bg[1]], axis=0)
    out_ref[:, 1024:] = mm(ext_order(subl(SQUARE), lanes(SQUARE)), split(both)).astype(BF16)
    wait_all(columns, d_ref, d_hbm, d_sem)


def total_of(ext):
    shape = (8, 128)
    pick = ((lanes(shape) & 7) == subl(shape)).astype(BF16)
    v = mm(pick, ext)
    return v + half_turn(v)


def spread_total(v):
    return jnp.concatenate([split(v).astype(F32)] * S, axis=0).astype(BF16)


def grad_modes_kernel(r_ref, m_ref, fx_ref, fo_ref, gather_ref, left_ref, dp_ref, ext_ref):
    r = r_ref[:, :1024]
    a = mm(fx_ref[...], r)
    b = mm(fo_ref[...], r)
    row = subl((64, 128))
    first = ((row >> 1) & 1) == 0
    low = low_half((64, 128))
    for u in range(8):
        cols = slice(u * 128, u * 128 + 128)
        au, bu = a[:, cols], b[:, cols]
        left_ref[:, cols] = jnp.where(
            first, jnp.where(low, au, half_turn(bu)), jnp.where(low, half_turn(au), bu)
        ).astype(BF16)
    both = jnp.concatenate([m_ref[...], a.astype(BF16)], axis=0)
    dp_ref[...] = (mm(gather_ref[0], both[:, :512]) + mm(gather_ref[1], both[:, 512:])).astype(BF16)
    ext_ref[...] = spread_total(total_of(r_ref[:, 1024:]))


def adjoint_kernel(left_ref, w_hbm, ia_ref, ext_ref, out_ref, w_ref, v_ref, w_sem):
    start_all(modes_pair, w_hbm, w_ref, w_sem)
    row, lane = subl((8, 128)), lanes((8, 128))
    top = row < 4
    keep = (lane >> 6) == ((row >> 1) & 1)

    def step(u, carry):
        cols = pl.ds(pl.multiple_of(u * 128, 128), 128)
        pair = pl.ds(2 * u, 2)
        modes_pair(w_hbm, w_ref, w_sem, u).wait()
        for t in range(8):
            right = jnp.concatenate(
                [w_ref[2 * t, pair].reshape(128, 128), w_ref[2 * t + 1, pair].reshape(128, 128)],
                axis=0,
            )
            o = nt(left_ref[8 * t : 8 * t + 8, cols], right)
            res = jnp.where(top, o[:, :128], o[:, 128:])
            v_ref[8 * t : 8 * t + 8, cols] = jnp.where(keep, res, 0.0)
        return carry

    lax.fori_loop(0, L // 2, step, 0)
    out_ref[:, :1024] = mm(ia_ref[...], v_ref[...].astype(BF16)).astype(BF16)
    out_ref[:, 1024:] = ext_ref[...]


def assemble_kernel(r_ref, part_ref, out_ref):
    out_ref[:, :512] = part_ref[...]
    v = mm(ext_order(lanes(SQUARE), subl(SQUARE)), r_ref[:, 1024:])
    v = v + half_turn(v)
    low = low_half((8, 128))
    tiles = [jnp.where(low, v[p : p + 8], v[p + 8 : p + 16]) for p in range(0, C, 16)]
    diag = subl((C, 128)) == lanes((C, 128))
    hi, lo = halves_of(jnp.sum(jnp.where(diag, v[C:], 0.0), axis=0, keepdims=True))
    row = subl((8, 128))
    bias = jnp.where(row == 0, hi.astype(F32), jnp.where(row == 1, lo.astype(F32), 0.0))
    sums = jnp.concatenate(tiles + [bias], axis=1)
    out_ref[:, 512:] = jnp.concatenate([sums] * S, axis=0).astype(BF16)


def weight_grad_kernel(
    dp_ref, pick_ref, out_hbm, pg_hbm, bg_hbm, out_ref, pg_ref, bg_ref, o_sem, g_sem
):
    shape = (8, 128)
    which = onehot((lanes(shape) & 7) == subl(shape))
    sums = mm(which, dp_ref[:, 512:]) * (1.0 / 2048.0)
    for p in range(4):
        tile = sums[:, p * 128 : p * 128 + 128]
        pg_ref[p * 16 : p * 16 + 8, :] = tile[:, :C]
        pg_ref[p * 16 + 8 : p * 16 + 16, :] = half_turn(tile)[:, :C]
    bg_ref[...] = sums[0:1, 512 : 512 + C] + sums[1:2, 512 : 512 + C]
    copies = [
        pltpu.make_async_copy(pg_ref, pg_hbm, g_sem.at[0]),
        pltpu.make_async_copy(bg_ref, bg_hbm, g_sem.at[1]),
    ]
    for copy in copies:
        copy.start()
    low = low_half((32, 128))
    data = dp_ref[:, :512]
    for h in range(2):
        m = mm(pick_ref[h * 3], data)
        g1 = mm(pick_ref[h * 3 + 1], data)
        g2 = mm(pick_ref[h * 3 + 2], data)
        for v in range(4):
            cols = slice(v * 128, v * 128 + 128)
            a, b = g1[:, cols], g2[:, cols]
            right = jnp.concatenate(
                [jnp.where(low, a, half_turn(b)), jnp.where(low, half_turn(a), b)], axis=1
            )
            o = tn(m[:, cols].astype(BF16), right.astype(BF16)) * 0.25
            l = h * 8 + v * 2
            out_ref[l] = o[:64, :128]
            out_ref[l + 1] = o[64:, 128:]
        part = pl.ds(h * 8, 8)
        copies.append(pltpu.make_async_copy(out_ref.at[part], out_hbm.at[part], o_sem.at[h]))
        copies[-1].start()
    for copy in copies:
        copy.wait()


def input_grad_kernel(
    r_ref, d_hbm, w_ref, phase_ref,
    out_hbm,
    d_ref, ta_ref, tb_ref, o_ref, bl_ref, bt_ref, z_ref, d_sem, o_sem,
):
    start_all(columns, d_hbm, d_ref, d_sem)
    bl_ref[:, :Q] = unpack_back(r_ref[:, :1024], lane_order(), z_ref, bt_ref, False)
    bl_ref[:, Q:] = spread_weight(w_ref[...]).astype(F32).T.astype(BF16)

    def finish(n, own_ref):
        out = mm(bl_ref[:, :Q], own_ref[...]) + mm(bl_ref[:, Q:], d_ref[:, at(n)])
        o_ref[:, :, at(n)] = out.astype(BF16).reshape(C, XL, CHUNK)

    def make(carry, next_ref):
        return make_table(phase_ref, *carry, ((next_ref, 0),), range(4))

    def step(m, carry):
        n = 2 * m
        columns(d_hbm, d_ref, d_sem, n).wait()
        columns(d_hbm, d_ref, d_sem, n + 1).wait()
        finish(n, ta_ref)
        carry = make(carry, tb_ref)
        finish(n + 1, tb_ref)
        carry = make(carry, ta_ref)
        planes(o_ref, out_hbm, o_sem, n).start()
        planes(o_ref, out_hbm, o_sem, n + 1).start()
        return carry

    carry = make((phase_ref[:32, :], phase_ref[32:64, :]), ta_ref)
    carry = lax.fori_loop(0, STEPS // 2 - 1, step, carry)
    columns(d_hbm, d_ref, d_sem, STEPS - 2).wait()
    columns(d_hbm, d_ref, d_sem, STEPS - 1).wait()
    finish(STEPS - 2, ta_ref)
    planes(o_ref, out_hbm, o_sem, STEPS - 2).start()
    make(carry, tb_ref)
    finish(STEPS - 1, tb_ref)
    planes(o_ref, out_hbm, o_sem, STEPS - 1).start()
    wait_all(planes, o_ref, out_hbm, o_sem)


def call(kernel, name, outs, scratch, args, big=(), big_outs=(), sems=0, room=8):
    place = lambda n, far: pl.BlockSpec(memory_space=pltpu.HBM if n in far else pltpu.VMEM)
    return pl.pallas_call(
        kernel,
        in_specs=[place(n, big) for n in range(len(args))],
        out_specs=[place(n, big_outs) for n in range(len(outs))],
        out_shape=[
            (pltpu.HBM if n in big_outs else pltpu.VMEM)(shape, dtype)
            for n, (shape, dtype) in enumerate(outs)
        ],
        scratch_shapes=[pltpu.VMEM(shape, dtype) for shape, dtype in scratch]
        + [pltpu.SemaphoreType.DMA((STEPS,))] * sems,
        compiler_params=pltpu.CompilerParams(vmem_limit_bytes=room << 20),
        name=name,
    )(
        *[
            pltpu.with_memory_space_constraint(a, pltpu.HBM if n in big else pltpu.VMEM)
            for n, a in enumerate(args)
        ]
    )


def exchange(v, axis):
    width = v.shape[1]
    out = lax.all_to_all(v.reshape(S, 8, width), axis, split_axis=0, concat_axis=0, tiled=True)
    return out.reshape(128, width)


def body(field, cotangent, spectral_weight, point_weight, bias):
    k = constants()
    field3 = field.reshape(C, XL, CELLS)
    cot3 = cotangent.reshape(C, XL, CELLS)
    planes_shape = ((C, XL, CELLS), BF16)
    cells_shape = ((ROWS, CELLS), BF16)
    weight_shape = (spectral_weight.shape, BF16)

    phases = jnp.asarray(phase_tables())
    spectra, rows, weights = call(
        spectra_kernel,
        "spectra",
        [((128, 1024), BF16), ((Q + ROWS + 16, CELLS), BF16), weight_shape],
        [planes_shape, ((Q, CHUNK), BF16), ((Q, CHUNK), BF16), ((Q, ROWS), F32),
         ((L // 2, 128, 128), F32), ((160, 128), F32)],
        [field3, phases, spectral_weight],
        big=(0, 1, 2), sems=2,
    )
    arrived = exchange(spectra, "slab")
    back, modes = call(
        mix_kernel,
        "mix",
        [((128, 1024), BF16), ((64, 1024), BF16)],
        [((64, 1024), F32), ((64, 1024), F32)],
        [arrived, weights, k["fx"], k["iv"]],
    )
    arrived = exchange(back, "slab")
    grad_spectra, delta = call(
        delta_kernel,
        "delta",
        [((128, 1152), BF16), cells_shape],
        [
            planes_shape, cells_shape,
            ((ROWS, Q + ROWS), BF16), ((ROWS, 128), F32),
            ((ROWS, CHUNK), F32), ((ROWS, CHUNK), F32), ((ROWS, CHUNK), BF16), ((ROWS, CHUNK), BF16),
            ((Q + ROWS + 16, ROWS), F32), ((Q, ROWS), BF16), ((L // 2, 128, 128), F32),
        ],
        [arrived, rows, cot3, point_weight, bias.reshape(1, C)],
        big=(2,), big_outs=(1,), sems=2, room=16,
    )
    arrived = exchange(grad_spectra, "slab")
    left, part, sums = call(
        grad_modes_kernel,
        "grad_modes",
        [((64, 1024), BF16), ((128, 512), BF16), (SQUARE, BF16)],
        [],
        [arrived, modes, k["fx"], k["fo"], k["gather"]],
    )
    (adjoint,) = call(
        adjoint_kernel,
        "adjoint",
        [((128, 1152), BF16)],
        [weight_shape, ((64, 1024), F32)],
        [left, spectral_weight, k["ia"], sums],
        big=(1,), sems=1,
    )
    arrived = exchange(adjoint, "slab")
    (shared,) = call(assemble_kernel, "assemble", [((128, 1152), BF16)], [], [arrived, part])
    shared = exchange(shared, "dp")
    (input_grad,) = call(
        input_grad_kernel,
        "input_grad",
        [planes_shape],
        [cells_shape, ((Q, CHUNK), BF16), ((Q, CHUNK), BF16), planes_shape,
         ((ROWS, Q + ROWS), BF16), ((Q, ROWS), BF16), ((L // 2, 128, 128), F32)],
        [arrived, delta, point_weight, phases],
        big=(1,), big_outs=(0,), sems=2, room=16,
    )
    spectral_grad, point_grad, bias_grad = call(
        weight_grad_kernel,
        "weight_grad",
        [((L, C, 128), F32), ((C, C), F32), ((1, C), F32)],
        [((L, C, 128), F32), ((C, C), F32), ((1, C), F32)],
        [shared, k["pick"]],
        big_outs=(0, 1, 2), sems=2,
    )
    return (
        input_grad.reshape(field.shape),
        spectral_grad[None],
        point_grad,
        bias_grad.reshape(C),
    )


def solution(mesh):
    return jax.shard_map(
        body,
        mesh=mesh,
        in_specs=(
            P("dp", None, "slab", None),
            P("dp", None, "slab", None),
            P(None, "slab", None, None),
            P(),
            P(),
        ),
        out_specs=(P("dp", None, "slab", None), P("dp", "slab", None, None), P(), P()),
        check_vma=False,
    )
```

```python
import functools
import math

import jax
import jax.numpy as jnp
import numpy as np
from jax import lax
from jax.experimental import pallas as pl
from jax.experimental.pallas import tpu as pltpu
from jax.sharding import PartitionSpec as P

C = 64
N = 64
XL = 4
S = 16
L = 16
CELLS = 4096
ROWS = C * XL
Q = 512
F32 = jnp.float32
BF16 = jnp.bfloat16


def mm(a, b):
    return jnp.dot(a, b, preferred_element_type=F32)


def nt(a, b):
    return lax.dot_general(a, b, (((1,), (1,)), ((), ())), preferred_element_type=F32)


def tn(a, b):
    return lax.dot_general(a, b, (((0,), (0,)), ((), ())), preferred_element_type=F32)


def waves(count, size):
    return np.array([i if i < count // 2 else size - count + i for i in range(count)])


def phase_tables():
    f = np.float32
    k = np.tile(waves(S, N), 2)[:, None]
    part = np.repeat([0.0, np.pi / 2], S)[:, None]
    unit = 2.0 * np.pi / N
    ang = unit * (k * (np.arange(128) // N)[None, :]) + part
    turn = unit * np.broadcast_to(2 * k, (2 * S, 128))
    angz = unit * ((np.arange(L)[:, None] * (np.arange(128) % N)[None, :]) % N)
    pair = lambda a, scale: np.concatenate([np.cos(a), np.sin(a)]) * scale
    return np.concatenate([pair(ang, 1.0 / N), pair(turn, 1.0), pair(angz, 1.0)]).astype(f)


def x_tables():
    ang = 2.0 * np.pi * ((np.arange(N)[:, None] * waves(16, N)[None, :]) % N) / N
    return np.cos(ang) / 8.0, np.sin(ang) / 8.0


def constants():
    cos, sin = x_tables()
    fx = np.zeros((64, 128))
    fo = np.zeros((64, 128))
    iv = np.zeros((128, 64))
    ia = np.zeros((128, 64))
    for i in range(16):
        for h in range(2):
            for x in range(N):
                c, s = cos[x, i], sin[x, i]
                re, im = i * 4 + h * 2, i * 4 + h * 2 + 1
                fx[re, 2 * x : 2 * x + 2] = (c, s)
                fx[im, 2 * x : 2 * x + 2] = (-s, c)
                fo[re, 2 * x : 2 * x + 2] = (-s, c)
                fo[im, 2 * x : 2 * x + 2] = (-c, -s)
                vre, vim = (re, im) if h == 0 else (im, re)
                iv[2 * x, vre], iv[2 * x, vim] = c, -s
                iv[2 * x + 1, vre], iv[2 * x + 1, vim] = s, c
                ia[2 * x, re], ia[2 * x, im] = c, -s
                ia[2 * x + 1, re], ia[2 * x + 1, im] = s, c
    gather = np.zeros((2, 128, 128))
    for i in range(16):
        for h in range(2):
            for q in range(4):
                gather[h, i * 8 + h * 4 + q, (q // 2) * 64 + i * 4 + q % 2] = 1
    pick = np.zeros((6, 32, 128))
    for b in range(16):
        for h in range(2):
            base = b * 8 + h * 4
            pick[h * 3, b * 2, base] = 1
            pick[h * 3, b * 2 + 1, base + 1] = 1
            pick[h * 3 + 1, b * 2, base + 2] = 1
            pick[h * 3 + 1, b * 2 + 1, base + 3] = 1
            pick[h * 3 + 2, b * 2, base + 3] = 1
            pick[h * 3 + 2, b * 2 + 1, base + 2] = -1
    bf = lambda v: jnp.asarray(np.asarray(v, np.float32), BF16)
    return {
        "fx": bf(fx),
        "fo": bf(fo),
        "iv": bf(iv),
        "ia": bf(ia),
        "gather": bf(gather),
        "pick": bf(pick),
    }


def lanes(shape):
    return lax.broadcasted_iota(jnp.int32, shape, 1)


def subl(shape):
    return lax.broadcasted_iota(jnp.int32, shape, 0)


def low_half(shape):
    return (lanes(shape) & 64) == 0


def half_turn(v):
    return pltpu.roll(v, 64, 1)


def pack_spectra(acc, perm, z_ref, out_ref):
    s = mm(acc.astype(BF16), perm)
    low = low_half((32, 128))

    def put(x, u, v):
        z_ref[u, pl.ds(2 * x, S, stride=8), :] = v[:S]
        z_ref[u, pl.ds(2 * x + 1, S, stride=8), :] = v[S:]

    for u in range(L // 2):
        for t in range(2):
            a = s[u * 64 : u * 64 + 32, t * 128 : t * 128 + 128]
            b = s[u * 64 + 32 : u * 64 + 64, t * 128 : t * 128 + 128]
            put(2 * t, u, jnp.where(low, a, half_turn(b)))
            put(2 * t + 1, u, jnp.where(low, half_turn(a), b))
    for u in range(L // 2):
        out_ref[:, u * 128 : u * 128 + 128] = z_ref[u].astype(BF16)


def unpack_back(arrived, perm, z_ref, b_ref, doubled):
    for u in range(L // 2):
        z_ref[u] = arrived[:, u * 128 : u * 128 + 128].astype(F32)
    low = low_half((32, 128))

    def take(x, u):
        parts = [z_ref[u, pl.ds(2 * x + p, S, stride=8), :] for p in range(2)]
        return jnp.concatenate(parts, axis=0)

    for u in range(L // 2):
        for t in range(2):
            a, b = take(2 * t, u), take(2 * t + 1, u)
            first = jnp.where(low, a, half_turn(b))
            second = jnp.where(low, half_turn(a), b)
            if doubled:
                first = first * (1.0 if u == 0 else 2.0)
                second = second * 2.0
            b_ref[u * 64 : u * 64 + 32, t * 128 : t * 128 + 128] = first.astype(BF16)
            b_ref[u * 64 + 32 : u * 64 + 64, t * 128 : t * 128 + 128] = second.astype(BF16)
    return nt(perm, b_ref[...]).astype(BF16)


def halves_of(v):
    hi = v.astype(BF16)
    return hi, (v - hi.astype(F32)).astype(BF16)


def split(v):
    hi, lo = halves_of(v)
    return jnp.where(low_half(v.shape), hi.astype(F32), lo.astype(F32)).astype(BF16)


def spread_weight(w):
    e = (subl((ROWS, C)) // XL == lanes((ROWS, C))).astype(BF16)
    left = mm(e, w)
    full = nt(left.astype(BF16), e)
    same = (subl((ROWS, ROWS)) & 3) == (lanes((ROWS, ROWS)) & 3)
    return jnp.where(same, full, 0.0).astype(BF16)


def onehot(match):
    return jnp.where(match, 1.0, 0.0).astype(BF16)


def lane_order():
    r, k = subl((ROWS, ROWS)), lanes((ROWS, ROWS))
    return onehot(((r >> 2) == (k & 63)) & ((r & 3) == (k >> 6)))


def ext_order(r, k):
    return onehot(((r >> 3) == ((k >> 2) & 15)) & (((r >> 2) & 1) == (k >> 6)) & ((r & 3) == (k & 3)))


SQUARE = (128, 128)

STEPS = 8
CHUNK = CELLS // STEPS
EXACT = functools.partial(
    lax.dot_general, precision=lax.Precision.HIGHEST, preferred_element_type=F32
)
NT = (((1,), (1,)), ((), ()))
NN = (((1,), (0,)), ((), ()))


def at(step):
    if isinstance(step, int):
        return slice(step * CHUNK, step * CHUNK + CHUNK)
    return pl.ds(pl.multiple_of(step * CHUNK, CHUNK), CHUNK)


def planes(src, dst, sems, step):
    return pltpu.make_async_copy(src.at[:, :, at(step)], dst.at[:, :, at(step)], sems.at[step])


def columns(src, dst, sems, step):
    return pltpu.make_async_copy(src.at[:, at(step)], dst.at[:, at(step)], sems.at[step])


def start_all(copy, src, dst, sems):
    for n in range(STEPS):
        copy(src, dst, sems, n).start()


def wait_all(copy, src, dst, sems):
    for n in range(STEPS):
        copy(src, dst, sems, n).wait()


def make_table(phase_ref, ca, sa, refs, tiles):
    cr, sr = phase_ref[64:96, :], phase_ref[96:128, :]
    for g in tiles:
        for l in range(L):
            cb, sb = phase_ref[128 + l : 129 + l, :], phase_ref[144 + l : 145 + l, :]
            v = (ca * cb - sa * sb).astype(BF16)
            for ref, start in refs:
                ref[l * 32 : l * 32 + 32, pl.ds(start + g * 128, 128)] = v
        ca, sa = ca * cr - sa * sr, sa * cr + ca * sr
    return ca, sa


def spectra_kernel(
    f_hbm, phase_hbm, w_hbm,
    out_ref, tf_ref, w_ref,
    f_ref, ta_ref, tb_ref, acc_ref, z_ref, phase_ref, f_sem, p_sem,
):
    phases = pltpu.make_async_copy(phase_hbm, phase_ref, p_sem.at[0])
    phases.start()
    start_all(planes, f_hbm, f_ref, f_sem)
    weights = pltpu.make_async_copy(w_hbm, w_ref, p_sem.at[1])
    acc_ref[...] = jnp.zeros_like(acc_ref)
    tf_ref[Q + ROWS :, :] = jnp.ones((16, CELLS), BF16)
    perm = lane_order()
    phases.wait()

    def make(n, ca, sa, buf_ref):
        start = n * CHUNK if isinstance(n, int) else pl.multiple_of(n * CHUNK, CHUNK)
        return make_table(phase_ref, ca, sa, ((buf_ref, 0), (tf_ref, start)), range(4))

    def add(n, buf_ref):
        flat = f_ref[:, :, at(n)].reshape(ROWS, CHUNK)
        tf_ref[Q : Q + ROWS, at(n)] = flat
        acc_ref[...] += nt(buf_ref[...], flat)

    ca, sa = make(0, phase_ref[:32, :], phase_ref[32:64, :], ta_ref)
    weights.start()

    def step(m, carry):
        n = 2 * m
        planes(f_hbm, f_ref, f_sem, n).wait()
        planes(f_hbm, f_ref, f_sem, n + 1).wait()
        add(n, ta_ref)
        carry = make(n + 1, *carry, tb_ref)
        add(n + 1, tb_ref)
        return make(n + 2, *carry, ta_ref)

    ca, sa = lax.fori_loop(0, STEPS // 2 - 1, step, (ca, sa))
    planes(f_hbm, f_ref, f_sem, STEPS - 2).wait()
    planes(f_hbm, f_ref, f_sem, STEPS - 1).wait()
    add(STEPS - 2, ta_ref)
    make(STEPS - 1, ca, sa, tb_ref)
    add(STEPS - 1, tb_ref)
    pack_spectra(acc_ref[...], perm, z_ref, out_ref)
    weights.wait()


def mix_kernel(r_ref, w_ref, fx_ref, iv_ref, out_ref, m_ref, mask_ref, v_ref):
    m = mm(fx_ref[...], r_ref[...])
    m_ref[...] = m.astype(BF16)
    shape = m.shape
    own = ((lanes(shape) >> 6) & 1) == ((subl(shape) >> 1) & 1)
    mask_ref[...] = jnp.where(own, m, 0.0)
    row, lane = subl((8, 128)), lanes((8, 128))
    top = row < 4
    even = (row & 1) == 0
    sign = jnp.where(lane < 64, -1.0, 1.0)
    keep = (lane >> 6) == ((row >> 1) & 1)

    def step(u, carry):
        cols = pl.ds(pl.multiple_of(u * 128, 128), 128)
        pair = pl.ds(2 * u, 2)
        for t in range(8):
            left = mask_ref[8 * t : 8 * t + 8, cols].astype(BF16)
            right = jnp.concatenate(
                [w_ref[2 * t, pair].reshape(128, 128), w_ref[2 * t + 1, pair].reshape(128, 128)],
                axis=1,
            )
            o = mm(left, right)
            res = jnp.where(top, o[:, :128], o[:, 128:])
            turned = half_turn(res)
            above = pltpu.roll(turned, 7, 0)
            below = pltpu.roll(turned, 1, 0)
            v = jnp.where(even, res + sign * above, below - sign * res)
            v_ref[8 * t : 8 * t + 8, cols] = jnp.where(keep, v, 0.0)
        return carry

    lax.fori_loop(0, L // 2, step, 0)
    out_ref[...] = mm(iv_ref[...], v_ref[...].astype(BF16)).astype(BF16)


def slope(v):
    a = jnp.abs(v)
    e = jnp.exp2(v * v * (-0.5 / math.log(2.0)))
    t = 1.0 / (1.0 + (0.3275911 / math.sqrt(2.0)) * a)
    poly = t * (
        0.5 * 0.254829592
        + t
        * (
            0.5 * -0.284496736
            + t * (0.5 * 1.421413741 + t * (0.5 * -1.453152027 + t * (0.5 * 1.061405429)))
        )
    )
    tail = e * (poly - a * (1.0 / math.sqrt(2.0 * math.pi)))
    return jnp.where(v < 0, tail, 1.0 - tail)


def delta_kernel(
    r_ref, tf_ref, ct_hbm, w_ref, bias_ref,
    out_ref, d_hbm,
    ct_ref, d_ref, bl_ref, shift_ref, pa_ref, pb_ref, da_ref, db_ref,
    sg_ref, bt_ref, z_ref, ct_sem, d_sem,
):
    start_all(planes, ct_hbm, ct_ref, ct_sem)
    bl_ref[:, :Q] = unpack_back(r_ref[...], lane_order(), z_ref, bt_ref, True)
    bl_ref[:, Q:] = spread_weight(w_ref[...])
    e = (subl((ROWS, C)) // XL == lanes((ROWS, C))).astype(F32)
    shift_ref[...] = EXACT(e, jnp.broadcast_to(bias_ref[...], (128, C)), NT)
    sg_ref[...] = jnp.zeros_like(sg_ref)
    db_ref[...] = jnp.zeros_like(db_ref)

    def before(n, p_ref, halves=(0, 1)):
        for h in halves:
            cols = pl.ds(pl.multiple_of(n * CHUNK + h * 256, 256), 256)
            p_ref[:, h * 256 : h * 256 + 256] = mm(bl_ref[...], tf_ref[: Q + ROWS, cols])

    def add(n, own_ref, first, last):
        sg_ref[first:last, :] += nt(tf_ref[first:last, at(n)], own_ref[...])

    def bend(n, p_ref, own_ref, blocks):
        for r in blocks:
            rows = slice(r * 16, r * 16 + 16)
            v = p_ref[rows, :] + jnp.concatenate([shift_ref[rows, :]] * (CHUNK // 128), axis=1)
            ct = ct_ref[r * 4 : r * 4 + 4, :, at(n)].reshape(16, CHUNK)
            d = (ct.astype(F32) * slope(v)).astype(BF16)
            own_ref[rows, :] = d
            d_ref[rows, at(n)] = d

    def weave(n, p_ref, next_ref, own_ref, past_ref):
        past, later = jnp.maximum(n - 1, 0), jnp.minimum(n + 1, STEPS - 1)
        add(past, past_ref, 0, 256)
        bend(n, p_ref, own_ref, range(0, 3))
        add(past, past_ref, 256, 512)
        bend(n, p_ref, own_ref, range(3, 6))
        add(past, past_ref, 512, 784)
        bend(n, p_ref, own_ref, range(6, 9))
        before(later, next_ref, (0,))
        bend(n, p_ref, own_ref, range(9, 12))
        before(later, next_ref, (1,))
        bend(n, p_ref, own_ref, range(12, 16))
        columns(d_ref, d_hbm, d_sem, n).start()

    before(0, pa_ref)

    def step(m, carry):
        n = 2 * m
        planes(ct_hbm, ct_ref, ct_sem, n).wait()
        planes(ct_hbm, ct_ref, ct_sem, n + 1).wait()
        weave(n, pa_ref, pb_ref, da_ref, db_ref)
        weave(n + 1, pb_ref, pa_ref, db_ref, da_ref)
        return carry

    lax.fori_loop(0, STEPS // 2, step, 0)
    add(STEPS - 1, db_ref, 0, 784)
    doubled = jnp.where(subl((Q, ROWS)) < 32, 1.0, 2.0)
    pack_spectra(sg_ref[:Q, :] * doubled, lane_order(), z_ref, out_ref)
    same = (subl((ROWS, ROWS)) & 3) == (lanes((ROWS, ROWS)) & 3)
    g = jnp.where(same, sg_ref[Q : Q + ROWS, :], 0.0)
    e = onehot(subl((C, ROWS)) == lanes((C, ROWS)) // XL)
    e2 = onehot((subl((ROWS, 128)) // XL) == (lanes((ROWS, 128)) & 63))
    wg = [nt(e, half) for half in halves_of(g)]
    wg = [mm(half, e2) for half in halves_of(wg[0] + wg[1])]
    sums = jnp.broadcast_to(sg_ref[Q + ROWS : Q + ROWS + 1, :], (128, ROWS))
    bg = [nt(e, half) for half in halves_of(sums)]
    both = jnp.concatenate([wg[0] + wg[1], bg[0] + bg[1]], axis=0)
    out_ref[:, 1024:] = mm(ext_order(subl(SQUARE), lanes(SQUARE)), split(both)).astype(BF16)
    wait_all(columns, d_ref, d_hbm, d_sem)


def total_of(ext):
    shape = (8, 128)
    pick = ((lanes(shape) & 7) == subl(shape)).astype(BF16)
    v = mm(pick, ext)
    return v + half_turn(v)


def spread_total(v):
    return jnp.concatenate([split(v).astype(F32)] * S, axis=0).astype(BF16)


def adjoint_kernel(
    r_ref, m_ref, w_ref, fx_ref, fo_ref, ia_ref, gather_ref, out_ref, dp_ref, left_ref, v_ref
):
    r = r_ref[:, :1024]
    a = mm(fx_ref[...], r)
    b = mm(fo_ref[...], r)
    row = subl((64, 128))
    first = ((row >> 1) & 1) == 0
    low = low_half((64, 128))
    for u in range(8):
        cols = slice(u * 128, u * 128 + 128)
        au, bu = a[:, cols], b[:, cols]
        left_ref[:, cols] = jnp.where(
            first, jnp.where(low, au, half_turn(bu)), jnp.where(low, half_turn(au), bu)
        ).astype(BF16)
    both = jnp.concatenate([m_ref[...], a.astype(BF16)], axis=0)
    dp_ref[...] = (mm(gather_ref[0], both[:, :512]) + mm(gather_ref[1], both[:, 512:])).astype(BF16)
    out_ref[:, 1024:] = spread_total(total_of(r_ref[:, 1024:]))
    row, lane = subl((8, 128)), lanes((8, 128))
    top = row < 4
    keep = (lane >> 6) == ((row >> 1) & 1)

    def step(u, carry):
        cols = pl.ds(pl.multiple_of(u * 128, 128), 128)
        pair = pl.ds(2 * u, 2)
        for t in range(8):
            right = jnp.concatenate(
                [w_ref[2 * t, pair].reshape(128, 128), w_ref[2 * t + 1, pair].reshape(128, 128)],
                axis=0,
            )
            o = nt(left_ref[8 * t : 8 * t + 8, cols], right)
            res = jnp.where(top, o[:, :128], o[:, 128:])
            v_ref[8 * t : 8 * t + 8, cols] = jnp.where(keep, res, 0.0)
        return carry

    lax.fori_loop(0, L // 2, step, 0)
    out_ref[:, :1024] = mm(ia_ref[...], v_ref[...].astype(BF16)).astype(BF16)


def assemble_kernel(r_ref, part_ref, out_ref):
    out_ref[:, :512] = part_ref[...]
    v = mm(ext_order(lanes(SQUARE), subl(SQUARE)), r_ref[:, 1024:])
    v = v + half_turn(v)
    low = low_half((8, 128))
    tiles = [jnp.where(low, v[p : p + 8], v[p + 8 : p + 16]) for p in range(0, C, 16)]
    diag = subl((C, 128)) == lanes((C, 128))
    hi, lo = halves_of(jnp.sum(jnp.where(diag, v[C:], 0.0), axis=0, keepdims=True))
    row = subl((8, 128))
    bias = jnp.where(row == 0, hi.astype(F32), jnp.where(row == 1, lo.astype(F32), 0.0))
    sums = jnp.concatenate(tiles + [bias], axis=1)
    out_ref[:, 512:] = jnp.concatenate([sums] * S, axis=0).astype(BF16)


def weight_grad_kernel(
    dp_ref, pick_ref, out_hbm, pg_hbm, bg_hbm, out_ref, pg_ref, bg_ref, o_sem, g_sem
):
    shape = (8, 128)
    which = onehot((lanes(shape) & 7) == subl(shape))
    sums = mm(which, dp_ref[:, 512:]) * (1.0 / 2048.0)
    for p in range(4):
        tile = sums[:, p * 128 : p * 128 + 128]
        pg_ref[p * 16 : p * 16 + 8, :] = tile[:, :C]
        pg_ref[p * 16 + 8 : p * 16 + 16, :] = half_turn(tile)[:, :C]
    bg_ref[...] = sums[0:1, 512 : 512 + C] + sums[1:2, 512 : 512 + C]
    copies = [
        pltpu.make_async_copy(pg_ref, pg_hbm, g_sem.at[0]),
        pltpu.make_async_copy(bg_ref, bg_hbm, g_sem.at[1]),
    ]
    for copy in copies:
        copy.start()
    low = low_half((32, 128))
    data = dp_ref[:, :512]
    for h in range(2):
        m = mm(pick_ref[h * 3], data)
        g1 = mm(pick_ref[h * 3 + 1], data)
        g2 = mm(pick_ref[h * 3 + 2], data)
        for v in range(4):
            cols = slice(v * 128, v * 128 + 128)
            a, b = g1[:, cols], g2[:, cols]
            right = jnp.concatenate(
                [jnp.where(low, a, half_turn(b)), jnp.where(low, half_turn(a), b)], axis=1
            )
            o = tn(m[:, cols].astype(BF16), right.astype(BF16)) * 0.25
            l = h * 8 + v * 2
            out_ref[l] = o[:64, :128]
            out_ref[l + 1] = o[64:, 128:]
        part = pl.ds(h * 8, 8)
        copies.append(pltpu.make_async_copy(out_ref.at[part], out_hbm.at[part], o_sem.at[h]))
        copies[-1].start()
    for copy in copies:
        copy.wait()


def input_grad_kernel(
    r_ref, d_hbm, w_ref, phase_ref,
    out_hbm,
    d_ref, ta_ref, tb_ref, o_ref, bl_ref, bt_ref, z_ref, d_sem, o_sem,
):
    start_all(columns, d_hbm, d_ref, d_sem)
    bl_ref[:, :Q] = unpack_back(r_ref[:, :1024], lane_order(), z_ref, bt_ref, False)
    bl_ref[:, Q:] = spread_weight(w_ref[...]).astype(F32).T.astype(BF16)

    def finish(n, own_ref):
        out = mm(bl_ref[:, :Q], own_ref[...]) + mm(bl_ref[:, Q:], d_ref[:, at(n)])
        o_ref[:, :, at(n)] = out.astype(BF16).reshape(C, XL, CHUNK)

    def make(carry, next_ref):
        return make_table(phase_ref, *carry, ((next_ref, 0),), range(4))

    def step(m, carry):
        n = 2 * m
        columns(d_hbm, d_ref, d_sem, n).wait()
        columns(d_hbm, d_ref, d_sem, n + 1).wait()
        finish(n, ta_ref)
        carry = make(carry, tb_ref)
        finish(n + 1, tb_ref)
        carry = make(carry, ta_ref)
        planes(o_ref, out_hbm, o_sem, n).start()
        planes(o_ref, out_hbm, o_sem, n + 1).start()
        return carry

    carry = make((phase_ref[:32, :], phase_ref[32:64, :]), ta_ref)
    carry = lax.fori_loop(0, STEPS // 2 - 1, step, carry)
    columns(d_hbm, d_ref, d_sem, STEPS - 2).wait()
    columns(d_hbm, d_ref, d_sem, STEPS - 1).wait()
    finish(STEPS - 2, ta_ref)
    planes(o_ref, out_hbm, o_sem, STEPS - 2).start()
    make(carry, tb_ref)
    finish(STEPS - 1, tb_ref)
    planes(o_ref, out_hbm, o_sem, STEPS - 1).start()
    wait_all(planes, o_ref, out_hbm, o_sem)


def call(kernel, name, outs, scratch, args, big=(), big_outs=(), sems=0, room=8):
    place = lambda n, far: pl.BlockSpec(memory_space=pltpu.HBM if n in far else pltpu.VMEM)
    return pl.pallas_call(
        kernel,
        in_specs=[place(n, big) for n in range(len(args))],
        out_specs=[place(n, big_outs) for n in range(len(outs))],
        out_shape=[
            (pltpu.HBM if n in big_outs else pltpu.VMEM)(shape, dtype)
            for n, (shape, dtype) in enumerate(outs)
        ],
        scratch_shapes=[pltpu.VMEM(shape, dtype) for shape, dtype in scratch]
        + [pltpu.SemaphoreType.DMA((STEPS,))] * sems,
        compiler_params=pltpu.CompilerParams(vmem_limit_bytes=room << 20),
        name=name,
    )(
        *[
            pltpu.with_memory_space_constraint(a, pltpu.HBM if n in big else pltpu.VMEM)
            for n, a in enumerate(args)
        ]
    )


def exchange(v, axis):
    width = v.shape[1]
    out = lax.all_to_all(v.reshape(S, 8, width), axis, split_axis=0, concat_axis=0, tiled=True)
    return out.reshape(128, width)


def body(field, cotangent, spectral_weight, point_weight, bias):
    k = constants()
    field3 = field.reshape(C, XL, CELLS)
    cot3 = cotangent.reshape(C, XL, CELLS)
    planes_shape = ((C, XL, CELLS), BF16)
    cells_shape = ((ROWS, CELLS), BF16)
    weight_shape = (spectral_weight.shape, BF16)

    phases = jnp.asarray(phase_tables())
    spectra, rows, weights = call(
        spectra_kernel,
        "spectra",
        [((128, 1024), BF16), ((Q + ROWS + 16, CELLS), BF16), weight_shape],
        [planes_shape, ((Q, CHUNK), BF16), ((Q, CHUNK), BF16), ((Q, ROWS), F32),
         ((L // 2, 128, 128), F32), ((160, 128), F32)],
        [field3, phases, spectral_weight],
        big=(0, 1, 2), sems=2,
    )
    arrived = exchange(spectra, "slab")
    back, modes = call(
        mix_kernel,
        "mix",
        [((128, 1024), BF16), ((64, 1024), BF16)],
        [((64, 1024), F32), ((64, 1024), F32)],
        [arrived, weights, k["fx"], k["iv"]],
    )
    arrived = exchange(back, "slab")
    grad_spectra, delta = call(
        delta_kernel,
        "delta",
        [((128, 1152), BF16), cells_shape],
        [
            planes_shape, cells_shape,
            ((ROWS, Q + ROWS), BF16), ((ROWS, 128), F32),
            ((ROWS, CHUNK), F32), ((ROWS, CHUNK), F32), ((ROWS, CHUNK), BF16), ((ROWS, CHUNK), BF16),
            ((Q + ROWS + 16, ROWS), F32), ((Q, ROWS), BF16), ((L // 2, 128, 128), F32),
        ],
        [arrived, rows, cot3, point_weight, bias.reshape(1, C)],
        big=(2,), big_outs=(1,), sems=2, room=16,
    )
    arrived = exchange(grad_spectra, "slab")
    adjoint, part = call(
        adjoint_kernel,
        "adjoint",
        [((128, 1152), BF16), ((128, 512), BF16)],
        [((64, 1024), BF16), ((64, 1024), F32)],
        [arrived, modes, weights, k["fx"], k["fo"], k["ia"], k["gather"]],
    )
    arrived = exchange(adjoint, "slab")
    (shared,) = call(assemble_kernel, "assemble", [((128, 1152), BF16)], [], [arrived, part])
    shared = exchange(shared, "dp")
    (input_grad,) = call(
        input_grad_kernel,
        "input_grad",
        [planes_shape],
        [cells_shape, ((Q, CHUNK), BF16), ((Q, CHUNK), BF16), planes_shape,
         ((ROWS, Q + ROWS), BF16), ((Q, ROWS), BF16), ((L // 2, 128, 128), F32)],
        [arrived, delta, point_weight, phases],
        big=(1,), big_outs=(0,), sems=2, room=16,
    )
    spectral_grad, point_grad, bias_grad = call(
        weight_grad_kernel,
        "weight_grad",
        [((L, C, 128), F32), ((C, C), F32), ((1, C), F32)],
        [((L, C, 128), F32), ((C, C), F32), ((1, C), F32)],
        [shared, k["pick"]],
        big_outs=(0, 1, 2), sems=2,
    )
    return (
        input_grad.reshape(field.shape),
        spectral_grad[None],
        point_grad,
        bias_grad.reshape(C),
    )


def solution(mesh):
    return jax.shard_map(
        body,
        mesh=mesh,
        in_specs=(
            P("dp", None, "slab", None),
            P("dp", None, "slab", None),
            P(None, "slab", None, None),
            P(),
            P(),
        ),
        out_specs=(P("dp", None, "slab", None), P("dp", "slab", None, None), P(), P()),
        check_vma=False,
    )
```

```python
import functools
import math

import jax
import jax.numpy as jnp
import numpy as np
from jax import lax
from jax.experimental import pallas as pl
from jax.experimental.pallas import tpu as pltpu
from jax.sharding import PartitionSpec as P

C = 64
N = 64
XL = 4
S = 16
L = 16
CELLS = 4096
ROWS = C * XL
Q = 512
F32 = jnp.float32
BF16 = jnp.bfloat16


def mm(a, b):
    return jnp.dot(a, b, preferred_element_type=F32)


def nt(a, b):
    return lax.dot_general(a, b, (((1,), (1,)), ((), ())), preferred_element_type=F32)


def tn(a, b):
    return lax.dot_general(a, b, (((0,), (0,)), ((), ())), preferred_element_type=F32)


def waves(count, size):
    return np.array([i if i < count // 2 else size - count + i for i in range(count)])


def phase_tables():
    f = np.float32
    k = np.tile(waves(S, N), 2)[:, None]
    part = np.repeat([0.0, np.pi / 2], S)[:, None]
    unit = 2.0 * np.pi / N
    ang = unit * (k * (np.arange(128) // N)[None, :]) + part
    turn = unit * np.broadcast_to(2 * k, (2 * S, 128))
    angz = unit * ((np.arange(L)[:, None] * (np.arange(128) % N)[None, :]) % N)
    pair = lambda a, scale: np.concatenate([np.cos(a), np.sin(a)]) * scale
    return np.concatenate([pair(ang, 1.0 / N), pair(turn, 1.0), pair(angz, 1.0)]).astype(f)


def x_tables():
    ang = 2.0 * np.pi * ((np.arange(N)[:, None] * waves(16, N)[None, :]) % N) / N
    return np.cos(ang) / 8.0, np.sin(ang) / 8.0


def constants():
    cos, sin = x_tables()
    fx = np.zeros((64, 128))
    fo = np.zeros((64, 128))
    iv = np.zeros((128, 64))
    ia = np.zeros((128, 64))
    for i in range(16):
        for h in range(2):
            for x in range(N):
                c, s = cos[x, i], sin[x, i]
                re, im = i * 4 + h * 2, i * 4 + h * 2 + 1
                fx[re, 2 * x : 2 * x + 2] = (c, s)
                fx[im, 2 * x : 2 * x + 2] = (-s, c)
                fo[re, 2 * x : 2 * x + 2] = (-s, c)
                fo[im, 2 * x : 2 * x + 2] = (-c, -s)
                vre, vim = (re, im) if h == 0 else (im, re)
                iv[2 * x, vre], iv[2 * x, vim] = c, -s
                iv[2 * x + 1, vre], iv[2 * x + 1, vim] = s, c
                ia[2 * x, re], ia[2 * x, im] = c, -s
                ia[2 * x + 1, re], ia[2 * x + 1, im] = s, c
    gather = np.zeros((2, 128, 128))
    for i in range(16):
        for h in range(2):
            for q in range(4):
                gather[h, i * 8 + h * 4 + q, (q // 2) * 64 + i * 4 + q % 2] = 1
    pick = np.zeros((6, 32, 128))
    for b in range(16):
        for h in range(2):
            base = b * 8 + h * 4
            pick[h * 3, b * 2, base] = 1
            pick[h * 3, b * 2 + 1, base + 1] = 1
            pick[h * 3 + 1, b * 2, base + 2] = 1
            pick[h * 3 + 1, b * 2 + 1, base + 3] = 1
            pick[h * 3 + 2, b * 2, base + 3] = 1
            pick[h * 3 + 2, b * 2 + 1, base + 2] = -1
    bf = lambda v: jnp.asarray(np.asarray(v, np.float32), BF16)
    return {
        "fx": bf(fx),
        "fo": bf(fo),
        "iv": bf(iv),
        "ia": bf(ia),
        "gather": bf(gather),
        "pick": bf(pick),
    }


def lanes(shape):
    return lax.broadcasted_iota(jnp.int32, shape, 1)


def subl(shape):
    return lax.broadcasted_iota(jnp.int32, shape, 0)


def low_half(shape):
    return (lanes(shape) & 64) == 0


def half_turn(v):
    return pltpu.roll(v, 64, 1)


def pack_spectra(acc, perm, z_ref, out_ref):
    s = mm(acc.astype(BF16), perm)
    low = low_half((32, 128))

    def put(x, u, v):
        z_ref[u, pl.ds(2 * x, S, stride=8), :] = v[:S]
        z_ref[u, pl.ds(2 * x + 1, S, stride=8), :] = v[S:]

    for u in range(L // 2):
        for t in range(2):
            a = s[u * 64 : u * 64 + 32, t * 128 : t * 128 + 128]
            b = s[u * 64 + 32 : u * 64 + 64, t * 128 : t * 128 + 128]
            put(2 * t, u, jnp.where(low, a, half_turn(b)))
            put(2 * t + 1, u, jnp.where(low, half_turn(a), b))
    for u in range(L // 2):
        out_ref[:, u * 128 : u * 128 + 128] = z_ref[u].astype(BF16)


def unpack_back(arrived, perm, z_ref, b_ref, doubled):
    for u in range(L // 2):
        z_ref[u] = arrived[:, u * 128 : u * 128 + 128].astype(F32)
    low = low_half((32, 128))

    def take(x, u):
        parts = [z_ref[u, pl.ds(2 * x + p, S, stride=8), :] for p in range(2)]
        return jnp.concatenate(parts, axis=0)

    for u in range(L // 2):
        for t in range(2):
            a, b = take(2 * t, u), take(2 * t + 1, u)
            first = jnp.where(low, a, half_turn(b))
            second = jnp.where(low, half_turn(a), b)
            if doubled:
                first = first * (1.0 if u == 0 else 2.0)
                second = second * 2.0
            b_ref[u * 64 : u * 64 + 32, t * 128 : t * 128 + 128] = first.astype(BF16)
            b_ref[u * 64 + 32 : u * 64 + 64, t * 128 : t * 128 + 128] = second.astype(BF16)
    return nt(perm, b_ref[...]).astype(BF16)


def halves_of(v):
    hi = v.astype(BF16)
    return hi, (v - hi.astype(F32)).astype(BF16)


def split(v):
    hi, lo = halves_of(v)
    return jnp.where(low_half(v.shape), hi.astype(F32), lo.astype(F32)).astype(BF16)


def spread_weight(w):
    e = (subl((ROWS, C)) // XL == lanes((ROWS, C))).astype(BF16)
    left = mm(e, w)
    full = nt(left.astype(BF16), e)
    same = (subl((ROWS, ROWS)) & 3) == (lanes((ROWS, ROWS)) & 3)
    return jnp.where(same, full, 0.0).astype(BF16)


def onehot(match):
    return jnp.where(match, 1.0, 0.0).astype(BF16)


def lane_order():
    r, k = subl((ROWS, ROWS)), lanes((ROWS, ROWS))
    return onehot(((r >> 2) == (k & 63)) & ((r & 3) == (k >> 6)))


def ext_order(r, k):
    return onehot(((r >> 3) == ((k >> 2) & 15)) & (((r >> 2) & 1) == (k >> 6)) & ((r & 3) == (k & 3)))


SQUARE = (128, 128)

STEPS = 8
CHUNK = CELLS // STEPS
EXACT = functools.partial(
    lax.dot_general, precision=lax.Precision.HIGHEST, preferred_element_type=F32
)
NT = (((1,), (1,)), ((), ()))
NN = (((1,), (0,)), ((), ()))


def at(step):
    if isinstance(step, int):
        return slice(step * CHUNK, step * CHUNK + CHUNK)
    return pl.ds(pl.multiple_of(step * CHUNK, CHUNK), CHUNK)


def planes(src, dst, sems, step):
    return pltpu.make_async_copy(src.at[:, :, at(step)], dst.at[:, :, at(step)], sems.at[step])


def columns(src, dst, sems, step):
    return pltpu.make_async_copy(src.at[:, at(step)], dst.at[:, at(step)], sems.at[step])


def start_all(copy, src, dst, sems):
    for n in range(STEPS):
        copy(src, dst, sems, n).start()


def wait_all(copy, src, dst, sems):
    for n in range(STEPS):
        copy(src, dst, sems, n).wait()


def make_table(phase_ref, ca, sa, refs, tiles):
    cr, sr = phase_ref[64:96, :], phase_ref[96:128, :]
    for g in tiles:
        for l in range(L):
            cb, sb = phase_ref[128 + l : 129 + l, :], phase_ref[144 + l : 145 + l, :]
            v = (ca * cb - sa * sb).astype(BF16)
            for ref, start in refs:
                ref[l * 32 : l * 32 + 32, pl.ds(start + g * 128, 128)] = v
        ca, sa = ca * cr - sa * sr, sa * cr + ca * sr
    return ca, sa


def spectra_kernel(
    f_hbm, phase_hbm, w_hbm,
    out_ref, tf_ref, w_ref,
    f_ref, ta_ref, tb_ref, acc_ref, z_ref, phase_ref, f_sem, p_sem,
):
    phases = pltpu.make_async_copy(phase_hbm, phase_ref, p_sem.at[0])
    phases.start()
    start_all(planes, f_hbm, f_ref, f_sem)
    weights = pltpu.make_async_copy(w_hbm, w_ref, p_sem.at[1])
    acc_ref[...] = jnp.zeros_like(acc_ref)
    tf_ref[Q + ROWS :, :] = jnp.ones((16, CELLS), BF16)
    perm = lane_order()
    phases.wait()

    def make(n, ca, sa, buf_ref):
        start = n * CHUNK if isinstance(n, int) else pl.multiple_of(n * CHUNK, CHUNK)
        return make_table(phase_ref, ca, sa, ((buf_ref, 0), (tf_ref, start)), range(4))

    def add(n, buf_ref):
        flat = f_ref[:, :, at(n)].reshape(ROWS, CHUNK)
        tf_ref[Q : Q + ROWS, at(n)] = flat
        acc_ref[...] += nt(buf_ref[...], flat)

    ca, sa = make(0, phase_ref[:32, :], phase_ref[32:64, :], ta_ref)
    weights.start()

    def step(m, carry):
        n = 2 * m
        planes(f_hbm, f_ref, f_sem, n).wait()
        planes(f_hbm, f_ref, f_sem, n + 1).wait()
        add(n, ta_ref)
        carry = make(n + 1, *carry, tb_ref)
        add(n + 1, tb_ref)
        return make(n + 2, *carry, ta_ref)

    for m in range(STEPS // 2 - 1):
        ca, sa = step(m, (ca, sa))
    planes(f_hbm, f_ref, f_sem, STEPS - 2).wait()
    planes(f_hbm, f_ref, f_sem, STEPS - 1).wait()
    add(STEPS - 2, ta_ref)
    make(STEPS - 1, ca, sa, tb_ref)
    add(STEPS - 1, tb_ref)
    pack_spectra(acc_ref[...], perm, z_ref, out_ref)
    weights.wait()


def mix_kernel(r_ref, w_ref, fx_ref, iv_ref, out_ref, m_ref, mask_ref, v_ref):
    m = mm(fx_ref[...], r_ref[...])
    m_ref[...] = m.astype(BF16)
    shape = m.shape
    own = ((lanes(shape) >> 6) & 1) == ((subl(shape) >> 1) & 1)
    mask_ref[...] = jnp.where(own, m, 0.0)
    row, lane = subl((8, 128)), lanes((8, 128))
    top = row < 4
    even = (row & 1) == 0
    sign = jnp.where(lane < 64, -1.0, 1.0)
    keep = (lane >> 6) == ((row >> 1) & 1)

    def step(u):
        cols = slice(u * 128, u * 128 + 128)
        pair = slice(2 * u, 2 * u + 2)
        for t in range(8):
            left = mask_ref[8 * t : 8 * t + 8, cols].astype(BF16)
            right = jnp.concatenate(
                [w_ref[2 * t, pair].reshape(128, 128), w_ref[2 * t + 1, pair].reshape(128, 128)],
                axis=1,
            )
            o = mm(left, right)
            res = jnp.where(top, o[:, :128], o[:, 128:])
            turned = half_turn(res)
            above = pltpu.roll(turned, 7, 0)
            below = pltpu.roll(turned, 1, 0)
            v = jnp.where(even, res + sign * above, below - sign * res)
            v_ref[8 * t : 8 * t + 8, cols] = jnp.where(keep, v, 0.0)

    for u in range(L // 2):
        step(u)
    out_ref[...] = mm(iv_ref[...], v_ref[...].astype(BF16)).astype(BF16)


def slope(v):
    a = jnp.abs(v)
    e = jnp.exp2(v * v * (-0.5 / math.log(2.0)))
    t = 1.0 / (1.0 + (0.3275911 / math.sqrt(2.0)) * a)
    poly = t * (
        0.5 * 0.254829592
        + t
        * (
            0.5 * -0.284496736
            + t * (0.5 * 1.421413741 + t * (0.5 * -1.453152027 + t * (0.5 * 1.061405429)))
        )
    )
    tail = e * (poly - a * (1.0 / math.sqrt(2.0 * math.pi)))
    return jnp.where(v < 0, tail, 1.0 - tail)


def delta_kernel(
    r_ref, tf_ref, ct_hbm, w_ref, bias_ref,
    out_ref, d_hbm,
    ct_ref, d_ref, bl_ref, shift_ref, pa_ref, pb_ref, da_ref, db_ref,
    sg_ref, bt_ref, z_ref, ct_sem, d_sem,
):
    start_all(planes, ct_hbm, ct_ref, ct_sem)
    bl_ref[:, :Q] = unpack_back(r_ref[...], lane_order(), z_ref, bt_ref, True)
    bl_ref[:, Q:] = spread_weight(w_ref[...])
    e = (subl((ROWS, C)) // XL == lanes((ROWS, C))).astype(F32)
    shift_ref[...] = EXACT(e, jnp.broadcast_to(bias_ref[...], (128, C)), NT)
    sg_ref[...] = jnp.zeros_like(sg_ref)
    db_ref[...] = jnp.zeros_like(db_ref)

    def before(n, p_ref, halves=(0, 1)):
        for h in halves:
            cols = pl.ds(pl.multiple_of(n * CHUNK + h * 256, 256), 256)
            p_ref[:, h * 256 : h * 256 + 256] = mm(bl_ref[...], tf_ref[: Q + ROWS, cols])

    def add(n, own_ref, first, last):
        sg_ref[first:last, :] += nt(tf_ref[first:last, at(n)], own_ref[...])

    def bend(n, p_ref, own_ref, blocks):
        for r in blocks:
            rows = slice(r * 16, r * 16 + 16)
            v = p_ref[rows, :] + jnp.concatenate([shift_ref[rows, :]] * (CHUNK // 128), axis=1)
            ct = ct_ref[r * 4 : r * 4 + 4, :, at(n)].reshape(16, CHUNK)
            d = (ct.astype(F32) * slope(v)).astype(BF16)
            own_ref[rows, :] = d
            d_ref[rows, at(n)] = d

    def weave(n, p_ref, next_ref, own_ref, past_ref):
        past, later = jnp.maximum(n - 1, 0), jnp.minimum(n + 1, STEPS - 1)
        add(past, past_ref, 0, 256)
        bend(n, p_ref, own_ref, range(0, 3))
        add(past, past_ref, 256, 512)
        bend(n, p_ref, own_ref, range(3, 6))
        add(past, past_ref, 512, 784)
        bend(n, p_ref, own_ref, range(6, 9))
        before(later, next_ref, (0,))
        bend(n, p_ref, own_ref, range(9, 12))
        before(later, next_ref, (1,))
        bend(n, p_ref, own_ref, range(12, 16))
        columns(d_ref, d_hbm, d_sem, n).start()

    before(0, pa_ref)

    def step(m, carry):
        n = 2 * m
        planes(ct_hbm, ct_ref, ct_sem, n).wait()
        planes(ct_hbm, ct_ref, ct_sem, n + 1).wait()
        weave(n, pa_ref, pb_ref, da_ref, db_ref)
        weave(n + 1, pb_ref, pa_ref, db_ref, da_ref)
        return carry

    lax.fori_loop(0, STEPS // 2, step, 0)
    add(STEPS - 1, db_ref, 0, 784)
    doubled = jnp.where(subl((Q, ROWS)) < 32, 1.0, 2.0)
    pack_spectra(sg_ref[:Q, :] * doubled, lane_order(), z_ref, out_ref)
    same = (subl((ROWS, ROWS)) & 3) == (lanes((ROWS, ROWS)) & 3)
    g = jnp.where(same, sg_ref[Q : Q + ROWS, :], 0.0)
    e = onehot(subl((C, ROWS)) == lanes((C, ROWS)) // XL)
    e2 = onehot((subl((ROWS, 128)) // XL) == (lanes((ROWS, 128)) & 63))
    wg = [nt(e, half) for half in halves_of(g)]
    wg = [mm(half, e2) for half in halves_of(wg[0] + wg[1])]
    sums = jnp.broadcast_to(sg_ref[Q + ROWS : Q + ROWS + 1, :], (128, ROWS))
    bg = [nt(e, half) for half in halves_of(sums)]
    both = jnp.concatenate([wg[0] + wg[1], bg[0] + bg[1]], axis=0)
    out_ref[:, 1024:] = mm(ext_order(subl(SQUARE), lanes(SQUARE)), split(both)).astype(BF16)
    wait_all(columns, d_ref, d_hbm, d_sem)


def total_of(ext):
    shape = (8, 128)
    pick = ((lanes(shape) & 7) == subl(shape)).astype(BF16)
    v = mm(pick, ext)
    return v + half_turn(v)


def spread_total(v):
    return jnp.concatenate([split(v).astype(F32)] * S, axis=0).astype(BF16)


def adjoint_kernel(
    r_ref, m_ref, w_ref, fx_ref, fo_ref, ia_ref, gather_ref, out_ref, dp_ref, left_ref, v_ref
):
    r = r_ref[:, :1024]
    a = mm(fx_ref[...], r)
    b = mm(fo_ref[...], r)
    row = subl((64, 128))
    first = ((row >> 1) & 1) == 0
    low = low_half((64, 128))
    for u in range(8):
        cols = slice(u * 128, u * 128 + 128)
        au, bu = a[:, cols], b[:, cols]
        left_ref[:, cols] = jnp.where(
            first, jnp.where(low, au, half_turn(bu)), jnp.where(low, half_turn(au), bu)
        ).astype(BF16)
    both = jnp.concatenate([m_ref[...], a.astype(BF16)], axis=0)
    dp_ref[...] = (mm(gather_ref[0], both[:, :512]) + mm(gather_ref[1], both[:, 512:])).astype(BF16)
    out_ref[:, 1024:] = spread_total(total_of(r_ref[:, 1024:]))
    row, lane = subl((8, 128)), lanes((8, 128))
    top = row < 4
    keep = (lane >> 6) == ((row >> 1) & 1)

    def step(u):
        cols = slice(u * 128, u * 128 + 128)
        pair = slice(2 * u, 2 * u + 2)
        for t in range(8):
            right = jnp.concatenate(
                [w_ref[2 * t, pair].reshape(128, 128), w_ref[2 * t + 1, pair].reshape(128, 128)],
                axis=0,
            )
            o = nt(left_ref[8 * t : 8 * t + 8, cols], right)
            res = jnp.where(top, o[:, :128], o[:, 128:])
            v_ref[8 * t : 8 * t + 8, cols] = jnp.where(keep, res, 0.0)

    for u in range(L // 2):
        step(u)
    out_ref[:, :1024] = mm(ia_ref[...], v_ref[...].astype(BF16)).astype(BF16)


def assemble_kernel(r_ref, part_ref, out_ref):
    out_ref[:, :512] = part_ref[...]
    v = mm(ext_order(lanes(SQUARE), subl(SQUARE)), r_ref[:, 1024:])
    v = v + half_turn(v)
    low = low_half((8, 128))
    tiles = [jnp.where(low, v[p : p + 8], v[p + 8 : p + 16]) for p in range(0, C, 16)]
    diag = subl((C, 128)) == lanes((C, 128))
    hi, lo = halves_of(jnp.sum(jnp.where(diag, v[C:], 0.0), axis=0, keepdims=True))
    row = subl((8, 128))
    bias = jnp.where(row == 0, hi.astype(F32), jnp.where(row == 1, lo.astype(F32), 0.0))
    sums = jnp.concatenate(tiles + [bias], axis=1)
    out_ref[:, 512:] = jnp.concatenate([sums] * S, axis=0).astype(BF16)


def weight_grad_kernel(
    dp_ref, pick_ref, out_hbm, pg_hbm, bg_hbm, out_ref, pg_ref, bg_ref, o_sem, g_sem
):
    shape = (8, 128)
    which = onehot((lanes(shape) & 7) == subl(shape))
    sums = mm(which, dp_ref[:, 512:]) * (1.0 / 2048.0)
    for p in range(4):
        tile = sums[:, p * 128 : p * 128 + 128]
        pg_ref[p * 16 : p * 16 + 8, :] = tile[:, :C]
        pg_ref[p * 16 + 8 : p * 16 + 16, :] = half_turn(tile)[:, :C]
    bg_ref[...] = sums[0:1, 512 : 512 + C] + sums[1:2, 512 : 512 + C]
    copies = [
        pltpu.make_async_copy(pg_ref, pg_hbm, g_sem.at[0]),
        pltpu.make_async_copy(bg_ref, bg_hbm, g_sem.at[1]),
    ]
    for copy in copies:
        copy.start()
    low = low_half((32, 128))
    data = dp_ref[:, :512]
    for h in range(2):
        m = mm(pick_ref[h * 3], data)
        g1 = mm(pick_ref[h * 3 + 1], data)
        g2 = mm(pick_ref[h * 3 + 2], data)
        for v in range(4):
            cols = slice(v * 128, v * 128 + 128)
            a, b = g1[:, cols], g2[:, cols]
            right = jnp.concatenate(
                [jnp.where(low, a, half_turn(b)), jnp.where(low, half_turn(a), b)], axis=1
            )
            o = tn(m[:, cols].astype(BF16), right.astype(BF16)) * 0.25
            l = h * 8 + v * 2
            out_ref[l] = o[:64, :128]
            out_ref[l + 1] = o[64:, 128:]
        part = pl.ds(h * 8, 8)
        copies.append(pltpu.make_async_copy(out_ref.at[part], out_hbm.at[part], o_sem.at[h]))
        copies[-1].start()
    for copy in copies:
        copy.wait()


def input_grad_kernel(
    r_ref, d_hbm, w_ref, phase_ref,
    out_hbm,
    d_ref, ta_ref, tb_ref, o_ref, bl_ref, bt_ref, z_ref, d_sem, o_sem,
):
    start_all(columns, d_hbm, d_ref, d_sem)
    bl_ref[:, :Q] = unpack_back(r_ref[:, :1024], lane_order(), z_ref, bt_ref, False)
    bl_ref[:, Q:] = spread_weight(w_ref[...]).astype(F32).T.astype(BF16)

    def finish(n, own_ref):
        out = mm(bl_ref[:, :Q], own_ref[...]) + mm(bl_ref[:, Q:], d_ref[:, at(n)])
        o_ref[:, :, at(n)] = out.astype(BF16).reshape(C, XL, CHUNK)

    def make(carry, next_ref):
        return make_table(phase_ref, *carry, ((next_ref, 0),), range(4))

    def step(m, carry):
        n = 2 * m
        columns(d_hbm, d_ref, d_sem, n).wait()
        columns(d_hbm, d_ref, d_sem, n + 1).wait()
        finish(n, ta_ref)
        carry = make(carry, tb_ref)
        finish(n + 1, tb_ref)
        carry = make(carry, ta_ref)
        planes(o_ref, out_hbm, o_sem, n).start()
        planes(o_ref, out_hbm, o_sem, n + 1).start()
        return carry

    carry = make((phase_ref[:32, :], phase_ref[32:64, :]), ta_ref)
    carry = lax.fori_loop(0, STEPS // 2 - 1, step, carry)
    columns(d_hbm, d_ref, d_sem, STEPS - 2).wait()
    columns(d_hbm, d_ref, d_sem, STEPS - 1).wait()
    finish(STEPS - 2, ta_ref)
    planes(o_ref, out_hbm, o_sem, STEPS - 2).start()
    make(carry, tb_ref)
    finish(STEPS - 1, tb_ref)
    planes(o_ref, out_hbm, o_sem, STEPS - 1).start()
    wait_all(planes, o_ref, out_hbm, o_sem)


def call(kernel, name, outs, scratch, args, big=(), big_outs=(), sems=0, room=8):
    place = lambda n, far: pl.BlockSpec(memory_space=pltpu.HBM if n in far else pltpu.VMEM)
    return pl.pallas_call(
        kernel,
        in_specs=[place(n, big) for n in range(len(args))],
        out_specs=[place(n, big_outs) for n in range(len(outs))],
        out_shape=[
            (pltpu.HBM if n in big_outs else pltpu.VMEM)(shape, dtype)
            for n, (shape, dtype) in enumerate(outs)
        ],
        scratch_shapes=[pltpu.VMEM(shape, dtype) for shape, dtype in scratch]
        + [pltpu.SemaphoreType.DMA((STEPS,))] * sems,
        compiler_params=pltpu.CompilerParams(vmem_limit_bytes=room << 20),
        name=name,
    )(
        *[
            pltpu.with_memory_space_constraint(a, pltpu.HBM if n in big else pltpu.VMEM)
            for n, a in enumerate(args)
        ]
    )


def exchange(v, axis):
    width = v.shape[1]
    out = lax.all_to_all(v.reshape(S, 8, width), axis, split_axis=0, concat_axis=0, tiled=True)
    return out.reshape(128, width)


def body(field, cotangent, spectral_weight, point_weight, bias):
    k = constants()
    field3 = field.reshape(C, XL, CELLS)
    cot3 = cotangent.reshape(C, XL, CELLS)
    planes_shape = ((C, XL, CELLS), BF16)
    cells_shape = ((ROWS, CELLS), BF16)
    weight_shape = (spectral_weight.shape, BF16)

    phases = jnp.asarray(phase_tables())
    spectra, rows, weights = call(
        spectra_kernel,
        "spectra",
        [((128, 1024), BF16), ((Q + ROWS + 16, CELLS), BF16), weight_shape],
        [planes_shape, ((Q, CHUNK), BF16), ((Q, CHUNK), BF16), ((Q, ROWS), F32),
         ((L // 2, 128, 128), F32), ((160, 128), F32)],
        [field3, phases, spectral_weight],
        big=(0, 1, 2), sems=2,
    )
    arrived = exchange(spectra, "slab")
    back, modes = call(
        mix_kernel,
        "mix",
        [((128, 1024), BF16), ((64, 1024), BF16)],
        [((64, 1024), F32), ((64, 1024), F32)],
        [arrived, weights, k["fx"], k["iv"]],
    )
    arrived = exchange(back, "slab")
    grad_spectra, delta = call(
        delta_kernel,
        "delta",
        [((128, 1152), BF16), cells_shape],
        [
            planes_shape, cells_shape,
            ((ROWS, Q + ROWS), BF16), ((ROWS, 128), F32),
            ((ROWS, CHUNK), F32), ((ROWS, CHUNK), F32), ((ROWS, CHUNK), BF16), ((ROWS, CHUNK), BF16),
            ((Q + ROWS + 16, ROWS), F32), ((Q, ROWS), BF16), ((L // 2, 128, 128), F32),
        ],
        [arrived, rows, cot3, point_weight, bias.reshape(1, C)],
        big=(2,), big_outs=(1,), sems=2, room=16,
    )
    arrived = exchange(grad_spectra, "slab")
    adjoint, part = call(
        adjoint_kernel,
        "adjoint",
        [((128, 1152), BF16), ((128, 512), BF16)],
        [((64, 1024), BF16), ((64, 1024), F32)],
        [arrived, modes, weights, k["fx"], k["fo"], k["ia"], k["gather"]],
    )
    arrived = exchange(adjoint, "slab")
    (shared,) = call(assemble_kernel, "assemble", [((128, 1152), BF16)], [], [arrived, part])
    shared = exchange(shared, "dp")
    (input_grad,) = call(
        input_grad_kernel,
        "input_grad",
        [planes_shape],
        [cells_shape, ((Q, CHUNK), BF16), ((Q, CHUNK), BF16), planes_shape,
         ((ROWS, Q + ROWS), BF16), ((Q, ROWS), BF16), ((L // 2, 128, 128), F32)],
        [arrived, delta, point_weight, phases],
        big=(1,), big_outs=(0,), sems=2, room=16,
    )
    spectral_grad, point_grad, bias_grad = call(
        weight_grad_kernel,
        "weight_grad",
        [((L, C, 128), F32), ((C, C), F32), ((1, C), F32)],
        [((L, C, 128), F32), ((C, C), F32), ((1, C), F32)],
        [shared, k["pick"]],
        big_outs=(0, 1, 2), sems=2,
    )
    return (
        input_grad.reshape(field.shape),
        spectral_grad[None],
        point_grad,
        bias_grad.reshape(C),
    )


def solution(mesh):
    return jax.shard_map(
        body,
        mesh=mesh,
        in_specs=(
            P("dp", None, "slab", None),
            P("dp", None, "slab", None),
            P(None, "slab", None, None),
            P(),
            P(),
        ),
        out_specs=(P("dp", None, "slab", None), P("dp", "slab", None, None), P(), P()),
        check_vma=False,
    )
```

```python
import functools
import math

import jax
import jax.numpy as jnp
import numpy as np
from jax import lax
from jax.experimental import pallas as pl
from jax.experimental.pallas import tpu as pltpu
from jax.sharding import PartitionSpec as P

C = 64
N = 64
XL = 4
S = 16
L = 16
CELLS = 4096
ROWS = C * XL
Q = 512
F32 = jnp.float32
BF16 = jnp.bfloat16


def mm(a, b):
    return jnp.dot(a, b, preferred_element_type=F32)


def nt(a, b):
    return lax.dot_general(a, b, (((1,), (1,)), ((), ())), preferred_element_type=F32)


def tn(a, b):
    return lax.dot_general(a, b, (((0,), (0,)), ((), ())), preferred_element_type=F32)


def waves(count, size):
    return np.array([i if i < count // 2 else size - count + i for i in range(count)])


def phase_tables():
    f = np.float32
    k = np.tile(waves(S, N), 2)[:, None]
    part = np.repeat([0.0, np.pi / 2], S)[:, None]
    unit = 2.0 * np.pi / N
    ang = unit * (k * (np.arange(128) // N)[None, :]) + part
    turn = unit * np.broadcast_to(2 * k, (2 * S, 128))
    angz = unit * ((np.arange(L)[:, None] * (np.arange(128) % N)[None, :]) % N)
    pair = lambda a, scale: np.concatenate([np.cos(a), np.sin(a)]) * scale
    return np.concatenate([pair(ang, 1.0 / N), pair(turn, 1.0), pair(angz, 1.0)]).astype(f)


def x_tables():
    ang = 2.0 * np.pi * ((np.arange(N)[:, None] * waves(16, N)[None, :]) % N) / N
    return np.cos(ang) / 8.0, np.sin(ang) / 8.0


def constants():
    cos, sin = x_tables()
    fx = np.zeros((64, 128))
    fo = np.zeros((64, 128))
    iv = np.zeros((128, 64))
    ia = np.zeros((128, 64))
    for i in range(16):
        for h in range(2):
            for x in range(N):
                c, s = cos[x, i], sin[x, i]
                re, im = i * 4 + h * 2, i * 4 + h * 2 + 1
                fx[re, 2 * x : 2 * x + 2] = (c, s)
                fx[im, 2 * x : 2 * x + 2] = (-s, c)
                fo[re, 2 * x : 2 * x + 2] = (-s, c)
                fo[im, 2 * x : 2 * x + 2] = (-c, -s)
                vre, vim = (re, im) if h == 0 else (im, re)
                iv[2 * x, vre], iv[2 * x, vim] = c, -s
                iv[2 * x + 1, vre], iv[2 * x + 1, vim] = s, c
                ia[2 * x, re], ia[2 * x, im] = c, -s
                ia[2 * x + 1, re], ia[2 * x + 1, im] = s, c
    gather = np.zeros((2, 128, 128))
    for i in range(16):
        for h in range(2):
            for q in range(4):
                gather[h, i * 8 + h * 4 + q, (q // 2) * 64 + i * 4 + q % 2] = 1
    pick = np.zeros((6, 32, 128))
    for b in range(16):
        for h in range(2):
            base = b * 8 + h * 4
            pick[h * 3, b * 2, base] = 1
            pick[h * 3, b * 2 + 1, base + 1] = 1
            pick[h * 3 + 1, b * 2, base + 2] = 1
            pick[h * 3 + 1, b * 2 + 1, base + 3] = 1
            pick[h * 3 + 2, b * 2, base + 3] = 1
            pick[h * 3 + 2, b * 2 + 1, base + 2] = -1
    bf = lambda v: jnp.asarray(np.asarray(v, np.float32), BF16)
    return {
        "fx": bf(fx),
        "fo": bf(fo),
        "iv": bf(iv),
        "ia": bf(ia),
        "gather": bf(gather),
        "pick": bf(pick),
    }


def lanes(shape):
    return lax.broadcasted_iota(jnp.int32, shape, 1)


def subl(shape):
    return lax.broadcasted_iota(jnp.int32, shape, 0)


def low_half(shape):
    return (lanes(shape) & 64) == 0


def half_turn(v):
    return pltpu.roll(v, 64, 1)


def pack_spectra(acc, perm, z_ref, out_ref):
    s = mm(acc.astype(BF16), perm)
    low = low_half((32, 128))

    def put(x, u, v):
        z_ref[u, pl.ds(2 * x, S, stride=8), :] = v[:S]
        z_ref[u, pl.ds(2 * x + 1, S, stride=8), :] = v[S:]

    for u in range(L // 2):
        for t in range(2):
            a = s[u * 64 : u * 64 + 32, t * 128 : t * 128 + 128]
            b = s[u * 64 + 32 : u * 64 + 64, t * 128 : t * 128 + 128]
            put(2 * t, u, jnp.where(low, a, half_turn(b)))
            put(2 * t + 1, u, jnp.where(low, half_turn(a), b))
    for u in range(L // 2):
        out_ref[:, u * 128 : u * 128 + 128] = z_ref[u].astype(BF16)


def unpack_back(arrived, perm, z_ref, b_ref, doubled):
    for u in range(L // 2):
        z_ref[u] = arrived[:, u * 128 : u * 128 + 128].astype(F32)
    low = low_half((32, 128))

    def take(x, u):
        parts = [z_ref[u, pl.ds(2 * x + p, S, stride=8), :] for p in range(2)]
        return jnp.concatenate(parts, axis=0)

    for u in range(L // 2):
        for t in range(2):
            a, b = take(2 * t, u), take(2 * t + 1, u)
            first = jnp.where(low, a, half_turn(b))
            second = jnp.where(low, half_turn(a), b)
            if doubled:
                first = first * (1.0 if u == 0 else 2.0)
                second = second * 2.0
            b_ref[u * 64 : u * 64 + 32, t * 128 : t * 128 + 128] = first.astype(BF16)
            b_ref[u * 64 + 32 : u * 64 + 64, t * 128 : t * 128 + 128] = second.astype(BF16)
    return nt(perm, b_ref[...]).astype(BF16)


def halves_of(v):
    hi = v.astype(BF16)
    return hi, (v - hi.astype(F32)).astype(BF16)


def split(v):
    hi, lo = halves_of(v)
    return jnp.where(low_half(v.shape), hi.astype(F32), lo.astype(F32)).astype(BF16)


def spread_weight(w):
    e = (subl((ROWS, C)) // XL == lanes((ROWS, C))).astype(BF16)
    left = mm(e, w)
    full = nt(left.astype(BF16), e)
    same = (subl((ROWS, ROWS)) & 3) == (lanes((ROWS, ROWS)) & 3)
    return jnp.where(same, full, 0.0).astype(BF16)


def onehot(match):
    return jnp.where(match, 1.0, 0.0).astype(BF16)


def lane_order():
    r, k = subl((ROWS, ROWS)), lanes((ROWS, ROWS))
    return onehot(((r >> 2) == (k & 63)) & ((r & 3) == (k >> 6)))


def ext_order(r, k):
    return onehot(((r >> 3) == ((k >> 2) & 15)) & (((r >> 2) & 1) == (k >> 6)) & ((r & 3) == (k & 3)))


SQUARE = (128, 128)

STEPS = 8
CHUNK = CELLS // STEPS
EXACT = functools.partial(
    lax.dot_general, precision=lax.Precision.HIGHEST, preferred_element_type=F32
)
NT = (((1,), (1,)), ((), ()))
NN = (((1,), (0,)), ((), ()))


def at(step):
    if isinstance(step, int):
        return slice(step * CHUNK, step * CHUNK + CHUNK)
    return pl.ds(pl.multiple_of(step * CHUNK, CHUNK), CHUNK)


def planes(src, dst, sems, step):
    return pltpu.make_async_copy(src.at[:, :, at(step)], dst.at[:, :, at(step)], sems.at[step])


def columns(src, dst, sems, step):
    return pltpu.make_async_copy(src.at[:, at(step)], dst.at[:, at(step)], sems.at[step])


def start_all(copy, src, dst, sems):
    for n in range(STEPS):
        copy(src, dst, sems, n).start()


def wait_all(copy, src, dst, sems):
    for n in range(STEPS):
        copy(src, dst, sems, n).wait()


def make_table(phase_ref, ca, sa, refs, tiles):
    cr, sr = phase_ref[64:96, :], phase_ref[96:128, :]
    for g in tiles:
        for l in range(L):
            cb, sb = phase_ref[128 + l : 129 + l, :], phase_ref[144 + l : 145 + l, :]
            v = (ca * cb - sa * sb).astype(BF16)
            for ref, start in refs:
                ref[l * 32 : l * 32 + 32, pl.ds(start + g * 128, 128)] = v
        ca, sa = ca * cr - sa * sr, sa * cr + ca * sr
    return ca, sa


def spectra_kernel(
    f_hbm, phase_hbm, w_hbm,
    out_ref, tf_ref, w_ref,
    f_ref, ta_ref, tb_ref, acc_ref, z_ref, phase_ref, f_sem, p_sem,
):
    phases = pltpu.make_async_copy(phase_hbm, phase_ref, p_sem.at[0])
    phases.start()
    start_all(planes, f_hbm, f_ref, f_sem)
    weights = pltpu.make_async_copy(w_hbm, w_ref, p_sem.at[1])
    acc_ref[...] = jnp.zeros_like(acc_ref)
    tf_ref[Q + ROWS :, :] = jnp.ones((16, CELLS), BF16)
    perm = lane_order()
    phases.wait()

    def make(n, ca, sa, buf_ref):
        start = n * CHUNK if isinstance(n, int) else pl.multiple_of(n * CHUNK, CHUNK)
        return make_table(phase_ref, ca, sa, ((buf_ref, 0), (tf_ref, start)), range(4))

    def add(n, buf_ref):
        flat = f_ref[:, :, at(n)].reshape(ROWS, CHUNK)
        tf_ref[Q : Q + ROWS, at(n)] = flat
        acc_ref[...] += nt(buf_ref[...], flat)

    ca, sa = make(0, phase_ref[:32, :], phase_ref[32:64, :], ta_ref)
    weights.start()

    def step(m, carry):
        n = 2 * m
        planes(f_hbm, f_ref, f_sem, n).wait()
        planes(f_hbm, f_ref, f_sem, n + 1).wait()
        add(n, ta_ref)
        carry = make(n + 1, *carry, tb_ref)
        add(n + 1, tb_ref)
        return make(n + 2, *carry, ta_ref)

    for m in range(STEPS // 2 - 1):
        ca, sa = step(m, (ca, sa))
    planes(f_hbm, f_ref, f_sem, STEPS - 2).wait()
    planes(f_hbm, f_ref, f_sem, STEPS - 1).wait()
    add(STEPS - 2, ta_ref)
    make(STEPS - 1, ca, sa, tb_ref)
    add(STEPS - 1, tb_ref)
    pack_spectra(acc_ref[...], perm, z_ref, out_ref)
    weights.wait()


def mix_kernel(r_ref, w_ref, fx_ref, iv_ref, out_ref, m_ref, mask_ref, v_ref):
    m = mm(fx_ref[...], r_ref[...])
    m_ref[...] = m.astype(BF16)
    shape = m.shape
    own = ((lanes(shape) >> 6) & 1) == ((subl(shape) >> 1) & 1)
    mask_ref[...] = jnp.where(own, m, 0.0)
    row, lane = subl((8, 128)), lanes((8, 128))
    top = row < 4
    even = (row & 1) == 0
    sign = jnp.where(lane < 64, -1.0, 1.0)
    keep = (lane >> 6) == ((row >> 1) & 1)

    def step(u):
        cols = slice(u * 128, u * 128 + 128)
        pair = slice(2 * u, 2 * u + 2)
        for t in range(8):
            left = mask_ref[8 * t : 8 * t + 8, cols].astype(BF16)
            right = jnp.concatenate(
                [w_ref[2 * t, pair].reshape(128, 128), w_ref[2 * t + 1, pair].reshape(128, 128)],
                axis=1,
            )
            o = mm(left, right)
            res = jnp.where(top, o[:, :128], o[:, 128:])
            turned = half_turn(res)
            above = pltpu.roll(turned, 7, 0)
            below = pltpu.roll(turned, 1, 0)
            v = jnp.where(even, res + sign * above, below - sign * res)
            v_ref[8 * t : 8 * t + 8, cols] = jnp.where(keep, v, 0.0)

    for u in range(L // 2):
        step(u)
    out_ref[...] = mm(iv_ref[...], v_ref[...].astype(BF16)).astype(BF16)


def slope(v):
    a = jnp.abs(v)
    e = jnp.exp2(v * v * (-0.5 / math.log(2.0)))
    t = 1.0 / (1.0 + (0.3275911 / math.sqrt(2.0)) * a)
    poly = t * (
        0.5 * 0.254829592
        + t
        * (
            0.5 * -0.284496736
            + t * (0.5 * 1.421413741 + t * (0.5 * -1.453152027 + t * (0.5 * 1.061405429)))
        )
    )
    tail = e * (poly - a * (1.0 / math.sqrt(2.0 * math.pi)))
    return jnp.where(v < 0, tail, 1.0 - tail)


def delta_kernel(
    r_ref, tf_ref, ct_hbm, w_ref, bias_ref,
    out_ref, d_hbm,
    ct_ref, d_ref, bl_ref, shift_ref, pa_ref, pb_ref, da_ref, db_ref,
    sg_ref, bt_ref, z_ref, ct_sem, d_sem,
):
    start_all(planes, ct_hbm, ct_ref, ct_sem)
    bl_ref[:, :Q] = unpack_back(r_ref[...], lane_order(), z_ref, bt_ref, True)
    bl_ref[:, Q:] = spread_weight(w_ref[...])
    e = (subl((ROWS, C)) // XL == lanes((ROWS, C))).astype(F32)
    shift_ref[...] = EXACT(e, jnp.broadcast_to(bias_ref[...], (128, C)), NT)
    sg_ref[...] = jnp.zeros_like(sg_ref)

    def before(n, p_ref, halves=(0, 1)):
        for h in halves:
            cols = slice(n * CHUNK + h * 256, n * CHUNK + h * 256 + 256)
            p_ref[:, h * 256 : h * 256 + 256] = mm(bl_ref[...], tf_ref[: Q + ROWS, cols])

    def add(n, own_ref, first, last):
        sg_ref[first:last, :] += nt(tf_ref[first:last, at(n)], own_ref[...])

    def bend(n, p_ref, own_ref, blocks):
        for r in blocks:
            rows = slice(r * 16, r * 16 + 16)
            v = p_ref[rows, :] + jnp.concatenate([shift_ref[rows, :]] * (CHUNK // 128), axis=1)
            ct = ct_ref[r * 4 : r * 4 + 4, :, at(n)].reshape(16, CHUNK)
            d = (ct.astype(F32) * slope(v)).astype(BF16)
            own_ref[rows, :] = d
            d_ref[rows, at(n)] = d

    before(0, pa_ref)
    bufs = ((pa_ref, pb_ref, da_ref, db_ref), (pb_ref, pa_ref, db_ref, da_ref))
    for n in range(STEPS):
        p_ref, next_ref, own_ref, past_ref = bufs[n % 2]
        if n % 2 == 0:
            planes(ct_hbm, ct_ref, ct_sem, n).wait()
            planes(ct_hbm, ct_ref, ct_sem, n + 1).wait()
        ends = (0, 256, 512, 784)
        for q in range(3):
            if n > 0:
                add(n - 1, past_ref, ends[q], ends[q + 1])
            bend(n, p_ref, own_ref, range(3 * q, 3 * q + 3))
        for h in range(2):
            if n < STEPS - 1:
                before(n + 1, next_ref, (h,))
            bend(n, p_ref, own_ref, range(9 + 3 * h, 12 + 4 * h))
        columns(d_ref, d_hbm, d_sem, n).start()
    add(STEPS - 1, db_ref, 0, 784)
    doubled = jnp.where(subl((Q, ROWS)) < 32, 1.0, 2.0)
    pack_spectra(sg_ref[:Q, :] * doubled, lane_order(), z_ref, out_ref)
    same = (subl((ROWS, ROWS)) & 3) == (lanes((ROWS, ROWS)) & 3)
    g = jnp.where(same, sg_ref[Q : Q + ROWS, :], 0.0)
    e = onehot(subl((C, ROWS)) == lanes((C, ROWS)) // XL)
    e2 = onehot((subl((ROWS, 128)) // XL) == (lanes((ROWS, 128)) & 63))
    wg = [nt(e, half) for half in halves_of(g)]
    wg = [mm(half, e2) for half in halves_of(wg[0] + wg[1])]
    sums = jnp.broadcast_to(sg_ref[Q + ROWS : Q + ROWS + 1, :], (128, ROWS))
    bg = [nt(e, half) for half in halves_of(sums)]
    both = jnp.concatenate([wg[0] + wg[1], bg[0] + bg[1]], axis=0)
    out_ref[:, 1024:] = mm(ext_order(subl(SQUARE), lanes(SQUARE)), split(both)).astype(BF16)
    wait_all(columns, d_ref, d_hbm, d_sem)


def total_of(ext):
    shape = (8, 128)
    pick = ((lanes(shape) & 7) == subl(shape)).astype(BF16)
    v = mm(pick, ext)
    return v + half_turn(v)


def spread_total(v):
    return jnp.concatenate([split(v).astype(F32)] * S, axis=0).astype(BF16)


def adjoint_kernel(
    r_ref, m_ref, w_ref, fx_ref, fo_ref, ia_ref, gather_ref, out_ref, dp_ref, left_ref, v_ref
):
    r = r_ref[:, :1024]
    a = mm(fx_ref[...], r)
    b = mm(fo_ref[...], r)
    row = subl((64, 128))
    first = ((row >> 1) & 1) == 0
    low = low_half((64, 128))
    for u in range(8):
        cols = slice(u * 128, u * 128 + 128)
        au, bu = a[:, cols], b[:, cols]
        left_ref[:, cols] = jnp.where(
            first, jnp.where(low, au, half_turn(bu)), jnp.where(low, half_turn(au), bu)
        ).astype(BF16)
    both = jnp.concatenate([m_ref[...], a.astype(BF16)], axis=0)
    dp_ref[...] = (mm(gather_ref[0], both[:, :512]) + mm(gather_ref[1], both[:, 512:])).astype(BF16)
    out_ref[:, 1024:] = spread_total(total_of(r_ref[:, 1024:]))
    row, lane = subl((8, 128)), lanes((8, 128))
    top = row < 4
    keep = (lane >> 6) == ((row >> 1) & 1)

    def step(u):
        cols = slice(u * 128, u * 128 + 128)
        pair = slice(2 * u, 2 * u + 2)
        for t in range(8):
            right = jnp.concatenate(
                [w_ref[2 * t, pair].reshape(128, 128), w_ref[2 * t + 1, pair].reshape(128, 128)],
                axis=0,
            )
            o = nt(left_ref[8 * t : 8 * t + 8, cols], right)
            res = jnp.where(top, o[:, :128], o[:, 128:])
            v_ref[8 * t : 8 * t + 8, cols] = jnp.where(keep, res, 0.0)

    for u in range(L // 2):
        step(u)
    out_ref[:, :1024] = mm(ia_ref[...], v_ref[...].astype(BF16)).astype(BF16)


def assemble_kernel(r_ref, part_ref, out_ref):
    out_ref[:, :512] = part_ref[...]
    v = mm(ext_order(lanes(SQUARE), subl(SQUARE)), r_ref[:, 1024:])
    v = v + half_turn(v)
    low = low_half((8, 128))
    tiles = [jnp.where(low, v[p : p + 8], v[p + 8 : p + 16]) for p in range(0, C, 16)]
    diag = subl((C, 128)) == lanes((C, 128))
    hi, lo = halves_of(jnp.sum(jnp.where(diag, v[C:], 0.0), axis=0, keepdims=True))
    row = subl((8, 128))
    bias = jnp.where(row == 0, hi.astype(F32), jnp.where(row == 1, lo.astype(F32), 0.0))
    sums = jnp.concatenate(tiles + [bias], axis=1)
    out_ref[:, 512:] = jnp.concatenate([sums] * S, axis=0).astype(BF16)


def weight_grad_kernel(
    dp_ref, pick_ref, out_hbm, pg_hbm, bg_hbm, out_ref, pg_ref, bg_ref, o_sem, g_sem
):
    shape = (8, 128)
    which = onehot((lanes(shape) & 7) == subl(shape))
    sums = mm(which, dp_ref[:, 512:]) * (1.0 / 2048.0)
    for p in range(4):
        tile = sums[:, p * 128 : p * 128 + 128]
        pg_ref[p * 16 : p * 16 + 8, :] = tile[:, :C]
        pg_ref[p * 16 + 8 : p * 16 + 16, :] = half_turn(tile)[:, :C]
    bg_ref[...] = sums[0:1, 512 : 512 + C] + sums[1:2, 512 : 512 + C]
    copies = [
        pltpu.make_async_copy(pg_ref, pg_hbm, g_sem.at[0]),
        pltpu.make_async_copy(bg_ref, bg_hbm, g_sem.at[1]),
    ]
    for copy in copies:
        copy.start()
    low = low_half((32, 128))
    data = dp_ref[:, :512]
    for h in range(2):
        m = mm(pick_ref[h * 3], data)
        g1 = mm(pick_ref[h * 3 + 1], data)
        g2 = mm(pick_ref[h * 3 + 2], data)
        for v in range(4):
            cols = slice(v * 128, v * 128 + 128)
            a, b = g1[:, cols], g2[:, cols]
            right = jnp.concatenate(
                [jnp.where(low, a, half_turn(b)), jnp.where(low, half_turn(a), b)], axis=1
            )
            o = tn(m[:, cols].astype(BF16), right.astype(BF16)) * 0.25
            l = h * 8 + v * 2
            out_ref[l] = o[:64, :128]
            out_ref[l + 1] = o[64:, 128:]
        part = pl.ds(h * 8, 8)
        copies.append(pltpu.make_async_copy(out_ref.at[part], out_hbm.at[part], o_sem.at[h]))
        copies[-1].start()
    for copy in copies:
        copy.wait()


def input_grad_kernel(
    r_ref, d_hbm, w_ref, phase_ref,
    out_hbm,
    d_ref, ta_ref, tb_ref, o_ref, bl_ref, bt_ref, z_ref, d_sem, o_sem,
):
    start_all(columns, d_hbm, d_ref, d_sem)
    bl_ref[:, :Q] = unpack_back(r_ref[:, :1024], lane_order(), z_ref, bt_ref, False)
    bl_ref[:, Q:] = spread_weight(w_ref[...]).astype(F32).T.astype(BF16)

    def finish(n, own_ref):
        out = mm(bl_ref[:, :Q], own_ref[...]) + mm(bl_ref[:, Q:], d_ref[:, at(n)])
        o_ref[:, :, at(n)] = out.astype(BF16).reshape(C, XL, CHUNK)

    def make(carry, next_ref):
        return make_table(phase_ref, *carry, ((next_ref, 0),), range(4))

    def step(m, carry):
        n = 2 * m
        columns(d_hbm, d_ref, d_sem, n).wait()
        columns(d_hbm, d_ref, d_sem, n + 1).wait()
        finish(n, ta_ref)
        carry = make(carry, tb_ref)
        finish(n + 1, tb_ref)
        carry = make(carry, ta_ref)
        planes(o_ref, out_hbm, o_sem, n).start()
        planes(o_ref, out_hbm, o_sem, n + 1).start()
        return carry

    carry = make((phase_ref[:32, :], phase_ref[32:64, :]), ta_ref)
    carry = lax.fori_loop(0, STEPS // 2 - 1, step, carry)
    columns(d_hbm, d_ref, d_sem, STEPS - 2).wait()
    columns(d_hbm, d_ref, d_sem, STEPS - 1).wait()
    finish(STEPS - 2, ta_ref)
    planes(o_ref, out_hbm, o_sem, STEPS - 2).start()
    make(carry, tb_ref)
    finish(STEPS - 1, tb_ref)
    planes(o_ref, out_hbm, o_sem, STEPS - 1).start()
    wait_all(planes, o_ref, out_hbm, o_sem)


def call(kernel, name, outs, scratch, args, big=(), big_outs=(), sems=0, room=8):
    place = lambda n, far: pl.BlockSpec(memory_space=pltpu.HBM if n in far else pltpu.VMEM)
    return pl.pallas_call(
        kernel,
        in_specs=[place(n, big) for n in range(len(args))],
        out_specs=[place(n, big_outs) for n in range(len(outs))],
        out_shape=[
            (pltpu.HBM if n in big_outs else pltpu.VMEM)(shape, dtype)
            for n, (shape, dtype) in enumerate(outs)
        ],
        scratch_shapes=[pltpu.VMEM(shape, dtype) for shape, dtype in scratch]
        + [pltpu.SemaphoreType.DMA((STEPS,))] * sems,
        compiler_params=pltpu.CompilerParams(vmem_limit_bytes=room << 20),
        name=name,
    )(
        *[
            pltpu.with_memory_space_constraint(a, pltpu.HBM if n in big else pltpu.VMEM)
            for n, a in enumerate(args)
        ]
    )


def exchange(v, axis):
    width = v.shape[1]
    out = lax.all_to_all(v.reshape(S, 8, width), axis, split_axis=0, concat_axis=0, tiled=True)
    return out.reshape(128, width)


def body(field, cotangent, spectral_weight, point_weight, bias):
    k = constants()
    field3 = field.reshape(C, XL, CELLS)
    cot3 = cotangent.reshape(C, XL, CELLS)
    planes_shape = ((C, XL, CELLS), BF16)
    cells_shape = ((ROWS, CELLS), BF16)
    weight_shape = (spectral_weight.shape, BF16)

    phases = jnp.asarray(phase_tables())
    spectra, rows, weights = call(
        spectra_kernel,
        "spectra",
        [((128, 1024), BF16), ((Q + ROWS + 16, CELLS), BF16), weight_shape],
        [planes_shape, ((Q, CHUNK), BF16), ((Q, CHUNK), BF16), ((Q, ROWS), F32),
         ((L // 2, 128, 128), F32), ((160, 128), F32)],
        [field3, phases, spectral_weight],
        big=(0, 1, 2), sems=2,
    )
    arrived = exchange(spectra, "slab")
    back, modes = call(
        mix_kernel,
        "mix",
        [((128, 1024), BF16), ((64, 1024), BF16)],
        [((64, 1024), F32), ((64, 1024), F32)],
        [arrived, weights, k["fx"], k["iv"]],
    )
    arrived = exchange(back, "slab")
    grad_spectra, delta = call(
        delta_kernel,
        "delta",
        [((128, 1152), BF16), cells_shape],
        [
            planes_shape, cells_shape,
            ((ROWS, Q + ROWS), BF16), ((ROWS, 128), F32),
            ((ROWS, CHUNK), F32), ((ROWS, CHUNK), F32), ((ROWS, CHUNK), BF16), ((ROWS, CHUNK), BF16),
            ((Q + ROWS + 16, ROWS), F32), ((Q, ROWS), BF16), ((L // 2, 128, 128), F32),
        ],
        [arrived, rows, cot3, point_weight, bias.reshape(1, C)],
        big=(2,), big_outs=(1,), sems=2, room=16,
    )
    arrived = exchange(grad_spectra, "slab")
    adjoint, part = call(
        adjoint_kernel,
        "adjoint",
        [((128, 1152), BF16), ((128, 512), BF16)],
        [((64, 1024), BF16), ((64, 1024), F32)],
        [arrived, modes, weights, k["fx"], k["fo"], k["ia"], k["gather"]],
    )
    arrived = exchange(adjoint, "slab")
    (shared,) = call(assemble_kernel, "assemble", [((128, 1152), BF16)], [], [arrived, part])
    shared = exchange(shared, "dp")
    (input_grad,) = call(
        input_grad_kernel,
        "input_grad",
        [planes_shape],
        [cells_shape, ((Q, CHUNK), BF16), ((Q, CHUNK), BF16), planes_shape,
         ((ROWS, Q + ROWS), BF16), ((Q, ROWS), BF16), ((L // 2, 128, 128), F32)],
        [arrived, delta, point_weight, phases],
        big=(1,), big_outs=(0,), sems=2, room=16,
    )
    spectral_grad, point_grad, bias_grad = call(
        weight_grad_kernel,
        "weight_grad",
        [((L, C, 128), F32), ((C, C), F32), ((1, C), F32)],
        [((L, C, 128), F32), ((C, C), F32), ((1, C), F32)],
        [shared, k["pick"]],
        big_outs=(0, 1, 2), sems=2,
    )
    return (
        input_grad.reshape(field.shape),
        spectral_grad[None],
        point_grad,
        bias_grad.reshape(C),
    )


def solution(mesh):
    return jax.shard_map(
        body,
        mesh=mesh,
        in_specs=(
            P("dp", None, "slab", None),
            P("dp", None, "slab", None),
            P(None, "slab", None, None),
            P(),
            P(),
        ),
        out_specs=(P("dp", None, "slab", None), P("dp", "slab", None, None), P(), P()),
        check_vma=False,
    )
```

```python
import functools
import math

import jax
import jax.numpy as jnp
import numpy as np
from jax import lax
from jax.experimental import pallas as pl
from jax.experimental.pallas import tpu as pltpu
from jax.sharding import PartitionSpec as P

C = 64
N = 64
XL = 4
S = 16
L = 16
CELLS = 4096
ROWS = C * XL
Q = 512
F32 = jnp.float32
BF16 = jnp.bfloat16


def mm(a, b):
    return jnp.dot(a, b, preferred_element_type=F32)


def nt(a, b):
    return lax.dot_general(a, b, (((1,), (1,)), ((), ())), preferred_element_type=F32)


def tn(a, b):
    return lax.dot_general(a, b, (((0,), (0,)), ((), ())), preferred_element_type=F32)


def waves(count, size):
    return np.array([i if i < count // 2 else size - count + i for i in range(count)])


def phase_tables():
    f = np.float32
    k = np.tile(waves(S, N), 2)[:, None]
    part = np.repeat([0.0, np.pi / 2], S)[:, None]
    unit = 2.0 * np.pi / N
    ang = unit * (k * (np.arange(128) // N)[None, :]) + part
    turn = unit * np.broadcast_to(2 * k, (2 * S, 128))
    angz = unit * ((np.arange(L)[:, None] * (np.arange(128) % N)[None, :]) % N)
    pair = lambda a, scale: np.concatenate([np.cos(a), np.sin(a)]) * scale
    return np.concatenate([pair(ang, 1.0 / N), pair(turn, 1.0), pair(angz, 1.0)]).astype(f)


def x_tables():
    ang = 2.0 * np.pi * ((np.arange(N)[:, None] * waves(16, N)[None, :]) % N) / N
    return np.cos(ang) / 8.0, np.sin(ang) / 8.0


def constants():
    cos, sin = x_tables()
    fx = np.zeros((64, 128))
    fo = np.zeros((64, 128))
    iv = np.zeros((128, 64))
    ia = np.zeros((128, 64))
    for i in range(16):
        for h in range(2):
            for x in range(N):
                c, s = cos[x, i], sin[x, i]
                re, im = i * 4 + h * 2, i * 4 + h * 2 + 1
                fx[re, 2 * x : 2 * x + 2] = (c, s)
                fx[im, 2 * x : 2 * x + 2] = (-s, c)
                fo[re, 2 * x : 2 * x + 2] = (-s, c)
                fo[im, 2 * x : 2 * x + 2] = (-c, -s)
                vre, vim = (re, im) if h == 0 else (im, re)
                iv[2 * x, vre], iv[2 * x, vim] = c, -s
                iv[2 * x + 1, vre], iv[2 * x + 1, vim] = s, c
                ia[2 * x, re], ia[2 * x, im] = c, -s
                ia[2 * x + 1, re], ia[2 * x + 1, im] = s, c
    gather = np.zeros((2, 128, 128))
    for i in range(16):
        for h in range(2):
            for q in range(4):
                gather[h, i * 8 + h * 4 + q, (q // 2) * 64 + i * 4 + q % 2] = 1
    pick = np.zeros((6, 32, 128))
    for b in range(16):
        for h in range(2):
            base = b * 8 + h * 4
            pick[h * 3, b * 2, base] = 1
            pick[h * 3, b * 2 + 1, base + 1] = 1
            pick[h * 3 + 1, b * 2, base + 2] = 1
            pick[h * 3 + 1, b * 2 + 1, base + 3] = 1
            pick[h * 3 + 2, b * 2, base + 3] = 1
            pick[h * 3 + 2, b * 2 + 1, base + 2] = -1
    bf = lambda v: jnp.asarray(np.asarray(v, np.float32), BF16)
    return {
        "fx": bf(fx),
        "fo": bf(fo),
        "iv": bf(iv),
        "ia": bf(ia),
        "gather": bf(gather),
        "pick": bf(pick),
    }


def lanes(shape):
    return lax.broadcasted_iota(jnp.int32, shape, 1)


def subl(shape):
    return lax.broadcasted_iota(jnp.int32, shape, 0)


def low_half(shape):
    return (lanes(shape) & 64) == 0


def half_turn(v):
    return pltpu.roll(v, 64, 1)


def pack_spectra(acc, perm, z_ref, out_ref):
    s = mm(acc.astype(BF16), perm)
    low = low_half((32, 128))

    def put(x, u, v):
        z_ref[u, pl.ds(2 * x, S, stride=8), :] = v[:S]
        z_ref[u, pl.ds(2 * x + 1, S, stride=8), :] = v[S:]

    for u in range(L // 2):
        for t in range(2):
            a = s[u * 64 : u * 64 + 32, t * 128 : t * 128 + 128]
            b = s[u * 64 + 32 : u * 64 + 64, t * 128 : t * 128 + 128]
            put(2 * t, u, jnp.where(low, a, half_turn(b)))
            put(2 * t + 1, u, jnp.where(low, half_turn(a), b))
    for u in range(L // 2):
        out_ref[:, u * 128 : u * 128 + 128] = z_ref[u].astype(BF16)


def unpack_back(arrived, perm, z_ref, b_ref, doubled):
    for u in range(L // 2):
        z_ref[u] = arrived[:, u * 128 : u * 128 + 128].astype(F32)
    low = low_half((32, 128))

    def take(x, u):
        parts = [z_ref[u, pl.ds(2 * x + p, S, stride=8), :] for p in range(2)]
        return jnp.concatenate(parts, axis=0)

    for u in range(L // 2):
        for t in range(2):
            a, b = take(2 * t, u), take(2 * t + 1, u)
            first = jnp.where(low, a, half_turn(b))
            second = jnp.where(low, half_turn(a), b)
            if doubled:
                first = first * (1.0 if u == 0 else 2.0)
                second = second * 2.0
            b_ref[u * 64 : u * 64 + 32, t * 128 : t * 128 + 128] = first.astype(BF16)
            b_ref[u * 64 + 32 : u * 64 + 64, t * 128 : t * 128 + 128] = second.astype(BF16)
    return nt(perm, b_ref[...]).astype(BF16)


def halves_of(v):
    hi = v.astype(BF16)
    return hi, (v - hi.astype(F32)).astype(BF16)


def split(v):
    hi, lo = halves_of(v)
    return jnp.where(low_half(v.shape), hi.astype(F32), lo.astype(F32)).astype(BF16)


def spread_weight(w):
    e = (subl((ROWS, C)) // XL == lanes((ROWS, C))).astype(BF16)
    left = mm(e, w)
    full = nt(left.astype(BF16), e)
    same = (subl((ROWS, ROWS)) & 3) == (lanes((ROWS, ROWS)) & 3)
    return jnp.where(same, full, 0.0).astype(BF16)


def onehot(match):
    return jnp.where(match, 1.0, 0.0).astype(BF16)


def lane_order():
    r, k = subl((ROWS, ROWS)), lanes((ROWS, ROWS))
    return onehot(((r >> 2) == (k & 63)) & ((r & 3) == (k >> 6)))


def ext_order(r, k):
    return onehot(((r >> 3) == ((k >> 2) & 15)) & (((r >> 2) & 1) == (k >> 6)) & ((r & 3) == (k & 3)))


SQUARE = (128, 128)

STEPS = 8
CHUNK = CELLS // STEPS
EXACT = functools.partial(
    lax.dot_general, precision=lax.Precision.HIGHEST, preferred_element_type=F32
)
NT = (((1,), (1,)), ((), ()))
NN = (((1,), (0,)), ((), ()))


def at(step):
    if isinstance(step, int):
        return slice(step * CHUNK, step * CHUNK + CHUNK)
    return pl.ds(pl.multiple_of(step * CHUNK, CHUNK), CHUNK)


def planes(src, dst, sems, step):
    return pltpu.make_async_copy(src.at[:, :, at(step)], dst.at[:, :, at(step)], sems.at[step])


def columns(src, dst, sems, step):
    return pltpu.make_async_copy(src.at[:, at(step)], dst.at[:, at(step)], sems.at[step])


def start_all(copy, src, dst, sems):
    for n in range(STEPS):
        copy(src, dst, sems, n).start()


def wait_all(copy, src, dst, sems):
    for n in range(STEPS):
        copy(src, dst, sems, n).wait()


def make_table(phase_ref, ca, sa, refs, tiles):
    cr, sr = phase_ref[64:96, :], phase_ref[96:128, :]
    for g in tiles:
        for l in range(L):
            cb, sb = phase_ref[128 + l : 129 + l, :], phase_ref[144 + l : 145 + l, :]
            v = (ca * cb - sa * sb).astype(BF16)
            for ref, start in refs:
                ref[l * 32 : l * 32 + 32, pl.ds(start + g * 128, 128)] = v
        ca, sa = ca * cr - sa * sr, sa * cr + ca * sr
    return ca, sa


def spectra_kernel(
    f_hbm, phase_hbm, w_hbm,
    out_ref, tf_ref, w_ref,
    f_ref, ta_ref, tb_ref, acc_ref, z_ref, phase_ref, f_sem, p_sem,
):
    phases = pltpu.make_async_copy(phase_hbm, phase_ref, p_sem.at[0])
    phases.start()
    start_all(planes, f_hbm, f_ref, f_sem)
    weights = pltpu.make_async_copy(w_hbm, w_ref, p_sem.at[1])
    acc_ref[...] = jnp.zeros_like(acc_ref)
    tf_ref[Q + ROWS :, :] = jnp.ones((16, CELLS), BF16)
    perm = lane_order()
    phases.wait()

    def make(n, ca, sa, buf_ref):
        start = n * CHUNK if isinstance(n, int) else pl.multiple_of(n * CHUNK, CHUNK)
        return make_table(phase_ref, ca, sa, ((buf_ref, 0), (tf_ref, start)), range(4))

    def add(n, buf_ref):
        flat = f_ref[:, :, at(n)].reshape(ROWS, CHUNK)
        tf_ref[Q : Q + ROWS, at(n)] = flat
        acc_ref[...] += nt(buf_ref[...], flat)

    ca, sa = make(0, phase_ref[:32, :], phase_ref[32:64, :], ta_ref)
    weights.start()

    def step(m, carry):
        n = 2 * m
        planes(f_hbm, f_ref, f_sem, n).wait()
        planes(f_hbm, f_ref, f_sem, n + 1).wait()
        add(n, ta_ref)
        carry = make(n + 1, *carry, tb_ref)
        add(n + 1, tb_ref)
        return make(n + 2, *carry, ta_ref)

    for m in range(STEPS // 2 - 1):
        ca, sa = step(m, (ca, sa))
    planes(f_hbm, f_ref, f_sem, STEPS - 2).wait()
    planes(f_hbm, f_ref, f_sem, STEPS - 1).wait()
    add(STEPS - 2, ta_ref)
    make(STEPS - 1, ca, sa, tb_ref)
    add(STEPS - 1, tb_ref)
    pack_spectra(acc_ref[...], perm, z_ref, out_ref)
    weights.wait()


def mix_kernel(r_ref, w_ref, fx_ref, iv_ref, out_ref, m_ref, mask_ref, v_ref):
    m = mm(fx_ref[...], r_ref[...])
    m_ref[...] = m.astype(BF16)
    shape = m.shape
    own = ((lanes(shape) >> 6) & 1) == ((subl(shape) >> 1) & 1)
    mask_ref[...] = jnp.where(own, m, 0.0)
    row, lane = subl((8, 128)), lanes((8, 128))
    top = row < 4
    even = (row & 1) == 0
    sign = jnp.where(lane < 64, -1.0, 1.0)
    keep = (lane >> 6) == ((row >> 1) & 1)

    def step(u):
        cols = slice(u * 128, u * 128 + 128)
        pair = slice(2 * u, 2 * u + 2)
        for t in range(8):
            left = mask_ref[8 * t : 8 * t + 8, cols].astype(BF16)
            right = jnp.concatenate(
                [w_ref[2 * t, pair].reshape(128, 128), w_ref[2 * t + 1, pair].reshape(128, 128)],
                axis=1,
            )
            o = mm(left, right)
            res = jnp.where(top, o[:, :128], o[:, 128:])
            turned = half_turn(res)
            above = pltpu.roll(turned, 7, 0)
            below = pltpu.roll(turned, 1, 0)
            v = jnp.where(even, res + sign * above, below - sign * res)
            v_ref[8 * t : 8 * t + 8, cols] = jnp.where(keep, v, 0.0)

    for u in range(L // 2):
        step(u)
    out_ref[...] = mm(iv_ref[...], v_ref[...].astype(BF16)).astype(BF16)


def slope(v):
    a = jnp.abs(v)
    e = jnp.exp2(v * v * (-0.5 / math.log(2.0)))
    t = 1.0 / (1.0 + (0.3275911 / math.sqrt(2.0)) * a)
    poly = t * (
        0.5 * 0.254829592
        + t
        * (
            0.5 * -0.284496736
            + t * (0.5 * 1.421413741 + t * (0.5 * -1.453152027 + t * (0.5 * 1.061405429)))
        )
    )
    tail = e * (poly - a * (1.0 / math.sqrt(2.0 * math.pi)))
    return jnp.where(v < 0, tail, 1.0 - tail)


def delta_kernel(
    r_ref, tf_ref, ct_hbm, w_ref, bias_ref,
    out_ref, d_hbm,
    ct_ref, d_ref, bl_ref, shift_ref, pa_ref, pb_ref, da_ref, db_ref,
    sg_ref, bt_ref, z_ref, ct_sem, d_sem,
):
    start_all(planes, ct_hbm, ct_ref, ct_sem)
    bl_ref[:, :Q] = unpack_back(r_ref[...], lane_order(), z_ref, bt_ref, True)
    bl_ref[:, Q:] = spread_weight(w_ref[...])
    e = (subl((ROWS, C)) // XL == lanes((ROWS, C))).astype(F32)
    shift_ref[...] = EXACT(e, jnp.broadcast_to(bias_ref[...], (128, C)), NT)
    sg_ref[...] = jnp.zeros_like(sg_ref)

    def before(n, p_ref, halves=(0, 1)):
        for h in halves:
            cols = slice(n * CHUNK + h * 256, n * CHUNK + h * 256 + 256)
            p_ref[:, h * 256 : h * 256 + 256] = mm(bl_ref[...], tf_ref[: Q + ROWS, cols])

    def add(n, own_ref, first, last):
        sg_ref[first:last, :] += nt(tf_ref[first:last, at(n)], own_ref[...])

    def bend(n, p_ref, own_ref, blocks):
        for r in blocks:
            rows = slice(r * 16, r * 16 + 16)
            v = p_ref[rows, :] + jnp.concatenate([shift_ref[rows, :]] * (CHUNK // 128), axis=1)
            ct = ct_ref[r * 4 : r * 4 + 4, :, at(n)].reshape(16, CHUNK)
            d = (ct.astype(F32) * slope(v)).astype(BF16)
            own_ref[rows, :] = d
            d_ref[rows, at(n)] = d

    before(0, pa_ref)
    bufs = ((pa_ref, pb_ref, da_ref, db_ref), (pb_ref, pa_ref, db_ref, da_ref))
    for n in range(STEPS):
        p_ref, next_ref, own_ref, past_ref = bufs[n % 2]
        if n % 2 == 0:
            planes(ct_hbm, ct_ref, ct_sem, n).wait()
            planes(ct_hbm, ct_ref, ct_sem, n + 1).wait()
        ends = (0, 400, 784)
        for q in range(2):
            if n > 0:
                add(n - 1, past_ref, ends[q], ends[q + 1])
            bend(n, p_ref, own_ref, range(4 * q, 4 * q + 4))
        for h in range(2):
            if n < STEPS - 1:
                before(n + 1, next_ref, (h,))
            bend(n, p_ref, own_ref, range(8 + 4 * h, 12 + 4 * h))
        columns(d_ref, d_hbm, d_sem, n).start()
    add(STEPS - 1, db_ref, 0, 784)
    doubled = jnp.where(subl((Q, ROWS)) < 32, 1.0, 2.0)
    pack_spectra(sg_ref[:Q, :] * doubled, lane_order(), z_ref, out_ref)
    same = (subl((ROWS, ROWS)) & 3) == (lanes((ROWS, ROWS)) & 3)
    g = jnp.where(same, sg_ref[Q : Q + ROWS, :], 0.0)
    e = onehot(subl((C, ROWS)) == lanes((C, ROWS)) // XL)
    e2 = onehot((subl((ROWS, 128)) // XL) == (lanes((ROWS, 128)) & 63))
    wg = [nt(e, half) for half in halves_of(g)]
    wg = [mm(half, e2) for half in halves_of(wg[0] + wg[1])]
    sums = jnp.broadcast_to(sg_ref[Q + ROWS : Q + ROWS + 1, :], (128, ROWS))
    bg = [nt(e, half) for half in halves_of(sums)]
    both = jnp.concatenate([wg[0] + wg[1], bg[0] + bg[1]], axis=0)
    out_ref[:, 1024:] = mm(ext_order(subl(SQUARE), lanes(SQUARE)), split(both)).astype(BF16)
    wait_all(columns, d_ref, d_hbm, d_sem)


def total_of(ext):
    shape = (8, 128)
    pick = ((lanes(shape) & 7) == subl(shape)).astype(BF16)
    v = mm(pick, ext)
    return v + half_turn(v)


def spread_total(v):
    return jnp.concatenate([split(v).astype(F32)] * S, axis=0).astype(BF16)


def adjoint_kernel(
    r_ref, m_ref, w_ref, fx_ref, fo_ref, ia_ref, gather_ref, out_ref, dp_ref, left_ref, v_ref
):
    r = r_ref[:, :1024]
    a = mm(fx_ref[...], r)
    b = mm(fo_ref[...], r)
    row = subl((64, 128))
    first = ((row >> 1) & 1) == 0
    low = low_half((64, 128))
    for u in range(8):
        cols = slice(u * 128, u * 128 + 128)
        au, bu = a[:, cols], b[:, cols]
        left_ref[:, cols] = jnp.where(
            first, jnp.where(low, au, half_turn(bu)), jnp.where(low, half_turn(au), bu)
        ).astype(BF16)
    both = jnp.concatenate([m_ref[...], a.astype(BF16)], axis=0)
    dp_ref[...] = (mm(gather_ref[0], both[:, :512]) + mm(gather_ref[1], both[:, 512:])).astype(BF16)
    out_ref[:, 1024:] = spread_total(total_of(r_ref[:, 1024:]))
    row, lane = subl((8, 128)), lanes((8, 128))
    top = row < 4
    keep = (lane >> 6) == ((row >> 1) & 1)

    def step(u):
        cols = slice(u * 128, u * 128 + 128)
        pair = slice(2 * u, 2 * u + 2)
        for t in range(8):
            right = jnp.concatenate(
                [w_ref[2 * t, pair].reshape(128, 128), w_ref[2 * t + 1, pair].reshape(128, 128)],
                axis=0,
            )
            o = nt(left_ref[8 * t : 8 * t + 8, cols], right)
            res = jnp.where(top, o[:, :128], o[:, 128:])
            v_ref[8 * t : 8 * t + 8, cols] = jnp.where(keep, res, 0.0)

    for u in range(L // 2):
        step(u)
    out_ref[:, :1024] = mm(ia_ref[...], v_ref[...].astype(BF16)).astype(BF16)


def assemble_kernel(r_ref, part_ref, out_ref):
    out_ref[:, :512] = part_ref[...]
    v = mm(ext_order(lanes(SQUARE), subl(SQUARE)), r_ref[:, 1024:])
    v = v + half_turn(v)
    low = low_half((8, 128))
    tiles = [jnp.where(low, v[p : p + 8], v[p + 8 : p + 16]) for p in range(0, C, 16)]
    diag = subl((C, 128)) == lanes((C, 128))
    hi, lo = halves_of(jnp.sum(jnp.where(diag, v[C:], 0.0), axis=0, keepdims=True))
    row = subl((8, 128))
    bias = jnp.where(row == 0, hi.astype(F32), jnp.where(row == 1, lo.astype(F32), 0.0))
    sums = jnp.concatenate(tiles + [bias], axis=1)
    out_ref[:, 512:] = jnp.concatenate([sums] * S, axis=0).astype(BF16)


def weight_grad_kernel(
    dp_ref, pick_ref, out_hbm, pg_hbm, bg_hbm, out_ref, pg_ref, bg_ref, o_sem, g_sem
):
    shape = (8, 128)
    which = onehot((lanes(shape) & 7) == subl(shape))
    sums = mm(which, dp_ref[:, 512:]) * (1.0 / 2048.0)
    for p in range(4):
        tile = sums[:, p * 128 : p * 128 + 128]
        pg_ref[p * 16 : p * 16 + 8, :] = tile[:, :C]
        pg_ref[p * 16 + 8 : p * 16 + 16, :] = half_turn(tile)[:, :C]
    bg_ref[...] = sums[0:1, 512 : 512 + C] + sums[1:2, 512 : 512 + C]
    copies = [
        pltpu.make_async_copy(pg_ref, pg_hbm, g_sem.at[0]),
        pltpu.make_async_copy(bg_ref, bg_hbm, g_sem.at[1]),
    ]
    for copy in copies:
        copy.start()
    low = low_half((32, 128))
    data = dp_ref[:, :512]
    for h in range(2):
        m = mm(pick_ref[h * 3], data)
        g1 = mm(pick_ref[h * 3 + 1], data)
        g2 = mm(pick_ref[h * 3 + 2], data)
        for v in range(4):
            cols = slice(v * 128, v * 128 + 128)
            a, b = g1[:, cols], g2[:, cols]
            right = jnp.concatenate(
                [jnp.where(low, a, half_turn(b)), jnp.where(low, half_turn(a), b)], axis=1
            )
            o = tn(m[:, cols].astype(BF16), right.astype(BF16)) * 0.25
            l = h * 8 + v * 2
            out_ref[l] = o[:64, :128]
            out_ref[l + 1] = o[64:, 128:]
        part = pl.ds(h * 8, 8)
        copies.append(pltpu.make_async_copy(out_ref.at[part], out_hbm.at[part], o_sem.at[h]))
        copies[-1].start()
    for copy in copies:
        copy.wait()


def input_grad_kernel(
    r_ref, d_hbm, w_ref, phase_ref,
    out_hbm,
    d_ref, ta_ref, tb_ref, o_ref, bl_ref, bt_ref, z_ref, d_sem, o_sem,
):
    start_all(columns, d_hbm, d_ref, d_sem)
    bl_ref[:, :Q] = unpack_back(r_ref[:, :1024], lane_order(), z_ref, bt_ref, False)
    bl_ref[:, Q:] = spread_weight(w_ref[...]).astype(F32).T.astype(BF16)

    def finish(n, own_ref):
        out = mm(bl_ref[:, :Q], own_ref[...]) + mm(bl_ref[:, Q:], d_ref[:, at(n)])
        o_ref[:, :, at(n)] = out.astype(BF16).reshape(C, XL, CHUNK)

    def make(carry, next_ref):
        return make_table(phase_ref, *carry, ((next_ref, 0),), range(4))

    def step(m, carry):
        n = 2 * m
        columns(d_hbm, d_ref, d_sem, n).wait()
        columns(d_hbm, d_ref, d_sem, n + 1).wait()
        finish(n, ta_ref)
        carry = make(carry, tb_ref)
        finish(n + 1, tb_ref)
        carry = make(carry, ta_ref)
        planes(o_ref, out_hbm, o_sem, n).start()
        planes(o_ref, out_hbm, o_sem, n + 1).start()
        return carry

    carry = make((phase_ref[:32, :], phase_ref[32:64, :]), ta_ref)
    carry = lax.fori_loop(0, STEPS // 2 - 1, step, carry)
    columns(d_hbm, d_ref, d_sem, STEPS - 2).wait()
    columns(d_hbm, d_ref, d_sem, STEPS - 1).wait()
    finish(STEPS - 2, ta_ref)
    planes(o_ref, out_hbm, o_sem, STEPS - 2).start()
    make(carry, tb_ref)
    finish(STEPS - 1, tb_ref)
    planes(o_ref, out_hbm, o_sem, STEPS - 1).start()
    wait_all(planes, o_ref, out_hbm, o_sem)


def call(kernel, name, outs, scratch, args, big=(), big_outs=(), sems=0, room=8):
    place = lambda n, far: pl.BlockSpec(memory_space=pltpu.HBM if n in far else pltpu.VMEM)
    return pl.pallas_call(
        kernel,
        in_specs=[place(n, big) for n in range(len(args))],
        out_specs=[place(n, big_outs) for n in range(len(outs))],
        out_shape=[
            (pltpu.HBM if n in big_outs else pltpu.VMEM)(shape, dtype)
            for n, (shape, dtype) in enumerate(outs)
        ],
        scratch_shapes=[pltpu.VMEM(shape, dtype) for shape, dtype in scratch]
        + [pltpu.SemaphoreType.DMA((STEPS,))] * sems,
        compiler_params=pltpu.CompilerParams(vmem_limit_bytes=room << 20),
        name=name,
    )(
        *[
            pltpu.with_memory_space_constraint(a, pltpu.HBM if n in big else pltpu.VMEM)
            for n, a in enumerate(args)
        ]
    )


def exchange(v, axis):
    width = v.shape[1]
    out = lax.all_to_all(v.reshape(S, 8, width), axis, split_axis=0, concat_axis=0, tiled=True)
    return out.reshape(128, width)


def body(field, cotangent, spectral_weight, point_weight, bias):
    k = constants()
    field3 = field.reshape(C, XL, CELLS)
    cot3 = cotangent.reshape(C, XL, CELLS)
    planes_shape = ((C, XL, CELLS), BF16)
    cells_shape = ((ROWS, CELLS), BF16)
    weight_shape = (spectral_weight.shape, BF16)

    phases = jnp.asarray(phase_tables())
    spectra, rows, weights = call(
        spectra_kernel,
        "spectra",
        [((128, 1024), BF16), ((Q + ROWS + 16, CELLS), BF16), weight_shape],
        [planes_shape, ((Q, CHUNK), BF16), ((Q, CHUNK), BF16), ((Q, ROWS), F32),
         ((L // 2, 128, 128), F32), ((160, 128), F32)],
        [field3, phases, spectral_weight],
        big=(0, 1, 2), sems=2,
    )
    arrived = exchange(spectra, "slab")
    back, modes = call(
        mix_kernel,
        "mix",
        [((128, 1024), BF16), ((64, 1024), BF16)],
        [((64, 1024), F32), ((64, 1024), F32)],
        [arrived, weights, k["fx"], k["iv"]],
    )
    arrived = exchange(back, "slab")
    grad_spectra, delta = call(
        delta_kernel,
        "delta",
        [((128, 1152), BF16), cells_shape],
        [
            planes_shape, cells_shape,
            ((ROWS, Q + ROWS), BF16), ((ROWS, 128), F32),
            ((ROWS, CHUNK), F32), ((ROWS, CHUNK), F32), ((ROWS, CHUNK), BF16), ((ROWS, CHUNK), BF16),
            ((Q + ROWS + 16, ROWS), F32), ((Q, ROWS), BF16), ((L // 2, 128, 128), F32),
        ],
        [arrived, rows, cot3, point_weight, bias.reshape(1, C)],
        big=(2,), big_outs=(1,), sems=2, room=16,
    )
    arrived = exchange(grad_spectra, "slab")
    adjoint, part = call(
        adjoint_kernel,
        "adjoint",
        [((128, 1152), BF16), ((128, 512), BF16)],
        [((64, 1024), BF16), ((64, 1024), F32)],
        [arrived, modes, weights, k["fx"], k["fo"], k["ia"], k["gather"]],
    )
    arrived = exchange(adjoint, "slab")
    (shared,) = call(assemble_kernel, "assemble", [((128, 1152), BF16)], [], [arrived, part])
    shared = exchange(shared, "dp")
    (input_grad,) = call(
        input_grad_kernel,
        "input_grad",
        [planes_shape],
        [cells_shape, ((Q, CHUNK), BF16), ((Q, CHUNK), BF16), planes_shape,
         ((ROWS, Q + ROWS), BF16), ((Q, ROWS), BF16), ((L // 2, 128, 128), F32)],
        [arrived, delta, point_weight, phases],
        big=(1,), big_outs=(0,), sems=2, room=16,
    )
    spectral_grad, point_grad, bias_grad = call(
        weight_grad_kernel,
        "weight_grad",
        [((L, C, 128), F32), ((C, C), F32), ((1, C), F32)],
        [((L, C, 128), F32), ((C, C), F32), ((1, C), F32)],
        [shared, k["pick"]],
        big_outs=(0, 1, 2), sems=2,
    )
    return (
        input_grad.reshape(field.shape),
        spectral_grad[None],
        point_grad,
        bias_grad.reshape(C),
    )


def solution(mesh):
    return jax.shard_map(
        body,
        mesh=mesh,
        in_specs=(
            P("dp", None, "slab", None),
            P("dp", None, "slab", None),
            P(None, "slab", None, None),
            P(),
            P(),
        ),
        out_specs=(P("dp", None, "slab", None), P("dp", "slab", None, None), P(), P()),
        check_vma=False,
    )
```
